32 devices in a mesh: dp: 4 (over z), head: 4 (over y, core), mp: 2 (over x).
Axes of the slice: x: 2, y: 2, z: 4, core: 2. Of those that a mesh axis runs over, the one named last changes fastest.
Arguments:
- inputs: bfloat16 [2, 8192, 2048], P(None, ('dp', 'head', 'mp')), may hold values from -6 to 6
- cotangent: bfloat16 [2, 8192, 2048], P(None, ('dp', 'head', 'mp')), may hold values from -6 to 6
- seq_counts: int32 [8], replicated, may hold values from 1024 to 2048, as said below
- seq_bucket: int32 [8], replicated, may hold values from 0 to 7, each once
- attn_norm_gain: float32 [2048], replicated, may hold values from 0.5 to 1.5
- q_norm_gain: float32 [128], replicated, may hold values from 0.1 to 1.9
- k_norm_gain: float32 [128], replicated, may hold values from 0.1 to 1.9
- w_query: bfloat16 [2048, 2048], P(('dp', 'mp'), 'head'), may hold values from -0.125 to 0.125
- w_key: bfloat16 [2048, 1024], P(('dp', 'mp'), 'head'), may hold values from -0.125 to 0.125
- w_value: bfloat16 [2048, 1024], P(('dp', 'mp'), 'head'), may hold values from -0.125 to 0.125
- w_headgate: bfloat16 [2048, 16], P(('dp', 'mp'), 'head'), may hold values from -0.125 to 0.125
- w_out: bfloat16 [2048, 2048], P('head', ('dp', 'mp')), may hold values from -4 to 4
- ffn_norm_gain: float32 [2048], replicated, may hold values from 0.5 to 1.5
- w_gate: bfloat16 [2048, 6144], P(('dp', 'head'), 'mp'), may hold values from -0.125 to 0.125
- w_up: bfloat16 [2048, 6144], P(('dp', 'head'), 'mp'), may hold values from -0.125 to 0.125
- w_down: bfloat16 [6144, 2048], P('mp', ('dp', 'head')), may hold values from -0.078125 to 0.078125
Outputs:
- block_out: bfloat16 [2, 8192, 2048], P(None, ('dp', 'head', 'mp'))
- input_grad: bfloat16 [2, 8192, 2048], P(None, ('dp', 'head', 'mp'))
- grad_attn_norm_gain: float32 [2048], replicated
- grad_q_norm_gain: float32 [128], replicated
- grad_k_norm_gain: float32 [128], replicated
- grad_w_query: float32 [2048, 2048], P(('dp', 'mp'), 'head')
- grad_w_key: float32 [2048, 1024], P(('dp', 'mp'), 'head')
- grad_w_value: float32 [2048, 1024], P(('dp', 'mp'), 'head')
- grad_w_headgate: float32 [2048, 16], P(('dp', 'mp'), 'head')
- grad_w_out: float32 [2048, 2048], P('head', ('dp', 'mp'))
- grad_ffn_norm_gain: float32 [2048], replicated
- grad_w_gate: float32 [2048, 6144], P(('dp', 'head'), 'mp')
- grad_w_up: float32 [2048, 6144], P(('dp', 'head'), 'mp')
- grad_w_down: float32 [6144, 2048], P('mp', ('dp', 'head'))
The draws below stay inside these ranges and needn't reach their ends.
Inputs may be any that keep to these rules, and one draw needn't show every extreme that they name: `seq_counts`: at least one sequence has exactly 2048 tokens. `seq_bucket`: A permutation: each bucket holds exactly one sequence.
All inputs are finite; a program needn't handle non-finite values.
Results may differ from the reference program's by a relative error of at most 0.024.
Values may be sent and summed in bfloat16 or wider, within the bound.
A program may use at most 184 MiB of HBM per device.

```python
import jax
import jax.numpy as jnp
from jax import lax

D = 2048
HEADS = 16
KV = 8
HD = 128
FF = 6144
LEN = 2048
MIN_LEN = 1024
MB = 2
SEQS = 8
ROWS = 8192
N_DP = 4


def draw_seq_counts(key, part):
    draw_key, pick_key = jax.random.split(key)
    levels = jax.random.randint(draw_key, (SEQS,), 0, 56)
    counts = MIN_LEN + (LEN - MIN_LEN) * levels * levels // 3025
    longest = jax.random.randint(pick_key, (), 0, SEQS)
    return jnp.where(jnp.arange(SEQS) == longest, LEN, counts).astype(jnp.int32)


def level_of(key, shape, cuts, low, largest):
    factor_of, own = 1.0, jax.random.fold_in(key, 6)
    for position, shards_of in cuts:
        draws = jnp.exp(jax.random.uniform(jax.random.fold_in(own, position), (shards_of,), jnp.float32, low / len(cuts), largest / len(cuts)))
        factor_of = factor_of * jnp.repeat(draws, shape[position] // shards_of).reshape([-1 if axis == position else 1 for axis in range(len(shape))])
    return factor_of


def gaussian(stream_key, extent, scale, limit, shards=(), held_as=jnp.bfloat16):
    factor_of = level_of(stream_key, extent, shards, -0.22, 0.18) if shards else 1.0
    result = jax.random.normal(stream_key, extent, jnp.float32) * scale * factor_of
    return jnp.minimum(jnp.maximum(result, -limit), limit).astype(held_as)


def setup_inputs(seed: int = 0) -> dict:
    arg_keys = jax.random.split(jax.random.key(seed), 17)
    inputs = gaussian(arg_keys[0], (MB, ROWS, D), 1.0, 6.0, ((1, 32),))
    cotangent = gaussian(arg_keys[1], (MB, ROWS, D), 1.0, 6.0, ((1, 32),))
    seq_counts = draw_seq_counts(jax.random.fold_in(arg_keys[16], 71), 0)
    seq_bucket = jax.random.permutation(arg_keys[3], SEQS).astype(jnp.int32)
    attn_norm_gain = jnp.clip(1.0 + 0.1 * jax.random.normal(arg_keys[4], (D,), jnp.float32), 0.5, 1.5)
    q_norm_gain = jnp.clip(1.0 + 0.18 * jax.random.normal(arg_keys[5], (HD,), jnp.float32), 0.1, 1.9)
    k_norm_gain = jnp.clip(1.0 + 0.18 * jax.random.normal(arg_keys[6], (HD,), jnp.float32), 0.1, 1.9)
    w_query = gaussian(arg_keys[7], (D, HEADS * HD), D ** -0.5, 0.125, ((0, 8), (1, 4)))
    w_key = gaussian(arg_keys[8], (D, KV * HD), D ** -0.5, 0.125, ((0, 8), (1, 4)))
    w_value = gaussian(arg_keys[9], (D, KV * HD), D ** -0.5, 0.125, ((0, 8), (1, 4)))
    w_headgate = gaussian(arg_keys[10], (D, HEADS), D ** -0.5, 0.125, ((0, 8), (1, 4)))
    w_out = gaussian(arg_keys[11], (HEADS * HD, D), (max(1, HEADS * HD // 1024)) ** -0.5, 4.0, ((0, 4), (1, 8)))
    ffn_norm_gain = jnp.clip(1.0 + 0.1 * jax.random.normal(arg_keys[12], (D,), jnp.float32), 0.5, 1.5)
    w_gate = gaussian(arg_keys[13], (D, FF), D ** -0.5, 0.125, ((0, 16), (1, 2)))
    w_up = gaussian(arg_keys[14], (D, FF), D ** -0.5, 0.125, ((0, 16), (1, 2)))
    w_down = gaussian(arg_keys[15], (FF, D), FF ** -0.5, 0.078125, ((0, 2), (1, 16)))
    return dict(inputs=inputs, cotangent=cotangent, seq_counts=seq_counts, seq_bucket=seq_bucket, attn_norm_gain=attn_norm_gain, q_norm_gain=q_norm_gain, k_norm_gain=k_norm_gain, w_query=w_query, w_key=w_key, w_value=w_value, w_headgate=w_headgate, w_out=w_out, ffn_norm_gain=ffn_norm_gain, w_gate=w_gate, w_up=w_up, w_down=w_down)


EPS = 1e-06
ROPE_BASE = 1000000.0
NEG_FILL = -1e+30
HIGH = lax.Precision.HIGHEST

@jax.custom_vjp
def low(v):
    return lax.optimization_barrier(v.astype(jnp.bfloat16)).astype(jnp.float32)

@jax.custom_vjp
def low_back(v):
    return v

def low_keep(v):
    return (low(v), None)

def low_pass(kept, grad):
    return (grad,)

def back_keep(v):
    return (v, None)

def back_low(kept, grad):
    return (low(grad),)
low.defvjp(low_keep, low_pass)
low_back.defvjp(back_keep, back_low)

def matmul(left, right):
    return jnp.dot(left, right, precision=HIGH, preferred_element_type=jnp.float32)

def rms_scale(values):
    return lax.rsqrt(lax.optimization_barrier(jnp.mean(values * values, axis=-1, keepdims=True)) + EPS)

def rope_tables(positions, half):
    freq = jnp.power(ROPE_BASE, -jnp.arange(half, dtype=jnp.float32) / half)
    angle = positions.astype(jnp.float32)[:, None] * freq[None, :]
    return (jnp.cos(angle)[:, None, :], jnp.sin(angle)[:, None, :])

def rotate(values, cosine, sine):
    half = values.shape[-1] // 2
    first = values[..., :half]
    second = values[..., half:]
    return jnp.concatenate([first * cosine - second * sine, second * cosine + first * sine], axis=-1)

def attend(query, key, value, live_count):
    group_size = HEADS // KV
    q_block = min(512, LEN)
    positions = jnp.arange(LEN, dtype=jnp.int32)
    live_key = positions < live_count

    def query_block(piece):
        q_piece, q_pos = piece
        q_group = q_piece.reshape(q_block, KV, group_size, HD)
        scores = low_back(jnp.einsum('qhgd,khd->hgqk', q_group, key, precision=HIGH))
        allowed = (positions[None, :] <= q_pos[:, None]) & live_key[None, :]
        scores = jnp.where(allowed, scores, NEG_FILL)
        row_max = lax.optimization_barrier(jnp.max(scores, axis=-1, keepdims=True))
        exp_scores = jnp.where(allowed, jnp.exp(scores - row_max), 0.0)
        prob_rows = exp_scores / lax.optimization_barrier(jnp.sum(exp_scores, axis=-1, keepdims=True))
        prob_low = low(prob_rows)
        attn_o = jnp.einsum('hgqk,khd->qhgd', prob_low, value, precision=HIGH)
        return attn_o.reshape(q_block, HEADS, HD)
    q_pieces = query.reshape(LEN // q_block, q_block, HEADS, HD)
    out_pieces = lax.map(jax.checkpoint(query_block), (q_pieces, positions.reshape(LEN // q_block, q_block)))
    return out_pieces.reshape(LEN, HEADS, HD)

def layer_forward(params, rows, live_count):
    g_attn, g_query, g_key, wq, wk, wv, wg, wo, g_ffn, wgate, wup, wdown = params
    positions = jnp.arange(LEN, dtype=jnp.int32)
    cosine, sine = rope_tables(positions, HD // 2)
    xn1 = low(rows * rms_scale(rows) * g_attn)
    q_raw = low_back(matmul(xn1, wq)).reshape(LEN, HEADS, HD)
    k_raw = low_back(matmul(xn1, wk)).reshape(LEN, KV, HD)
    value = low(low_back(matmul(xn1, wv))).reshape(LEN, KV, HD)
    gate_logit = low_back(matmul(xn1, wg))
    query = low(rotate(q_raw * rms_scale(q_raw) * g_query, cosine, sine) * HD ** (-0.5))
    key = low(rotate(k_raw * rms_scale(k_raw) * g_key, cosine, sine))
    attn_o = low_back(attend(query, key, value, live_count))
    gated = low(attn_o * jax.nn.sigmoid(gate_logit)[..., None]).reshape(LEN, HEADS * HD)
    hidden1 = rows + low_back(matmul(gated, wo))
    xn2 = low(hidden1 * rms_scale(hidden1) * g_ffn)
    gate_pre = low_back(matmul(xn2, wgate))
    up_pre = low_back(matmul(xn2, wup))
    hidden = low(jax.nn.silu(gate_pre) * up_pre)
    return hidden1 + low_back(matmul(hidden, wdown))

def reference(inputs, cotangent, seq_counts, seq_bucket, attn_norm_gain, q_norm_gain, k_norm_gain, w_query, w_key, w_value, w_headgate, w_out, ffn_norm_gain, w_gate, w_up, w_down):
    params = tuple((a.astype(jnp.float32) for a in (attn_norm_gain, q_norm_gain, k_norm_gain, w_query, w_key, w_value, w_headgate, w_out, ffn_norm_gain, w_gate, w_up, w_down)))
    slot_ids = jnp.arange(SEQS, dtype=jnp.int32)
    slot_count = lax.optimization_barrier(jnp.sum(jnp.where(seq_bucket[None, :] == slot_ids[:, None], seq_counts[None, :], 0), axis=1)).astype(jnp.int32)
    rows_all = inputs.astype(jnp.float32).reshape(MB * N_DP, LEN, D)
    cot_all = cotangent.astype(jnp.float32).reshape(MB * N_DP, LEN, D)
    positions = jnp.arange(LEN, dtype=jnp.int32)

    def per_slot(grad_sum, slot_item):
        rows, cot_rows, live_count = slot_item
        layer_out, pull_back = jax.vjp(lambda p, r: layer_forward(p, r, live_count), params, rows)
        live = (positions < live_count).astype(jnp.float32)[:, None]
        slot_grads, row_grads = pull_back(cot_rows * live)
        grad_sum = tuple((a + b for a, b in zip(grad_sum, slot_grads)))
        return (grad_sum, (layer_out.astype(jnp.bfloat16), row_grads.astype(jnp.bfloat16)))
    zero_grads = tuple((jnp.zeros_like(p) for p in params))
    grad_sum, (outputs, input_grads) = lax.scan(per_slot, zero_grads, (rows_all, cot_all, slot_count))
    return (outputs.reshape(MB, ROWS, D), input_grads.reshape(MB, ROWS, D), grad_sum[0], grad_sum[1], grad_sum[2], grad_sum[3], grad_sum[4], grad_sum[5], grad_sum[6], grad_sum[7], grad_sum[8], grad_sum[9], grad_sum[10], grad_sum[11])
```

```python
import functools

import jax
import jax.numpy as jnp
from jax import lax
from jax.experimental import pallas as pl
from jax.experimental.pallas import tpu as pltpu
from jax.sharding import PartitionSpec as P

EPS = 1e-06
ROPE_BASE = 1000000.0
NEG_FILL = -1e30


def rms_scale(values):
    return lax.rsqrt(jnp.mean(values * values, axis=-1, keepdims=True) + EPS)


def norm_back(grad_out, normed, scale_rows, gain):
    d_normed = grad_out * gain
    return scale_rows * (d_normed - normed * jnp.mean(d_normed * normed, axis=-1, keepdims=True))


def rope_tables(positions, half):
    freq = jnp.power(ROPE_BASE, -jnp.arange(half, dtype=jnp.float32) / half)
    angle = positions.astype(jnp.float32)[:, None] * freq[None, :]
    return (jnp.cos(angle)[:, None, :], jnp.sin(angle)[:, None, :])


def rotate(values, cosine, sine):
    half = values.shape[-1] // 2
    first = values[..., :half]
    second = values[..., half:]
    return jnp.concatenate(
        [first * cosine - second * sine, second * cosine + first * sine], axis=-1
    )


def rotate_back(grads, cosine, sine):
    half = grads.shape[-1] // 2
    first = grads[..., :half]
    second = grads[..., half:]
    return jnp.concatenate(
        [first * cosine + second * sine, second * cosine - first * sine], axis=-1
    )


def masked_scores(q_group, key_piece, query_pos, key_pos, live_count):
    scores = jnp.einsum("qhgd,khd->hgqk", q_group, key_piece, preferred_element_type=jnp.float32)
    allowed = (key_pos[None, :] <= query_pos[:, None]) & (key_pos[None, :] < live_count)
    return (scores, allowed)


def split_keys(keys, values, key_pos, key_block):
    n_blocks = keys.shape[0] // key_block
    key_pieces = keys.reshape(n_blocks, key_block, keys.shape[1], keys.shape[2])
    value_pieces = values.reshape(n_blocks, key_block, values.shape[1], values.shape[2])
    return (key_pieces, value_pieces, key_pos.reshape(n_blocks, key_block))


def attend_forward(q_group, keys, values, query_pos, key_pos, live_count, key_block):
    n_query, kv_here, group_size, head_dim = q_group.shape
    key_pieces, value_pieces, pos_pieces = split_keys(keys, values, key_pos, key_block)

    def stats(carry, piece):
        row_max, row_total = carry
        key_piece, piece_pos = piece
        scores, allowed = masked_scores(q_group, key_piece, query_pos, piece_pos, live_count)
        scores = jnp.where(allowed, scores, NEG_FILL)
        new_max = jnp.maximum(row_max, jnp.max(scores, axis=-1))
        kept_exp = jnp.where(allowed, jnp.exp(scores - new_max[..., None]), 0.0)
        row_total = row_total * jnp.exp(row_max - new_max) + jnp.sum(kept_exp, axis=-1)
        return ((new_max, row_total), None)

    start = (
        jnp.full((kv_here, group_size, n_query), NEG_FILL, jnp.float32),
        jnp.zeros((kv_here, group_size, n_query), jnp.float32),
    )
    (row_max, row_total), unused = lax.scan(stats, start, (key_pieces, pos_pieces))
    log_total = row_max + jnp.log(row_total)

    def weigh(acc, piece):
        key_piece, value_piece, piece_pos = piece
        scores, allowed = masked_scores(q_group, key_piece, query_pos, piece_pos, live_count)
        prob_low = jnp.where(allowed, jnp.exp(scores - log_total[..., None]), 0.0).astype(
            jnp.bfloat16
        )
        acc = acc + jnp.einsum(
            "hgqk,khd->qhgd", prob_low, value_piece, preferred_element_type=jnp.float32
        )
        return (acc, None)

    attn_o, unused = lax.scan(
        weigh, jnp.zeros(q_group.shape, jnp.float32), (key_pieces, value_pieces, pos_pieces)
    )
    return (attn_o, log_total)


def attend_backward(
    q_group, keys, values, query_pos, key_pos, live_count, key_block, log_total, d_out, delta
):
    kv_here = keys.shape[1]
    head_dim = keys.shape[2]
    key_pieces, value_pieces, pos_pieces = split_keys(keys, values, key_pos, key_block)

    def backstep(d_query, piece):
        key_piece, value_piece, piece_pos = piece
        scores, allowed = masked_scores(q_group, key_piece, query_pos, piece_pos, live_count)
        probs = jnp.where(allowed, jnp.exp(scores - log_total[..., None]), 0.0)
        d_probs = jnp.einsum(
            "qhgd,khd->hgqk", d_out, value_piece, preferred_element_type=jnp.float32
        )
        d_scores = (probs * (d_probs - delta[..., None])).astype(jnp.bfloat16)
        d_query = d_query + jnp.einsum(
            "hgqk,khd->qhgd", d_scores, key_piece, preferred_element_type=jnp.float32
        )
        d_key = jnp.einsum("hgqk,qhgd->khd", d_scores, q_group, preferred_element_type=jnp.float32)
        d_value = jnp.einsum(
            "hgqk,qhgd->khd", probs.astype(jnp.bfloat16), d_out, preferred_element_type=jnp.float32
        )
        return (d_query, (d_key, d_value))

    d_query, (d_key, d_value) = lax.scan(
        backstep, jnp.zeros(q_group.shape, jnp.float32), (key_pieces, value_pieces, pos_pieces)
    )
    return (d_query, d_key.reshape(-1, kv_here * head_dim), d_value.reshape(-1, kv_here * head_dim))


def gather_weights(w_query, w_key, w_value, w_headgate, w_out, w_gate, w_up, w_down):
    attn_parts = (
        lax.all_gather(w_query, ("dp", "mp"), axis=0, tiled=True),
        lax.all_gather(w_key, ("dp", "mp"), axis=0, tiled=True),
        lax.all_gather(w_value, ("dp", "mp"), axis=0, tiled=True),
        lax.all_gather(w_headgate, ("dp", "mp"), axis=0, tiled=True),
        lax.all_gather(w_out, ("dp", "mp"), axis=1, tiled=True),
    )
    ffn_parts = (
        lax.all_gather(w_gate, ("dp", "head"), axis=0, tiled=True),
        lax.all_gather(w_up, ("dp", "head"), axis=0, tiled=True),
        lax.all_gather(w_down, ("dp", "head"), axis=1, tiled=True),
    )
    return tuple(attn_parts) + tuple(ffn_parts)


def reduce_grads(g_query, g_key, g_value, g_headgate, g_out, g_gate, g_up, g_down):
    attn_parts = (
        lax.psum_scatter(
            g_query.astype(jnp.bfloat16), ("dp", "mp"), scatter_dimension=0, tiled=True
        ).astype(jnp.float32),
        lax.psum_scatter(
            g_key.astype(jnp.bfloat16), ("dp", "mp"), scatter_dimension=0, tiled=True
        ).astype(jnp.float32),
        lax.psum_scatter(
            g_value.astype(jnp.bfloat16), ("dp", "mp"), scatter_dimension=0, tiled=True
        ).astype(jnp.float32),
        lax.psum_scatter(
            g_headgate.astype(jnp.bfloat16), ("dp", "mp"), scatter_dimension=0, tiled=True
        ).astype(jnp.float32),
        lax.psum_scatter(
            g_out.astype(jnp.bfloat16), ("dp", "mp"), scatter_dimension=1, tiled=True
        ).astype(jnp.float32),
    )
    ffn_parts = (
        lax.psum_scatter(
            g_gate.astype(jnp.bfloat16), ("dp", "head"), scatter_dimension=0, tiled=True
        ).astype(jnp.float32),
        lax.psum_scatter(
            g_up.astype(jnp.bfloat16), ("dp", "head"), scatter_dimension=0, tiled=True
        ).astype(jnp.float32),
        lax.psum_scatter(
            g_down.astype(jnp.bfloat16), ("dp", "head"), scatter_dimension=1, tiled=True
        ).astype(jnp.float32),
    )
    return tuple(attn_parts) + tuple(ffn_parts)


def local(
    inputs,
    cotangent,
    seq_counts,
    seq_bucket,
    attn_norm_gain,
    q_norm_gain,
    k_norm_gain,
    w_query,
    w_key,
    w_value,
    w_headgate,
    w_out,
    ffn_norm_gain,
    w_gate,
    w_up,
    w_down,
):
    micro_batches, row_count, model_width = inputs.shape
    n_head = lax.axis_size("head")
    n_mp = lax.axis_size("mp")
    n_dp = lax.axis_size("dp")
    head_idx = lax.axis_index("head")
    mp_idx = lax.axis_index("mp")
    dp_idx = lax.axis_index("dp")
    head_dim = q_norm_gain.shape[0]
    q_heads = w_query.shape[1] // head_dim
    kv_heads = w_key.shape[1] // head_dim
    group_size = q_heads // kv_heads
    q_scale = head_dim ** (-0.5)
    seq_len = row_count * n_head * n_mp
    key_block = min(512, seq_len)
    n_query = n_head * row_count
    slot_ids = jnp.arange(micro_batches * n_dp, dtype=jnp.int32)
    slot_count = jnp.sum(
        jnp.where(seq_bucket[None, :] == slot_ids[:, None], seq_counts[None, :], 0), axis=1
    )
    local_idx = jnp.arange(row_count, dtype=jnp.int32)
    own_pos = head_idx * n_mp * row_count + mp_idx * row_count + local_idx
    query_idx = jnp.arange(n_query, dtype=jnp.int32)
    query_pos = (
        query_idx // row_count * n_mp * row_count + mp_idx * row_count + query_idx % row_count
    )
    key_idx = jnp.arange(seq_len, dtype=jnp.int32)
    key_pos = (
        key_idx % n_query // row_count * n_mp * row_count
        + key_idx // n_query * row_count
        + key_idx % row_count
    )
    rope_cos, rope_sin = rope_tables(query_pos, head_dim // 2)
    grad_total = None
    gain_attn = jnp.zeros((model_width,), jnp.float32)
    gain_query = jnp.zeros((head_dim,), jnp.float32)
    gain_key = jnp.zeros((head_dim,), jnp.float32)
    gain_ffn = jnp.zeros((model_width,), jnp.float32)
    outputs = []
    input_grads = []
    for micro_batch in range(micro_batches):
        weights = gather_weights(w_query, w_key, w_value, w_headgate, w_out, w_gate, w_up, w_down)
        wq_full, wk_full, wv_full, wg_full, wo_full, wgate_full, wup_full, wdown_full = weights
        live_count = slot_count[micro_batch * n_dp + dp_idx]
        x_float = inputs[micro_batch].astype(jnp.float32)
        scale1 = rms_scale(x_float)
        normed1 = x_float * scale1
        xn1 = (normed1 * attn_norm_gain).astype(jnp.bfloat16)
        gathered_rows = lax.all_gather(xn1, "head", axis=0, tiled=True)
        q_raw = jnp.dot(gathered_rows, wq_full, preferred_element_type=jnp.float32).reshape(
            n_query, q_heads, head_dim
        )
        k_raw = jnp.dot(gathered_rows, wk_full, preferred_element_type=jnp.float32).reshape(
            n_query, kv_heads, head_dim
        )
        value_low = jnp.dot(gathered_rows, wv_full, preferred_element_type=jnp.float32).astype(
            jnp.bfloat16
        )
        gate_logit = jnp.dot(gathered_rows, wg_full, preferred_element_type=jnp.float32)
        q_rms = rms_scale(q_raw)
        q_hat = q_raw * q_rms
        query_low = (rotate(q_hat * q_norm_gain, rope_cos, rope_sin) * q_scale).astype(jnp.bfloat16)
        k_rms = rms_scale(k_raw)
        k_hat = k_raw * k_rms
        key_low = rotate(k_hat * k_norm_gain, rope_cos, rope_sin).astype(jnp.bfloat16)
        all_keys, all_values = (
            lax.all_gather(key_low.reshape(n_query, kv_heads * head_dim), "mp", axis=0, tiled=True),
            lax.all_gather(value_low, "mp", axis=0, tiled=True),
        )
        all_keys = all_keys.reshape(seq_len, kv_heads, head_dim)
        all_values = all_values.reshape(seq_len, kv_heads, head_dim)
        q_group = query_low.reshape(n_query, kv_heads, group_size, head_dim)
        attn_o, log_total = attend_forward(
            q_group, all_keys, all_values, query_pos, key_pos, live_count, key_block
        )
        gate_prob = jax.nn.sigmoid(gate_logit)
        attn_heads = attn_o.reshape(n_query, q_heads, head_dim)
        gated = (
            (attn_heads * gate_prob[..., None])
            .reshape(n_query, q_heads * head_dim)
            .astype(jnp.bfloat16)
        )
        attn_sum = lax.psum_scatter(
            jnp.dot(gated, wo_full, preferred_element_type=jnp.float32).astype(jnp.bfloat16),
            "head",
            scatter_dimension=0,
            tiled=True,
        ).astype(jnp.float32)
        hidden1 = x_float + attn_sum
        scale2 = rms_scale(hidden1)
        normed2 = hidden1 * scale2
        xn2 = (normed2 * ffn_norm_gain).astype(jnp.bfloat16)
        live = (own_pos < live_count).astype(jnp.float32)[:, None]
        cot_live = cotangent[micro_batch].astype(jnp.float32) * live
        ffn_in, cot_rows = (
            lax.all_gather(xn2, "mp", axis=0, tiled=True),
            lax.all_gather(cot_live.astype(jnp.bfloat16), "mp", axis=0, tiled=True),
        )
        gate_pre = jnp.dot(ffn_in, wgate_full, preferred_element_type=jnp.float32)
        up_pre = jnp.dot(ffn_in, wup_full, preferred_element_type=jnp.float32)
        gate_sig = jax.nn.sigmoid(gate_pre)
        gate_act = gate_pre * gate_sig
        hidden = (gate_act * up_pre).astype(jnp.bfloat16)
        ffn_sum = lax.psum_scatter(
            jnp.dot(hidden, wdown_full, preferred_element_type=jnp.float32).astype(jnp.bfloat16),
            "mp",
            scatter_dimension=0,
            tiled=True,
        ).astype(jnp.float32)
        outputs.append((hidden1 + ffn_sum).astype(jnp.bfloat16))
        d_hidden = jnp.einsum("rd,fd->rf", cot_rows, wdown_full, preferred_element_type=jnp.float32)
        grad_down = jnp.einsum("rf,rd->fd", hidden, cot_rows, preferred_element_type=jnp.float32)
        d_up = (d_hidden * gate_act).astype(jnp.bfloat16)
        d_gate = (d_hidden * up_pre * gate_sig * (1.0 + gate_pre * (1.0 - gate_sig))).astype(
            jnp.bfloat16
        )
        grad_gate = jnp.einsum("rd,rf->df", ffn_in, d_gate, preferred_element_type=jnp.float32)
        grad_up = jnp.einsum("rd,rf->df", ffn_in, d_up, preferred_element_type=jnp.float32)
        ffn_term = jnp.einsum(
            "rf,df->rd", d_gate, wgate_full, preferred_element_type=jnp.float32
        ) + jnp.einsum("rf,df->rd", d_up, wup_full, preferred_element_type=jnp.float32)
        d_xn2 = lax.psum_scatter(
            ffn_term.astype(jnp.bfloat16), "mp", scatter_dimension=0, tiled=True
        ).astype(jnp.float32)
        gain_ffn = gain_ffn + jnp.sum(d_xn2 * normed2, axis=0)
        d_hidden1 = cot_live + norm_back(d_xn2, normed2, scale2, ffn_norm_gain)
        d_attn = lax.all_gather(d_hidden1.astype(jnp.bfloat16), "head", axis=0, tiled=True)
        d_gated = jnp.einsum(
            "rd,cd->rc", d_attn, wo_full, preferred_element_type=jnp.float32
        ).reshape(n_query, q_heads, head_dim)
        grad_out = jnp.einsum("rc,rd->cd", gated, d_attn, preferred_element_type=jnp.float32)
        d_out_low = (d_gated * gate_prob[..., None]).astype(jnp.bfloat16)
        d_gate_logit = (
            jnp.sum(d_gated * attn_heads, axis=-1) * gate_prob * (1.0 - gate_prob)
        ).astype(jnp.bfloat16)
        grad_headgate = jnp.einsum(
            "rd,rc->dc", gathered_rows, d_gate_logit, preferred_element_type=jnp.float32
        )
        d_out_group = d_out_low.reshape(n_query, kv_heads, group_size, head_dim)
        delta = jnp.transpose(jnp.sum(d_out_group.astype(jnp.float32) * attn_o, axis=-1), (1, 2, 0))
        d_query, d_key_all, d_value_all = attend_backward(
            q_group,
            all_keys,
            all_values,
            query_pos,
            key_pos,
            live_count,
            key_block,
            log_total,
            d_out_group,
            delta,
        )
        d_key_own, d_value_own = (
            lax.psum_scatter(
                d_key_all.astype(jnp.bfloat16), "mp", scatter_dimension=0, tiled=True
            ).astype(jnp.float32),
            lax.psum_scatter(
                d_value_all.astype(jnp.bfloat16), "mp", scatter_dimension=0, tiled=True
            ).astype(jnp.float32),
        )
        dq_norm = rotate_back(
            (d_query * q_scale).reshape(n_query, q_heads, head_dim), rope_cos, rope_sin
        )
        gain_query = gain_query + jnp.sum(dq_norm * q_hat, axis=(0, 1))
        d_q_raw = (
            norm_back(dq_norm, q_hat, q_rms, q_norm_gain)
            .reshape(n_query, q_heads * head_dim)
            .astype(jnp.bfloat16)
        )
        dk_norm = rotate_back(d_key_own.reshape(n_query, kv_heads, head_dim), rope_cos, rope_sin)
        gain_key = gain_key + jnp.sum(dk_norm * k_hat, axis=(0, 1))
        d_k_raw = (
            norm_back(dk_norm, k_hat, k_rms, k_norm_gain)
            .reshape(n_query, kv_heads * head_dim)
            .astype(jnp.bfloat16)
        )
        d_value_low = d_value_own.astype(jnp.bfloat16)
        grad_query = jnp.einsum(
            "rd,rc->dc", gathered_rows, d_q_raw, preferred_element_type=jnp.float32
        )
        grad_key = jnp.einsum(
            "rd,rc->dc", gathered_rows, d_k_raw, preferred_element_type=jnp.float32
        )
        grad_value = jnp.einsum(
            "rd,rc->dc", gathered_rows, d_value_low, preferred_element_type=jnp.float32
        )
        attn_term = jnp.einsum("rc,dc->rd", d_q_raw, wq_full, preferred_element_type=jnp.float32)
        attn_term = attn_term + jnp.einsum(
            "rc,dc->rd", d_k_raw, wk_full, preferred_element_type=jnp.float32
        )
        attn_term = attn_term + jnp.einsum(
            "rc,dc->rd", d_value_low, wv_full, preferred_element_type=jnp.float32
        )
        attn_term = attn_term + jnp.einsum(
            "rc,dc->rd", d_gate_logit, wg_full, preferred_element_type=jnp.float32
        )
        d_xn1 = lax.psum_scatter(
            attn_term.astype(jnp.bfloat16), "head", scatter_dimension=0, tiled=True
        ).astype(jnp.float32)
        gain_attn = gain_attn + jnp.sum(d_xn1 * normed1, axis=0)
        input_grads.append(
            (d_hidden1 + norm_back(d_xn1, normed1, scale1, attn_norm_gain)).astype(jnp.bfloat16)
        )
        batch_grads = reduce_grads(
            grad_query, grad_key, grad_value, grad_headgate, grad_out, grad_gate, grad_up, grad_down
        )
        if grad_total is None:
            grad_total = batch_grads
        else:
            grad_total = tuple((a + b for a, b in zip(grad_total, batch_grads)))
    sum_attn, sum_query, sum_key, sum_ffn = lax.psum(
        (gain_attn, gain_query, gain_key, gain_ffn), ("dp", "head", "mp")
    )
    return (
        jnp.stack(outputs),
        jnp.stack(input_grads),
        sum_attn,
        sum_query,
        sum_key,
        grad_total[0],
        grad_total[1],
        grad_total[2],
        grad_total[3],
        grad_total[4],
        sum_ffn,
        grad_total[5],
        grad_total[6],
        grad_total[7],
    )


PLANE = ("head", "mp")
BIT_X, BIT_C, BIT_Y = 1, 2, 4
NT = (((1,), (1,)), ((), ()))
NN = (((1,), (0,)), ((), ()))
TN = (((0,), (0,)), ((), ()))
F32 = jnp.float32
BF16 = jnp.bfloat16


def dot(left, right, dims=NN):
    return lax.dot_general(left, right, dims, preferred_element_type=F32)


def swap(values, bits):
    return lax.ppermute(values, PLANE, [(i, i ^ bits) for i in range(8)])


def swap_mixed(values):
    return lax.ppermute(
        values, PLANE, [(i, i ^ (BIT_Y if i & BIT_C else BIT_X)) for i in range(8)]
    )


def gather_rows(rows, core):
    from_x = swap(rows, BIT_X)
    from_y = swap(rows, BIT_Y)
    diagonal = swap_mixed(jnp.where(core == 0, from_y, from_x))
    mine = jnp.concatenate([rows, from_x, from_y, diagonal], axis=0)
    return (mine, swap(mine, BIT_C))


def scatter_rows(mine, other, core):
    count = mine.shape[0] // 4
    summed = (mine + swap(other.astype(BF16), BIT_C).astype(F32)).astype(BF16)
    own, to_x, to_y, diagonal = [summed[k * count : (k + 1) * count] for k in range(4)]
    passed = swap_mixed(diagonal).astype(F32)
    zero = jnp.zeros((), F32)
    to_x = (to_x.astype(F32) + jnp.where(core == 1, passed, zero)).astype(BF16)
    to_y = (to_y.astype(F32) + jnp.where(core == 0, passed, zero)).astype(BF16)
    return own.astype(F32) + swap(to_x, BIT_X).astype(F32) + swap(to_y, BIT_Y).astype(F32)


def norm_rope(raw, gain, cosine, sine):
    scale_rows = lax.rsqrt(jnp.mean(raw * raw, axis=-1, keepdims=True) + EPS)
    hat = raw * scale_rows
    turned = hat * gain
    return (turned * cosine + pltpu.roll(turned, 64, 1) * sine, hat, scale_rows)


def norm_rope_back(grad, hat, scale_rows, gain, cosine, sine):
    grad_n = grad * cosine - pltpu.roll(grad, 64, 1) * sine
    gain_part = jnp.sum(grad_n * hat, axis=0, keepdims=True)
    scaled = grad_n * gain
    raw = scale_rows * (scaled - hat * jnp.mean(scaled * hat, axis=-1, keepdims=True))
    return (raw, gain_part)


def two_lanes(first, second, shape):
    lane = lax.broadcasted_iota(jnp.int32, shape, 1)
    return jnp.where(lane == 0, first, jnp.where(lane == 1, second, 0.0))


def attend_forward_kernel(
    table, proj, cosine, sine, q_gain, k_gain, gated, attn_o, lse, keys, values, acc
):
    step = pl.program_id(0)
    rows = proj.shape[0]
    live = table[8]
    cos_b, sin_b = cosine[...], sine[...]
    here = pl.multiple_of(step * rows, rows)
    key, _, _ = norm_rope(proj[:, 256:384], k_gain[...], cos_b, sin_b)
    keys[pl.ds(here, rows), :] = key.astype(BF16)
    values[pl.ds(here, rows), 0:128] = proj[:, 384:512].astype(BF16)
    values[pl.ds(here, rows), 128:256] = jnp.ones((rows, 128), BF16)
    q_scale = 128**-0.5
    first, _, _ = norm_rope(proj[:, 0:128], q_gain[...], cos_b, sin_b)
    second, _, _ = norm_rope(proj[:, 128:256], q_gain[...], cos_b, sin_b)
    query = (jnp.concatenate([first, second], axis=0) * q_scale).astype(BF16)
    row = lax.broadcasted_iota(jnp.int32, (2 * rows, rows), 0)
    column = lax.broadcasted_iota(jnp.int32, (2 * rows, rows), 1)
    scores = dot(query, keys[pl.ds(here, rows), :], NT)
    allowed = (column <= jnp.where(row >= rows, row - rows, row)) & (column + here < live)
    weight = jnp.where(allowed, jnp.exp(scores), 0.0).astype(BF16)
    acc[...] = dot(weight, values[pl.ds(here, rows), :])

    def block(index, carry):
        there = pl.multiple_of(index * rows, rows)
        part = dot(query, keys[pl.ds(there, rows), :], NT)
        kept = jnp.where(column + there < live, jnp.exp(part), 0.0).astype(BF16)
        acc[...] += dot(kept, values[pl.ds(there, rows), :])
        return carry

    lax.fori_loop(0, step, block, 0)
    total = acc[:, 128:129]
    out = acc[:, 0:128] / total
    log_total = jnp.log(total)
    gate0 = jax.nn.sigmoid(proj[:, 512:513])
    gate1 = jax.nn.sigmoid(proj[:, 513:514])
    attn_o[:, 0:128] = out[:rows]
    attn_o[:, 128:256] = out[rows:]
    gated[:, 0:128] = (out[:rows] * gate0).astype(BF16)
    gated[:, 128:256] = (out[rows:] * gate1).astype(BF16)
    lse[...] = two_lanes(log_total[:rows], log_total[rows:], (rows, 128))


def attend_backward_kernel(
    table,
    proj,
    d_gated,
    attn_o,
    lse,
    cosine,
    sine,
    q_gain,
    k_gain,
    d_proj,
    gain_q,
    gain_k,
    keys,
    keys_t,
    values,
    k_raw,
    d_keys,
    d_values,
    d_query,
):
    step = pl.program_id(0)
    rows = proj.shape[0]
    live = table[8]
    here = pl.multiple_of(step * rows, rows)
    slot = pl.multiple_of(table[step] * rows, rows)
    cos_b, sin_b = cosine[pl.ds(here, rows), :], sine[pl.ds(here, rows), :]
    raw_key = proj[:, 256:384]
    k_raw[pl.ds(here, rows), :] = raw_key
    key, _, _ = norm_rope(raw_key, k_gain[...], cos_b, sin_b)
    key = key.astype(BF16)
    keys[pl.ds(here, rows), :] = key
    keys_t[step] = key.T
    value = proj[:, 384:512].astype(BF16)
    values[pl.ds(here, rows), :] = value
    q_scale = 128**-0.5
    first, hat0, scale0 = norm_rope(proj[:, 0:128], q_gain[...], cos_b, sin_b)
    second, hat1, scale1 = norm_rope(proj[:, 128:256], q_gain[...], cos_b, sin_b)
    query = (jnp.concatenate([first, second], axis=0) * q_scale).astype(BF16)
    gate0 = jax.nn.sigmoid(proj[:, 512:513])
    gate1 = jax.nn.sigmoid(proj[:, 513:514])
    dg0, dg1 = d_gated[:, 0:128], d_gated[:, 128:256]
    out0, out1 = attn_o[:, 0:128], attn_o[:, 128:256]
    do0, do1 = (dg0 * gate0).astype(BF16), (dg1 * gate1).astype(BF16)
    logit0 = jnp.sum(dg0 * out0, axis=-1, keepdims=True) * gate0 * (1.0 - gate0)
    logit1 = jnp.sum(dg1 * out1, axis=-1, keepdims=True) * gate1 * (1.0 - gate1)
    d_proj[pl.ds(slot, rows), 512:640] = two_lanes(logit0, logit1, (rows, 128)).astype(BF16)
    delta0 = jnp.sum(do0.astype(F32) * out0, axis=-1, keepdims=True)
    delta1 = jnp.sum(do1.astype(F32) * out1, axis=-1, keepdims=True)
    delta_t = two_lanes(delta0, delta1, (rows, 128)).T
    delta = jnp.concatenate([delta_t[0:1], delta_t[1:2]], axis=1)
    lse_t = lse[...].T
    log_total = jnp.concatenate([lse_t[0:1], lse_t[1:2]], axis=1)
    d_out = jnp.concatenate([do0, do1], axis=0)
    key_row = lax.broadcasted_iota(jnp.int32, (rows, 2 * rows), 0)
    q_col = lax.broadcasted_iota(jnp.int32, (rows, 2 * rows), 1)

    def pieces(key_b, value_b, allowed):
        scores = dot(key_b, query, NT)
        probs = jnp.where(allowed, jnp.exp(scores - log_total), 0.0)
        d_probs = dot(value_b, d_out, NT)
        d_scores = (probs * (d_probs - delta)).astype(BF16)
        return (probs.astype(BF16), d_scores)

    allowed = (key_row <= jnp.where(q_col >= rows, q_col - rows, q_col)) & (key_row + here < live)
    probs, d_scores = pieces(key, value, allowed)
    d_values[pl.ds(here, rows), :] = dot(probs, d_out)
    d_keys[pl.ds(here, rows), :] = dot(d_scores, query)
    d_query[...] = dot(keys_t[step], d_scores)

    def block(index, carry):
        there = pl.multiple_of(index * rows, rows)
        probs, d_scores = pieces(
            keys[pl.ds(there, rows), :], values[pl.ds(there, rows), :], key_row + there < live
        )
        d_values[pl.ds(there, rows), :] += dot(probs, d_out)
        d_keys[pl.ds(there, rows), :] += dot(d_scores, query)
        d_query[...] += dot(keys_t[index], d_scores)
        return carry

    lax.fori_loop(0, step, block, 0)
    grads = d_query[...].T * q_scale
    raw0, part0 = norm_rope_back(grads[:rows], hat0, scale0, q_gain[...], cos_b, sin_b)
    raw1, part1 = norm_rope_back(grads[rows:], hat1, scale1, q_gain[...], cos_b, sin_b)
    d_proj[pl.ds(slot, rows), 0:128] = raw0.astype(BF16)
    d_proj[pl.ds(slot, rows), 128:256] = raw1.astype(BF16)

    @pl.when(step == 0)
    def _():
        gain_q[...] = jnp.zeros_like(gain_q)
        gain_k[...] = jnp.zeros_like(gain_k)

    gain_q[0:1, :] += part0 + part1

    @pl.when(step == pl.num_programs(0) - 1)
    def _():
        def finish(index, carry):
            there = pl.multiple_of(index * rows, rows)
            to_slot = pl.multiple_of(table[index] * rows, rows)
            cos_k, sin_k = cosine[pl.ds(there, rows), :], sine[pl.ds(there, rows), :]
            _, hat, scale_rows = norm_rope(k_raw[pl.ds(there, rows), :], k_gain[...], cos_k, sin_k)
            raw, part = norm_rope_back(
                d_keys[pl.ds(there, rows), :], hat, scale_rows, k_gain[...], cos_k, sin_k
            )
            gain_k[0:1, :] += part
            d_proj[pl.ds(to_slot, rows), 256:384] = raw.astype(BF16)
            d_proj[pl.ds(to_slot, rows), 384:512] = d_values[pl.ds(there, rows), :].astype(BF16)
            return carry

        lax.fori_loop(0, pl.num_programs(0), finish, 0)


def attend_costs(seq_len, matmuls):
    pairs = 2 * seq_len * (seq_len + 256) // 2
    return pl.CostEstimate(
        flops=2 * matmuls * pairs * 128, bytes_accessed=12 * seq_len * 640, transcendentals=pairs
    )


def attend_forward_call(table, proj, cosine, sine, q_gain, k_gain):
    seq_len = proj.shape[0]
    rows = seq_len // 8
    by_slot = lambda i, t: (t[i], 0)
    by_place = lambda i, t: (i, 0)
    fixed = lambda i, t: (0, 0)
    return pl.pallas_call(
        attend_forward_kernel,
        grid_spec=pltpu.PrefetchScalarGridSpec(
            num_scalar_prefetch=1,
            grid=(8,),
            in_specs=[
                pl.BlockSpec((rows, 640), by_slot),
                pl.BlockSpec((rows, 128), by_place),
                pl.BlockSpec((rows, 128), by_place),
                pl.BlockSpec((1, 128), fixed),
                pl.BlockSpec((1, 128), fixed),
            ],
            out_specs=[
                pl.BlockSpec((rows, 256), by_slot),
                pl.BlockSpec((rows, 256), by_slot),
                pl.BlockSpec((rows, 128), by_slot),
            ],
            scratch_shapes=[
                pltpu.VMEM((seq_len, 128), BF16),
                pltpu.VMEM((seq_len, 256), BF16),
                pltpu.VMEM((2 * rows, 256), F32),
            ],
        ),
        out_shape=[
            jax.ShapeDtypeStruct((seq_len, 256), BF16),
            jax.ShapeDtypeStruct((seq_len, 256), F32),
            jax.ShapeDtypeStruct((seq_len, 128), F32),
        ],
        compiler_params=pltpu.CompilerParams(
            dimension_semantics=("arbitrary",), vmem_limit_bytes=32 << 20
        ),
        cost_estimate=attend_costs(seq_len, 2),
        name="attend_forward",
    )(table, proj, cosine, sine, q_gain, k_gain)


def attend_backward_call(table, proj, d_gated, attn_o, lse, cosine, sine, q_gain, k_gain):
    seq_len = proj.shape[0]
    rows = seq_len // 8
    by_slot = lambda i, t: (t[i], 0)
    fixed = lambda i, t: (0, 0)
    return pl.pallas_call(
        attend_backward_kernel,
        grid_spec=pltpu.PrefetchScalarGridSpec(
            num_scalar_prefetch=1,
            grid=(8,),
            in_specs=[
                pl.BlockSpec((rows, 640), by_slot),
                pl.BlockSpec((rows, 256), by_slot),
                pl.BlockSpec((rows, 256), by_slot),
                pl.BlockSpec((rows, 128), by_slot),
                pl.BlockSpec((seq_len, 128), fixed),
                pl.BlockSpec((seq_len, 128), fixed),
                pl.BlockSpec((1, 128), fixed),
                pl.BlockSpec((1, 128), fixed),
            ],
            out_specs=[
                pl.BlockSpec((seq_len, 640), fixed),
                pl.BlockSpec((8, 128), fixed),
                pl.BlockSpec((8, 128), fixed),
            ],
            scratch_shapes=[
                pltpu.VMEM((seq_len, 128), BF16),
                pltpu.VMEM((8, 128, rows), BF16),
                pltpu.VMEM((seq_len, 128), BF16),
                pltpu.VMEM((seq_len, 128), F32),
                pltpu.VMEM((seq_len, 128), F32),
                pltpu.VMEM((seq_len, 128), F32),
                pltpu.VMEM((128, 2 * rows), F32),
            ],
        ),
        out_shape=[
            jax.ShapeDtypeStruct((seq_len, 640), BF16),
            jax.ShapeDtypeStruct((8, 128), F32),
            jax.ShapeDtypeStruct((8, 128), F32),
        ],
        compiler_params=pltpu.CompilerParams(
            dimension_semantics=("arbitrary",), vmem_limit_bytes=40 << 20
        ),
        cost_estimate=attend_costs(seq_len, 5),
        name="attend_backward",
    )(table, proj, d_gated, attn_o, lse, cosine, sine, q_gain, k_gain)


def pick(flag, first, second):
    return jnp.where(flag, first, second)


def reorder_by(pieces, index):
    low, high = (index & 1) == 1, (index & 2) == 2
    swapped = [pick(low, pieces[j ^ 1], pieces[j]) for j in range(4)]
    return [pick(high, swapped[j ^ 2], swapped[j]) for j in range(4)]


def local_plane(
    inputs,
    cotangent,
    seq_counts,
    seq_bucket,
    attn_norm_gain,
    q_norm_gain,
    k_norm_gain,
    w_query,
    w_key,
    w_value,
    w_headgate,
    w_out,
    ffn_norm_gain,
    w_gate,
    w_up,
    w_down,
):
    micro_batches, row_count, model_width = inputs.shape
    n_dp = lax.axis_size("dp")
    head_idx = lax.axis_index("head")
    mp_idx = lax.axis_index("mp")
    dp_idx = lax.axis_index("dp")
    core = head_idx & 1
    plane_idx = head_idx * 2 + mp_idx
    seq_len = row_count * 8
    ffn_cols = w_gate.shape[1] // 4
    slot_ids = jnp.arange(micro_batches * n_dp, dtype=jnp.int32)
    slot_count = jnp.sum(
        jnp.where(seq_bucket[None, :] == slot_ids[:, None], seq_counts[None, :], 0), axis=1
    )
    own_pos = plane_idx * row_count + jnp.arange(row_count, dtype=jnp.int32)
    apart = jnp.arange(8, dtype=jnp.int32) ^ plane_idx
    slots = (apart & 1) | ((apart & 4) >> 1) | ((apart & 2) << 1)
    table_cos, table_sin = rope_tables(jnp.arange(seq_len, dtype=jnp.int32), 64)
    table_cos, table_sin = table_cos[:, 0, :], table_sin[:, 0, :]
    cosine = jnp.concatenate([table_cos, table_cos], axis=1)
    sine = jnp.concatenate([-table_sin, table_sin], axis=1)
    q_gain, k_gain = q_norm_gain[None, :], k_norm_gain[None, :]

    spare = jnp.zeros((row_count, 126), BF16)
    halves = [
        jnp.concatenate(
            [
                w_query[:, k * 256 : (k + 1) * 256],
                w_key[:, k * 128 : (k + 1) * 128],
                w_value[:, k * 128 : (k + 1) * 128],
                w_headgate[:, k * 2 : (k + 1) * 2],
                spare,
                w_out[k * 256 : (k + 1) * 256, :].T,
            ],
            axis=1,
        )
        for k in range(2)
    ]
    is_first = mp_idx == 0
    kept = pick(is_first, halves[0], halves[1])
    came = swap(pick(is_first, halves[1], halves[0]), BIT_X)
    attn_rows = jnp.concatenate([pick(is_first, kept, came), pick(is_first, came, kept)], axis=0)
    attn_full = lax.all_gather(attn_rows, "dp", axis=0, tiled=True)
    w_proj, w_out_t = attn_full[:, :640], attn_full[:, 640:]

    down_t = w_down.T
    quarters = jnp.stack(
        [
            jnp.concatenate(
                [w[:, k * ffn_cols : (k + 1) * ffn_cols] for w in (w_gate, w_up, down_t)], axis=1
            )
            for k in range(4)
        ]
    )
    traded = [lax.dynamic_index_in_dim(quarters, head_idx, 0, False)] + [
        swap(lax.dynamic_index_in_dim(quarters, head_idx ^ r, 0, False), r * 2) for r in (1, 2, 3)
    ]
    ffn_rows = jnp.concatenate(reorder_by(traded, head_idx), axis=0)
    w_gate_up = lax.all_gather(ffn_rows[:, : 2 * ffn_cols], "dp", axis=0, tiled=True)
    w_down_t = lax.all_gather(ffn_rows[:, 2 * ffn_cols :], "dp", axis=0, tiled=True)

    outputs, input_grads = ([], [])
    gain_attn = jnp.zeros((model_width,), F32)
    gain_ffn = jnp.zeros((model_width,), F32)
    gain_query = jnp.zeros((128,), F32)
    gain_key = jnp.zeros((128,), F32)
    grad_gate_up = grad_down_t = grad_proj = grad_out_t = None

    def plus(total, term):
        return term if total is None else total + term

    for micro_batch in range(micro_batches):
        live_count = slot_count[micro_batch * n_dp + dp_idx]
        table = jnp.concatenate([slots, live_count[None]]).astype(jnp.int32)
        x_float = inputs[micro_batch].astype(F32)
        scale1 = rms_scale(x_float)
        normed1 = x_float * scale1
        xn1 = gather_rows((normed1 * attn_norm_gain).astype(BF16), core)
        live = (own_pos < live_count).astype(F32)[:, None]
        cot_live = cotangent[micro_batch].astype(F32) * live
        cot_rows = gather_rows(cot_live.astype(BF16), core)
        proj = jnp.concatenate([dot(piece, w_proj) for piece in xn1], axis=0)
        gated, attn_o, lse = attend_forward_call(table, proj, cosine, sine, q_gain, k_gain)
        half = seq_len // 2
        gated_pieces = (gated[:half], gated[half:])
        out_other = dot(gated_pieces[1], w_out_t, NT)
        out_mine = dot(gated_pieces[0], w_out_t, NT)
        hidden1 = x_float + scatter_rows(out_mine, out_other, core)
        scale2 = rms_scale(hidden1)
        normed2 = hidden1 * scale2
        xn2 = gather_rows((normed2 * ffn_norm_gain).astype(BF16), core)
        down_parts, back_parts = ([], [])
        for xn2_piece, cot_piece in zip(xn2, cot_rows):
            pre = dot(xn2_piece, w_gate_up)
            gate_pre, up_pre = pre[:, :ffn_cols], pre[:, ffn_cols:]
            gate_sig = jax.nn.sigmoid(gate_pre)
            gate_act = gate_pre * gate_sig
            hidden = (gate_act * up_pre).astype(BF16)
            d_hidden = dot(cot_piece, w_down_t)
            d_up = (d_hidden * gate_act).astype(BF16)
            d_gate = (d_hidden * up_pre * gate_sig * (1.0 + gate_pre * (1.0 - gate_sig))).astype(
                BF16
            )
            d_both = jnp.concatenate([d_gate, d_up], axis=1)
            down_parts.append(dot(hidden, w_down_t, NT))
            back_parts.append(dot(d_both, w_gate_up, NT))
            grad_gate_up = plus(grad_gate_up, dot(xn2_piece, d_both, TN))
            grad_down_t = plus(grad_down_t, dot(cot_piece, hidden, TN))
        outputs.append((hidden1 + scatter_rows(down_parts[0], down_parts[1], core)).astype(BF16))
        d_xn2 = scatter_rows(back_parts[0], back_parts[1], core)
        gain_ffn = gain_ffn + jnp.sum(d_xn2 * normed2, axis=0)
        d_hidden1 = cot_live + norm_back(d_xn2, normed2, scale2, ffn_norm_gain)
        d_attn = gather_rows(d_hidden1.astype(BF16), core)
        d_gated = jnp.concatenate([dot(piece, w_out_t) for piece in d_attn], axis=0)
        for d_piece, gated_piece in zip(d_attn, gated_pieces):
            grad_out_t = plus(grad_out_t, dot(d_piece, gated_piece, TN))
        d_proj, part_q, part_k = attend_backward_call(
            table, proj, d_gated, attn_o, lse, cosine, sine, q_gain, k_gain
        )
        gain_query = gain_query + part_q[0]
        gain_key = gain_key + part_k[0]
        d_pieces = (d_proj[:half], d_proj[half:])
        for x_piece, d_piece in zip(xn1, d_pieces):
            grad_proj = plus(grad_proj, dot(x_piece, d_piece, TN))
        term_other = dot(d_pieces[1], w_proj, NT)
        term_mine = dot(d_pieces[0], w_proj, NT)
        d_xn1 = scatter_rows(term_mine, term_other, core)
        gain_attn = gain_attn + jnp.sum(d_xn1 * normed1, axis=0)
        input_grads.append(
            (d_hidden1 + norm_back(d_xn1, normed1, scale1, attn_norm_gain)).astype(BF16)
        )

    sum_ffn = [
        lax.psum_scatter(g.astype(BF16), "dp", scatter_dimension=0, tiled=True)
        for g in (grad_gate_up, grad_down_t)
    ]
    ffn_sum = jnp.concatenate(sum_ffn, axis=1).reshape(4, -1, 3 * ffn_cols)
    back = [lax.dynamic_index_in_dim(ffn_sum, head_idx, 0, False)] + [
        swap(lax.dynamic_index_in_dim(ffn_sum, head_idx ^ r, 0, False), r * 2) for r in (1, 2, 3)
    ]
    back = reorder_by(back, head_idx)
    grad_gate, grad_up, grad_down = [
        jnp.concatenate([b[:, k * ffn_cols : (k + 1) * ffn_cols] for b in back], axis=1).astype(F32)
        for k in range(3)
    ]
    grad_down = grad_down.T
    attn_grads = jnp.concatenate([grad_proj, grad_out_t], axis=1).astype(BF16)
    attn_sum = lax.psum_scatter(attn_grads, "dp", scatter_dimension=0, tiled=True)
    upper, lower = attn_sum[:row_count], attn_sum[row_count:]
    kept = pick(is_first, upper, lower)
    came = swap(pick(is_first, lower, upper), BIT_X)
    by_half = [v.astype(F32) for v in (pick(is_first, kept, came), pick(is_first, came, kept))]
    grad_query = jnp.concatenate([v[:, 0:256] for v in by_half], axis=1)
    grad_key = jnp.concatenate([v[:, 256:384] for v in by_half], axis=1)
    grad_value = jnp.concatenate([v[:, 384:512] for v in by_half], axis=1)
    grad_headgate = jnp.concatenate([v[:, 512:514] for v in by_half], axis=1)
    grad_out = jnp.concatenate([v[:, 640:896].T for v in by_half], axis=0)
    sum_attn, sum_query, sum_key, sum_gain_ffn = lax.psum(
        (gain_attn, gain_query, gain_key, gain_ffn), ("dp", "head", "mp")
    )
    return (
        jnp.stack(outputs),
        jnp.stack(input_grads),
        sum_attn,
        sum_query,
        sum_key,
        grad_query,
        grad_key,
        grad_value,
        grad_headgate,
        grad_out,
        sum_gain_ffn,
        grad_gate,
        grad_up,
        grad_down,
    )


def choose_local(mesh):
    if mesh.shape["head"] == 4 and mesh.shape["mp"] == 2:
        return local_plane
    return local


def solution(mesh):
    placed = (
        P(None, ("dp", "head", "mp"), None),
        P(None, ("dp", "head", "mp"), None),
        P(),
        P(),
        P(),
        P(),
        P(),
        P(("dp", "mp"), "head"),
        P(("dp", "mp"), "head"),
        P(("dp", "mp"), "head"),
        P(("dp", "mp"), "head"),
        P("head", ("dp", "mp")),
        P(),
        P(("dp", "head"), "mp"),
        P(("dp", "head"), "mp"),
        P("mp", ("dp", "head")),
    )
    return jax.shard_map(
        choose_local(mesh),
        mesh=mesh,
        in_specs=placed,
        out_specs=(
            P(None, ("dp", "head", "mp"), None),
            P(None, ("dp", "head", "mp"), None),
            P(),
            P(),
            P(),
            P(("dp", "mp"), "head"),
            P(("dp", "mp"), "head"),
            P(("dp", "mp"), "head"),
            P(("dp", "mp"), "head"),
            P("head", ("dp", "mp")),
            P(),
            P(("dp", "head"), "mp"),
            P(("dp", "head"), "mp"),
            P("mp", ("dp", "head")),
        ),
        check_vma=False,
    )
```

```python
import functools

import jax
import jax.numpy as jnp
from jax import lax
from jax.experimental import pallas as pl
from jax.experimental.pallas import tpu as pltpu
from jax.sharding import PartitionSpec as P

EPS = 1e-06
ROPE_BASE = 1000000.0
NEG_FILL = -1e30


def rms_scale(values):
    return lax.rsqrt(jnp.mean(values * values, axis=-1, keepdims=True) + EPS)


def norm_back(grad_out, normed, scale_rows, gain):
    d_normed = grad_out * gain
    return scale_rows * (d_normed - normed * jnp.mean(d_normed * normed, axis=-1, keepdims=True))


def rope_tables(positions, half):
    freq = jnp.power(ROPE_BASE, -jnp.arange(half, dtype=jnp.float32) / half)
    angle = positions.astype(jnp.float32)[:, None] * freq[None, :]
    return (jnp.cos(angle)[:, None, :], jnp.sin(angle)[:, None, :])


def rotate(values, cosine, sine):
    half = values.shape[-1] // 2
    first = values[..., :half]
    second = values[..., half:]
    return jnp.concatenate(
        [first * cosine - second * sine, second * cosine + first * sine], axis=-1
    )


def rotate_back(grads, cosine, sine):
    half = grads.shape[-1] // 2
    first = grads[..., :half]
    second = grads[..., half:]
    return jnp.concatenate(
        [first * cosine + second * sine, second * cosine - first * sine], axis=-1
    )


def masked_scores(q_group, key_piece, query_pos, key_pos, live_count):
    scores = jnp.einsum("qhgd,khd->hgqk", q_group, key_piece, preferred_element_type=jnp.float32)
    allowed = (key_pos[None, :] <= query_pos[:, None]) & (key_pos[None, :] < live_count)
    return (scores, allowed)


def split_keys(keys, values, key_pos, key_block):
    n_blocks = keys.shape[0] // key_block
    key_pieces = keys.reshape(n_blocks, key_block, keys.shape[1], keys.shape[2])
    value_pieces = values.reshape(n_blocks, key_block, values.shape[1], values.shape[2])
    return (key_pieces, value_pieces, key_pos.reshape(n_blocks, key_block))


def attend_forward(q_group, keys, values, query_pos, key_pos, live_count, key_block):
    n_query, kv_here, group_size, head_dim = q_group.shape
    key_pieces, value_pieces, pos_pieces = split_keys(keys, values, key_pos, key_block)

    def stats(carry, piece):
        row_max, row_total = carry
        key_piece, piece_pos = piece
        scores, allowed = masked_scores(q_group, key_piece, query_pos, piece_pos, live_count)
        scores = jnp.where(allowed, scores, NEG_FILL)
        new_max = jnp.maximum(row_max, jnp.max(scores, axis=-1))
        kept_exp = jnp.where(allowed, jnp.exp(scores - new_max[..., None]), 0.0)
        row_total = row_total * jnp.exp(row_max - new_max) + jnp.sum(kept_exp, axis=-1)
        return ((new_max, row_total), None)

    start = (
        jnp.full((kv_here, group_size, n_query), NEG_FILL, jnp.float32),
        jnp.zeros((kv_here, group_size, n_query), jnp.float32),
    )
    (row_max, row_total), unused = lax.scan(stats, start, (key_pieces, pos_pieces))
    log_total = row_max + jnp.log(row_total)

    def weigh(acc, piece):
        key_piece, value_piece, piece_pos = piece
        scores, allowed = masked_scores(q_group, key_piece, query_pos, piece_pos, live_count)
        prob_low = jnp.where(allowed, jnp.exp(scores - log_total[..., None]), 0.0).astype(
            jnp.bfloat16
        )
        acc = acc + jnp.einsum(
            "hgqk,khd->qhgd", prob_low, value_piece, preferred_element_type=jnp.float32
        )
        return (acc, None)

    attn_o, unused = lax.scan(
        weigh, jnp.zeros(q_group.shape, jnp.float32), (key_pieces, value_pieces, pos_pieces)
    )
    return (attn_o, log_total)


def attend_backward(
    q_group, keys, values, query_pos, key_pos, live_count, key_block, log_total, d_out, delta
):
    kv_here = keys.shape[1]
    head_dim = keys.shape[2]
    key_pieces, value_pieces, pos_pieces = split_keys(keys, values, key_pos, key_block)

    def backstep(d_query, piece):
        key_piece, value_piece, piece_pos = piece
        scores, allowed = masked_scores(q_group, key_piece, query_pos, piece_pos, live_count)
        probs = jnp.where(allowed, jnp.exp(scores - log_total[..., None]), 0.0)
        d_probs = jnp.einsum(
            "qhgd,khd->hgqk", d_out, value_piece, preferred_element_type=jnp.float32
        )
        d_scores = (probs * (d_probs - delta[..., None])).astype(jnp.bfloat16)
        d_query = d_query + jnp.einsum(
            "hgqk,khd->qhgd", d_scores, key_piece, preferred_element_type=jnp.float32
        )
        d_key = jnp.einsum("hgqk,qhgd->khd", d_scores, q_group, preferred_element_type=jnp.float32)
        d_value = jnp.einsum(
            "hgqk,qhgd->khd", probs.astype(jnp.bfloat16), d_out, preferred_element_type=jnp.float32
        )
        return (d_query, (d_key, d_value))

    d_query, (d_key, d_value) = lax.scan(
        backstep, jnp.zeros(q_group.shape, jnp.float32), (key_pieces, value_pieces, pos_pieces)
    )
    return (d_query, d_key.reshape(-1, kv_here * head_dim), d_value.reshape(-1, kv_here * head_dim))


def gather_weights(w_query, w_key, w_value, w_headgate, w_out, w_gate, w_up, w_down):
    attn_parts = (
        lax.all_gather(w_query, ("dp", "mp"), axis=0, tiled=True),
        lax.all_gather(w_key, ("dp", "mp"), axis=0, tiled=True),
        lax.all_gather(w_value, ("dp", "mp"), axis=0, tiled=True),
        lax.all_gather(w_headgate, ("dp", "mp"), axis=0, tiled=True),
        lax.all_gather(w_out, ("dp", "mp"), axis=1, tiled=True),
    )
    ffn_parts = (
        lax.all_gather(w_gate, ("dp", "head"), axis=0, tiled=True),
        lax.all_gather(w_up, ("dp", "head"), axis=0, tiled=True),
        lax.all_gather(w_down, ("dp", "head"), axis=1, tiled=True),
    )
    return tuple(attn_parts) + tuple(ffn_parts)


def reduce_grads(g_query, g_key, g_value, g_headgate, g_out, g_gate, g_up, g_down):
    attn_parts = (
        lax.psum_scatter(
            g_query.astype(jnp.bfloat16), ("dp", "mp"), scatter_dimension=0, tiled=True
        ).astype(jnp.float32),
        lax.psum_scatter(
            g_key.astype(jnp.bfloat16), ("dp", "mp"), scatter_dimension=0, tiled=True
        ).astype(jnp.float32),
        lax.psum_scatter(
            g_value.astype(jnp.bfloat16), ("dp", "mp"), scatter_dimension=0, tiled=True
        ).astype(jnp.float32),
        lax.psum_scatter(
            g_headgate.astype(jnp.bfloat16), ("dp", "mp"), scatter_dimension=0, tiled=True
        ).astype(jnp.float32),
        lax.psum_scatter(
            g_out.astype(jnp.bfloat16), ("dp", "mp"), scatter_dimension=1, tiled=True
        ).astype(jnp.float32),
    )
    ffn_parts = (
        lax.psum_scatter(
            g_gate.astype(jnp.bfloat16), ("dp", "head"), scatter_dimension=0, tiled=True
        ).astype(jnp.float32),
        lax.psum_scatter(
            g_up.astype(jnp.bfloat16), ("dp", "head"), scatter_dimension=0, tiled=True
        ).astype(jnp.float32),
        lax.psum_scatter(
            g_down.astype(jnp.bfloat16), ("dp", "head"), scatter_dimension=1, tiled=True
        ).astype(jnp.float32),
    )
    return tuple(attn_parts) + tuple(ffn_parts)


def local(
    inputs,
    cotangent,
    seq_counts,
    seq_bucket,
    attn_norm_gain,
    q_norm_gain,
    k_norm_gain,
    w_query,
    w_key,
    w_value,
    w_headgate,
    w_out,
    ffn_norm_gain,
    w_gate,
    w_up,
    w_down,
):
    micro_batches, row_count, model_width = inputs.shape
    n_head = lax.axis_size("head")
    n_mp = lax.axis_size("mp")
    n_dp = lax.axis_size("dp")
    head_idx = lax.axis_index("head")
    mp_idx = lax.axis_index("mp")
    dp_idx = lax.axis_index("dp")
    head_dim = q_norm_gain.shape[0]
    q_heads = w_query.shape[1] // head_dim
    kv_heads = w_key.shape[1] // head_dim
    group_size = q_heads // kv_heads
    q_scale = head_dim ** (-0.5)
    seq_len = row_count * n_head * n_mp
    key_block = min(512, seq_len)
    n_query = n_head * row_count
    slot_ids = jnp.arange(micro_batches * n_dp, dtype=jnp.int32)
    slot_count = jnp.sum(
        jnp.where(seq_bucket[None, :] == slot_ids[:, None], seq_counts[None, :], 0), axis=1
    )
    local_idx = jnp.arange(row_count, dtype=jnp.int32)
    own_pos = head_idx * n_mp * row_count + mp_idx * row_count + local_idx
    query_idx = jnp.arange(n_query, dtype=jnp.int32)
    query_pos = (
        query_idx // row_count * n_mp * row_count + mp_idx * row_count + query_idx % row_count
    )
    key_idx = jnp.arange(seq_len, dtype=jnp.int32)
    key_pos = (
        key_idx % n_query // row_count * n_mp * row_count
        + key_idx // n_query * row_count
        + key_idx % row_count
    )
    rope_cos, rope_sin = rope_tables(query_pos, head_dim // 2)
    grad_total = None
    gain_attn = jnp.zeros((model_width,), jnp.float32)
    gain_query = jnp.zeros((head_dim,), jnp.float32)
    gain_key = jnp.zeros((head_dim,), jnp.float32)
    gain_ffn = jnp.zeros((model_width,), jnp.float32)
    outputs = []
    input_grads = []
    for micro_batch in range(micro_batches):
        weights = gather_weights(w_query, w_key, w_value, w_headgate, w_out, w_gate, w_up, w_down)
        wq_full, wk_full, wv_full, wg_full, wo_full, wgate_full, wup_full, wdown_full = weights
        live_count = slot_count[micro_batch * n_dp + dp_idx]
        x_float = inputs[micro_batch].astype(jnp.float32)
        scale1 = rms_scale(x_float)
        normed1 = x_float * scale1
        xn1 = (normed1 * attn_norm_gain).astype(jnp.bfloat16)
        gathered_rows = lax.all_gather(xn1, "head", axis=0, tiled=True)
        q_raw = jnp.dot(gathered_rows, wq_full, preferred_element_type=jnp.float32).reshape(
            n_query, q_heads, head_dim
        )
        k_raw = jnp.dot(gathered_rows, wk_full, preferred_element_type=jnp.float32).reshape(
            n_query, kv_heads, head_dim
        )
        value_low = jnp.dot(gathered_rows, wv_full, preferred_element_type=jnp.float32).astype(
            jnp.bfloat16
        )
        gate_logit = jnp.dot(gathered_rows, wg_full, preferred_element_type=jnp.float32)
        q_rms = rms_scale(q_raw)
        q_hat = q_raw * q_rms
        query_low = (rotate(q_hat * q_norm_gain, rope_cos, rope_sin) * q_scale).astype(jnp.bfloat16)
        k_rms = rms_scale(k_raw)
        k_hat = k_raw * k_rms
        key_low = rotate(k_hat * k_norm_gain, rope_cos, rope_sin).astype(jnp.bfloat16)
        all_keys, all_values = (
            lax.all_gather(key_low.reshape(n_query, kv_heads * head_dim), "mp", axis=0, tiled=True),
            lax.all_gather(value_low, "mp", axis=0, tiled=True),
        )
        all_keys = all_keys.reshape(seq_len, kv_heads, head_dim)
        all_values = all_values.reshape(seq_len, kv_heads, head_dim)
        q_group = query_low.reshape(n_query, kv_heads, group_size, head_dim)
        attn_o, log_total = attend_forward(
            q_group, all_keys, all_values, query_pos, key_pos, live_count, key_block
        )
        gate_prob = jax.nn.sigmoid(gate_logit)
        attn_heads = attn_o.reshape(n_query, q_heads, head_dim)
        gated = (
            (attn_heads * gate_prob[..., None])
            .reshape(n_query, q_heads * head_dim)
            .astype(jnp.bfloat16)
        )
        attn_sum = lax.psum_scatter(
            jnp.dot(gated, wo_full, preferred_element_type=jnp.float32).astype(jnp.bfloat16),
            "head",
            scatter_dimension=0,
            tiled=True,
        ).astype(jnp.float32)
        hidden1 = x_float + attn_sum
        scale2 = rms_scale(hidden1)
        normed2 = hidden1 * scale2
        xn2 = (normed2 * ffn_norm_gain).astype(jnp.bfloat16)
        live = (own_pos < live_count).astype(jnp.float32)[:, None]
        cot_live = cotangent[micro_batch].astype(jnp.float32) * live
        ffn_in, cot_rows = (
            lax.all_gather(xn2, "mp", axis=0, tiled=True),
            lax.all_gather(cot_live.astype(jnp.bfloat16), "mp", axis=0, tiled=True),
        )
        gate_pre = jnp.dot(ffn_in, wgate_full, preferred_element_type=jnp.float32)
        up_pre = jnp.dot(ffn_in, wup_full, preferred_element_type=jnp.float32)
        gate_sig = jax.nn.sigmoid(gate_pre)
        gate_act = gate_pre * gate_sig
        hidden = (gate_act * up_pre).astype(jnp.bfloat16)
        ffn_sum = lax.psum_scatter(
            jnp.dot(hidden, wdown_full, preferred_element_type=jnp.float32).astype(jnp.bfloat16),
            "mp",
            scatter_dimension=0,
            tiled=True,
        ).astype(jnp.float32)
        outputs.append((hidden1 + ffn_sum).astype(jnp.bfloat16))
        d_hidden = jnp.einsum("rd,fd->rf", cot_rows, wdown_full, preferred_element_type=jnp.float32)
        grad_down = jnp.einsum("rf,rd->fd", hidden, cot_rows, preferred_element_type=jnp.float32)
        d_up = (d_hidden * gate_act).astype(jnp.bfloat16)
        d_gate = (d_hidden * up_pre * gate_sig * (1.0 + gate_pre * (1.0 - gate_sig))).astype(
            jnp.bfloat16
        )
        grad_gate = jnp.einsum("rd,rf->df", ffn_in, d_gate, preferred_element_type=jnp.float32)
        grad_up = jnp.einsum("rd,rf->df", ffn_in, d_up, preferred_element_type=jnp.float32)
        ffn_term = jnp.einsum(
            "rf,df->rd", d_gate, wgate_full, preferred_element_type=jnp.float32
        ) + jnp.einsum("rf,df->rd", d_up, wup_full, preferred_element_type=jnp.float32)
        d_xn2 = lax.psum_scatter(
            ffn_term.astype(jnp.bfloat16), "mp", scatter_dimension=0, tiled=True
        ).astype(jnp.float32)
        gain_ffn = gain_ffn + jnp.sum(d_xn2 * normed2, axis=0)
        d_hidden1 = cot_live + norm_back(d_xn2, normed2, scale2, ffn_norm_gain)
        d_attn = lax.all_gather(d_hidden1.astype(jnp.bfloat16), "head", axis=0, tiled=True)
        d_gated = jnp.einsum(
            "rd,cd->rc", d_attn, wo_full, preferred_element_type=jnp.float32
        ).reshape(n_query, q_heads, head_dim)
        grad_out = jnp.einsum("rc,rd->cd", gated, d_attn, preferred_element_type=jnp.float32)
        d_out_low = (d_gated * gate_prob[..., None]).astype(jnp.bfloat16)
        d_gate_logit = (
            jnp.sum(d_gated * attn_heads, axis=-1) * gate_prob * (1.0 - gate_prob)
        ).astype(jnp.bfloat16)
        grad_headgate = jnp.einsum(
            "rd,rc->dc", gathered_rows, d_gate_logit, preferred_element_type=jnp.float32
        )
        d_out_group = d_out_low.reshape(n_query, kv_heads, group_size, head_dim)
        delta = jnp.transpose(jnp.sum(d_out_group.astype(jnp.float32) * attn_o, axis=-1), (1, 2, 0))
        d_query, d_key_all, d_value_all = attend_backward(
            q_group,
            all_keys,
            all_values,
            query_pos,
            key_pos,
            live_count,
            key_block,
            log_total,
            d_out_group,
            delta,
        )
        d_key_own, d_value_own = (
            lax.psum_scatter(
                d_key_all.astype(jnp.bfloat16), "mp", scatter_dimension=0, tiled=True
            ).astype(jnp.float32),
            lax.psum_scatter(
                d_value_all.astype(jnp.bfloat16), "mp", scatter_dimension=0, tiled=True
            ).astype(jnp.float32),
        )
        dq_norm = rotate_back(
            (d_query * q_scale).reshape(n_query, q_heads, head_dim), rope_cos, rope_sin
        )
        gain_query = gain_query + jnp.sum(dq_norm * q_hat, axis=(0, 1))
        d_q_raw = (
            norm_back(dq_norm, q_hat, q_rms, q_norm_gain)
            .reshape(n_query, q_heads * head_dim)
            .astype(jnp.bfloat16)
        )
        dk_norm = rotate_back(d_key_own.reshape(n_query, kv_heads, head_dim), rope_cos, rope_sin)
        gain_key = gain_key + jnp.sum(dk_norm * k_hat, axis=(0, 1))
        d_k_raw = (
            norm_back(dk_norm, k_hat, k_rms, k_norm_gain)
            .reshape(n_query, kv_heads * head_dim)
            .astype(jnp.bfloat16)
        )
        d_value_low = d_value_own.astype(jnp.bfloat16)
        grad_query = jnp.einsum(
            "rd,rc->dc", gathered_rows, d_q_raw, preferred_element_type=jnp.float32
        )
        grad_key = jnp.einsum(
            "rd,rc->dc", gathered_rows, d_k_raw, preferred_element_type=jnp.float32
        )
        grad_value = jnp.einsum(
            "rd,rc->dc", gathered_rows, d_value_low, preferred_element_type=jnp.float32
        )
        attn_term = jnp.einsum("rc,dc->rd", d_q_raw, wq_full, preferred_element_type=jnp.float32)
        attn_term = attn_term + jnp.einsum(
            "rc,dc->rd", d_k_raw, wk_full, preferred_element_type=jnp.float32
        )
        attn_term = attn_term + jnp.einsum(
            "rc,dc->rd", d_value_low, wv_full, preferred_element_type=jnp.float32
        )
        attn_term = attn_term + jnp.einsum(
            "rc,dc->rd", d_gate_logit, wg_full, preferred_element_type=jnp.float32
        )
        d_xn1 = lax.psum_scatter(
            attn_term.astype(jnp.bfloat16), "head", scatter_dimension=0, tiled=True
        ).astype(jnp.float32)
        gain_attn = gain_attn + jnp.sum(d_xn1 * normed1, axis=0)
        input_grads.append(
            (d_hidden1 + norm_back(d_xn1, normed1, scale1, attn_norm_gain)).astype(jnp.bfloat16)
        )
        batch_grads = reduce_grads(
            grad_query, grad_key, grad_value, grad_headgate, grad_out, grad_gate, grad_up, grad_down
        )
        if grad_total is None:
            grad_total = batch_grads
        else:
            grad_total = tuple((a + b for a, b in zip(grad_total, batch_grads)))
    sum_attn, sum_query, sum_key, sum_ffn = lax.psum(
        (gain_attn, gain_query, gain_key, gain_ffn), ("dp", "head", "mp")
    )
    return (
        jnp.stack(outputs),
        jnp.stack(input_grads),
        sum_attn,
        sum_query,
        sum_key,
        grad_total[0],
        grad_total[1],
        grad_total[2],
        grad_total[3],
        grad_total[4],
        sum_ffn,
        grad_total[5],
        grad_total[6],
        grad_total[7],
    )


PLANE = ("head", "mp")
BIT_X, BIT_C, BIT_Y = 1, 2, 4
NT = (((1,), (1,)), ((), ()))
NN = (((1,), (0,)), ((), ()))
TN = (((0,), (0,)), ((), ()))
F32 = jnp.float32
BF16 = jnp.bfloat16


def dot(left, right, dims=NN):
    return lax.dot_general(left, right, dims, preferred_element_type=F32)


def swap(values, bits):
    return lax.ppermute(values, PLANE, [(i, i ^ bits) for i in range(8)])


def swap_mixed(values, core0, core1):
    return lax.ppermute(
        values, PLANE, [(i, i ^ (core1 if i & BIT_C else core0)) for i in range(8)]
    )


class Gather:
    def __init__(self, rows):
        self.rows = rows
        self.came = swap_mixed(rows, BIT_X, BIT_Y)

    def second(self):
        self.pair = jnp.concatenate([self.rows, self.came], axis=0)
        self.came = swap_mixed(self.pair, BIT_Y, BIT_X)
        return self.pair

    def third(self):
        self.mine = jnp.concatenate([self.pair, self.came], axis=0)
        self.other = swap(self.mine, BIT_C)
        return self.mine


class Scatter:
    def __init__(self, other):
        self.came = swap(other, BIT_C)

    def second(self, summed):
        half = summed.shape[0] // 2
        self.kept = summed[:half]
        self.came = swap_mixed(summed[half:], BIT_Y, BIT_X)

    def third(self):
        pair = (self.kept.astype(F32) + self.came.astype(F32)).astype(BF16)
        half = pair.shape[0] // 2
        self.kept = pair[:half]
        self.came = swap_mixed(pair[half:], BIT_X, BIT_Y)
        return pair

    def result(self):
        return self.kept.astype(F32) + self.came.astype(F32)


class Order:
    def __init__(self):
        self.ahead = []

    def need(self, *values):
        self.ahead.extend(values)

    def run(self, op, *operands):
        if self.ahead:
            held = lax.optimization_barrier((tuple(operands), tuple(self.ahead)))
            operands = held[0]
        out = op(*operands)
        self.ahead = [out[0] if isinstance(out, (tuple, list)) else out]
        return out


def norm_rope(raw, gain, cosine, sine):
    scale_rows = lax.rsqrt(jnp.mean(raw * raw, axis=-1, keepdims=True) + EPS)
    hat = raw * scale_rows
    turned = hat * gain
    return (turned * cosine + pltpu.roll(turned, 64, 1) * sine, hat, scale_rows)


def norm_rope_back(grad, hat, scale_rows, gain, cosine, sine):
    grad_n = grad * cosine - pltpu.roll(grad, 64, 1) * sine
    gain_part = jnp.sum(grad_n * hat, axis=0, keepdims=True)
    scaled = grad_n * gain
    raw = scale_rows * (scaled - hat * jnp.mean(scaled * hat, axis=-1, keepdims=True))
    return (raw, gain_part)


def two_lanes(first, second, shape):
    lane = lax.broadcasted_iota(jnp.int32, shape, 1)
    return jnp.where(lane == 0, first, jnp.where(lane == 1, second, 0.0))


def attend_forward_kernel(
    table, proj, cosine, sine, q_gain, k_gain, gated, attn_o, lse, keys, values, acc
):
    step = pl.program_id(0)
    rows = proj.shape[0]
    live = table[8]
    cos_b, sin_b = cosine[...], sine[...]
    here = pl.multiple_of(step * rows, rows)
    key, _, _ = norm_rope(proj[:, 256:384], k_gain[...], cos_b, sin_b)
    keys[pl.ds(here, rows), :] = key.astype(BF16)
    values[pl.ds(here, rows), 0:128] = proj[:, 384:512].astype(BF16)
    values[pl.ds(here, rows), 128:256] = jnp.ones((rows, 128), BF16)
    q_scale = 128**-0.5
    first, _, _ = norm_rope(proj[:, 0:128], q_gain[...], cos_b, sin_b)
    second, _, _ = norm_rope(proj[:, 128:256], q_gain[...], cos_b, sin_b)
    query = (jnp.concatenate([first, second], axis=0) * q_scale).astype(BF16)
    row = lax.broadcasted_iota(jnp.int32, (2 * rows, rows), 0)
    column = lax.broadcasted_iota(jnp.int32, (2 * rows, rows), 1)
    scores = dot(query, keys[pl.ds(here, rows), :], NT)
    allowed = (column <= jnp.where(row >= rows, row - rows, row)) & (column + here < live)
    weight = jnp.where(allowed, jnp.exp(scores), 0.0).astype(BF16)
    acc[...] = dot(weight, values[pl.ds(here, rows), :])

    def block(index, carry):
        there = pl.multiple_of(index * rows, rows)
        part = dot(query, keys[pl.ds(there, rows), :], NT)
        kept = jnp.where(column + there < live, jnp.exp(part), 0.0).astype(BF16)
        acc[...] += dot(kept, values[pl.ds(there, rows), :])
        return carry

    lax.fori_loop(0, step, block, 0)
    total = acc[:, 128:129]
    out = acc[:, 0:128] / total
    log_total = jnp.log(total)
    gate0 = jax.nn.sigmoid(proj[:, 512:513])
    gate1 = jax.nn.sigmoid(proj[:, 513:514])
    attn_o[:, 0:128] = out[:rows]
    attn_o[:, 128:256] = out[rows:]
    gated[:, 0:128] = (out[:rows] * gate0).astype(BF16)
    gated[:, 128:256] = (out[rows:] * gate1).astype(BF16)
    lse[...] = two_lanes(log_total[:rows], log_total[rows:], (rows, 128))


def attend_backward_kernel(
    table,
    proj,
    d_gated,
    attn_o,
    lse,
    cosine,
    sine,
    q_gain,
    k_gain,
    d_proj,
    gain_q,
    gain_k,
    keys,
    keys_t,
    values,
    k_raw,
    d_keys,
    d_values,
    d_query,
):
    step = pl.program_id(0)
    rows = proj.shape[0]
    live = table[8]
    here = pl.multiple_of(step * rows, rows)
    slot = pl.multiple_of(table[step] * rows, rows)
    cos_b, sin_b = cosine[pl.ds(here, rows), :], sine[pl.ds(here, rows), :]
    raw_key = proj[:, 256:384]
    k_raw[pl.ds(here, rows), :] = raw_key
    key, _, _ = norm_rope(raw_key, k_gain[...], cos_b, sin_b)
    key = key.astype(BF16)
    keys[pl.ds(here, rows), :] = key
    keys_t[step] = key.T
    value = proj[:, 384:512].astype(BF16)
    values[pl.ds(here, rows), :] = value
    q_scale = 128**-0.5
    first, hat0, scale0 = norm_rope(proj[:, 0:128], q_gain[...], cos_b, sin_b)
    second, hat1, scale1 = norm_rope(proj[:, 128:256], q_gain[...], cos_b, sin_b)
    query = (jnp.concatenate([first, second], axis=0) * q_scale).astype(BF16)
    gate0 = jax.nn.sigmoid(proj[:, 512:513])
    gate1 = jax.nn.sigmoid(proj[:, 513:514])
    dg0, dg1 = d_gated[:, 0:128], d_gated[:, 128:256]
    out0, out1 = attn_o[:, 0:128], attn_o[:, 128:256]
    do0, do1 = (dg0 * gate0).astype(BF16), (dg1 * gate1).astype(BF16)
    logit0 = jnp.sum(dg0 * out0, axis=-1, keepdims=True) * gate0 * (1.0 - gate0)
    logit1 = jnp.sum(dg1 * out1, axis=-1, keepdims=True) * gate1 * (1.0 - gate1)
    d_proj[pl.ds(slot, rows), 512:640] = two_lanes(logit0, logit1, (rows, 128)).astype(BF16)
    delta0 = jnp.sum(do0.astype(F32) * out0, axis=-1, keepdims=True)
    delta1 = jnp.sum(do1.astype(F32) * out1, axis=-1, keepdims=True)
    delta_t = two_lanes(delta0, delta1, (rows, 128)).T
    delta = jnp.concatenate([delta_t[0:1], delta_t[1:2]], axis=1)
    lse_t = lse[...].T
    log_total = jnp.concatenate([lse_t[0:1], lse_t[1:2]], axis=1)
    d_out = jnp.concatenate([do0, do1], axis=0)
    key_row = lax.broadcasted_iota(jnp.int32, (rows, 2 * rows), 0)
    q_col = lax.broadcasted_iota(jnp.int32, (rows, 2 * rows), 1)

    def pieces(key_b, value_b, allowed):
        scores = dot(key_b, query, NT)
        probs = jnp.where(allowed, jnp.exp(scores - log_total), 0.0)
        d_probs = dot(value_b, d_out, NT)
        d_scores = (probs * (d_probs - delta)).astype(BF16)
        return (probs.astype(BF16), d_scores)

    allowed = (key_row <= jnp.where(q_col >= rows, q_col - rows, q_col)) & (key_row + here < live)
    probs, d_scores = pieces(key, value, allowed)
    d_values[pl.ds(here, rows), :] = dot(probs, d_out)
    d_keys[pl.ds(here, rows), :] = dot(d_scores, query)
    d_query[...] = dot(keys_t[step], d_scores)

    def block(index, carry):
        there = pl.multiple_of(index * rows, rows)
        probs, d_scores = pieces(
            keys[pl.ds(there, rows), :], values[pl.ds(there, rows), :], key_row + there < live
        )
        d_values[pl.ds(there, rows), :] += dot(probs, d_out)
        d_keys[pl.ds(there, rows), :] += dot(d_scores, query)
        d_query[...] += dot(keys_t[index], d_scores)
        return carry

    lax.fori_loop(0, step, block, 0)
    grads = d_query[...].T * q_scale
    raw0, part0 = norm_rope_back(grads[:rows], hat0, scale0, q_gain[...], cos_b, sin_b)
    raw1, part1 = norm_rope_back(grads[rows:], hat1, scale1, q_gain[...], cos_b, sin_b)
    d_proj[pl.ds(slot, rows), 0:128] = raw0.astype(BF16)
    d_proj[pl.ds(slot, rows), 128:256] = raw1.astype(BF16)

    @pl.when(step == 0)
    def _():
        gain_q[...] = jnp.zeros_like(gain_q)
        gain_k[...] = jnp.zeros_like(gain_k)

    gain_q[0:1, :] += part0 + part1

    @pl.when(step == pl.num_programs(0) - 1)
    def _():
        def finish(index, carry):
            there = pl.multiple_of(index * rows, rows)
            to_slot = pl.multiple_of(table[index] * rows, rows)
            cos_k, sin_k = cosine[pl.ds(there, rows), :], sine[pl.ds(there, rows), :]
            _, hat, scale_rows = norm_rope(k_raw[pl.ds(there, rows), :], k_gain[...], cos_k, sin_k)
            raw, part = norm_rope_back(
                d_keys[pl.ds(there, rows), :], hat, scale_rows, k_gain[...], cos_k, sin_k
            )
            gain_k[0:1, :] += part
            d_proj[pl.ds(to_slot, rows), 256:384] = raw.astype(BF16)
            d_proj[pl.ds(to_slot, rows), 384:512] = d_values[pl.ds(there, rows), :].astype(BF16)
            return carry

        lax.fori_loop(0, pl.num_programs(0), finish, 0)


def attend_costs(seq_len, matmuls):
    pairs = 2 * seq_len * (seq_len + 256) // 2
    return pl.CostEstimate(
        flops=2 * matmuls * pairs * 128, bytes_accessed=12 * seq_len * 640, transcendentals=pairs
    )


def attend_forward_call(table, proj, cosine, sine, q_gain, k_gain):
    seq_len = proj.shape[0]
    rows = seq_len // 8
    by_slot = lambda i, t: (t[i], 0)
    by_place = lambda i, t: (i, 0)
    fixed = lambda i, t: (0, 0)
    return pl.pallas_call(
        attend_forward_kernel,
        grid_spec=pltpu.PrefetchScalarGridSpec(
            num_scalar_prefetch=1,
            grid=(8,),
            in_specs=[
                pl.BlockSpec((rows, 640), by_slot),
                pl.BlockSpec((rows, 128), by_place),
                pl.BlockSpec((rows, 128), by_place),
                pl.BlockSpec((1, 128), fixed),
                pl.BlockSpec((1, 128), fixed),
            ],
            out_specs=[
                pl.BlockSpec((rows, 256), by_slot),
                pl.BlockSpec((rows, 256), by_slot),
                pl.BlockSpec((rows, 128), by_slot),
            ],
            scratch_shapes=[
                pltpu.VMEM((seq_len, 128), BF16),
                pltpu.VMEM((seq_len, 256), BF16),
                pltpu.VMEM((2 * rows, 256), F32),
            ],
        ),
        out_shape=[
            jax.ShapeDtypeStruct((seq_len, 256), BF16),
            jax.ShapeDtypeStruct((seq_len, 256), F32),
            jax.ShapeDtypeStruct((seq_len, 128), F32),
        ],
        compiler_params=pltpu.CompilerParams(
            dimension_semantics=("arbitrary",), vmem_limit_bytes=32 << 20
        ),
        cost_estimate=attend_costs(seq_len, 2),
        name="attend_forward",
    )(table, proj, cosine, sine, q_gain, k_gain)


def attend_backward_call(table, proj, d_gated, attn_o, lse, cosine, sine, q_gain, k_gain):
    seq_len = proj.shape[0]
    rows = seq_len // 8
    by_slot = lambda i, t: (t[i], 0)
    fixed = lambda i, t: (0, 0)
    return pl.pallas_call(
        attend_backward_kernel,
        grid_spec=pltpu.PrefetchScalarGridSpec(
            num_scalar_prefetch=1,
            grid=(8,),
            in_specs=[
                pl.BlockSpec((rows, 640), by_slot),
                pl.BlockSpec((rows, 256), by_slot),
                pl.BlockSpec((rows, 256), by_slot),
                pl.BlockSpec((rows, 128), by_slot),
                pl.BlockSpec((seq_len, 128), fixed),
                pl.BlockSpec((seq_len, 128), fixed),
                pl.BlockSpec((1, 128), fixed),
                pl.BlockSpec((1, 128), fixed),
            ],
            out_specs=[
                pl.BlockSpec((seq_len, 640), fixed),
                pl.BlockSpec((8, 128), fixed),
                pl.BlockSpec((8, 128), fixed),
            ],
            scratch_shapes=[
                pltpu.VMEM((seq_len, 128), BF16),
                pltpu.VMEM((8, 128, rows), BF16),
                pltpu.VMEM((seq_len, 128), BF16),
                pltpu.VMEM((seq_len, 128), F32),
                pltpu.VMEM((seq_len, 128), F32),
                pltpu.VMEM((seq_len, 128), F32),
                pltpu.VMEM((128, 2 * rows), F32),
            ],
        ),
        out_shape=[
            jax.ShapeDtypeStruct((seq_len, 640), BF16),
            jax.ShapeDtypeStruct((8, 128), F32),
            jax.ShapeDtypeStruct((8, 128), F32),
        ],
        compiler_params=pltpu.CompilerParams(
            dimension_semantics=("arbitrary",), vmem_limit_bytes=40 << 20
        ),
        cost_estimate=attend_costs(seq_len, 5),
        name="attend_backward",
    )(table, proj, d_gated, attn_o, lse, cosine, sine, q_gain, k_gain)


def feed_forward_kernel(with_sum, *refs):
    if with_sum:
        rows, d_hidden, w_gate_up, w_down_t, down_in, back_in = refs[:6]
        hidden_out, d_pre_out, down_out, back_out = refs[6:]
    else:
        rows, d_hidden, w_gate_up, w_down_t = refs[:4]
        hidden_out, d_pre_out, down_out, back_out = refs[4:]
    units = d_hidden.shape[1]
    pre = dot(rows[...], w_gate_up[...])
    gate_pre, up_pre = pre[:, :units], pre[:, units:]
    gate_sig = jax.nn.sigmoid(gate_pre)
    gate_act = gate_pre * gate_sig
    d_hid = d_hidden[...].astype(F32)
    hidden = (gate_act * up_pre).astype(BF16)
    hidden_out[...] = hidden
    d_pre_out[:, units:] = (d_hid * gate_act).astype(BF16)
    d_pre_out[:, :units] = (
        d_hid * up_pre * gate_sig * (1.0 + gate_pre * (1.0 - gate_sig))
    ).astype(BF16)
    back = dot(d_pre_out[...], w_gate_up[...], NT)
    down = dot(hidden, w_down_t[...], NT)
    if with_sum:
        back = back + back_in[...].astype(F32)
        down = down + down_in[...].astype(F32)
    back_out[...] = back.astype(BF16)
    down_out[...] = down.astype(BF16)


def feed_forward_call(rows, d_hidden, w_gate_up, w_down_t, *sums):
    count, width = rows.shape
    units = d_hidden.shape[1]
    tile = min(256, count)
    by_row = lambda i: (i, 0)
    fixed = lambda i: (0, 0)
    wide = pl.BlockSpec((tile, width), by_row)
    return pl.pallas_call(
        functools.partial(feed_forward_kernel, bool(sums)),
        grid=(count // tile,),
        in_specs=[
            wide,
            pl.BlockSpec((tile, units), by_row),
            pl.BlockSpec((width, 2 * units), fixed, pipeline_mode=pl.Buffered(1)),
            pl.BlockSpec((width, units), fixed, pipeline_mode=pl.Buffered(1)),
        ]
        + [wide] * len(sums),
        out_specs=[
            pl.BlockSpec((tile, units), by_row),
            pl.BlockSpec((tile, 2 * units), by_row),
            wide,
            wide,
        ],
        out_shape=[
            jax.ShapeDtypeStruct((count, units), BF16),
            jax.ShapeDtypeStruct((count, 2 * units), BF16),
            jax.ShapeDtypeStruct((count, width), BF16),
            jax.ShapeDtypeStruct((count, width), BF16),
        ],
        compiler_params=pltpu.CompilerParams(
            dimension_semantics=("arbitrary",), vmem_limit_bytes=48 << 20
        ),
        cost_estimate=pl.CostEstimate(
            flops=2 * count * width * 5 * units,
            bytes_accessed=2 * (3 * count * width + 3 * width * units + 4 * count * units),
            transcendentals=count * units,
        ),
        name="feed_forward",
    )(rows, d_hidden, w_gate_up, w_down_t, *sums)


def pick(flag, first, second):
    return jnp.where(flag, first, second)


def reorder_by(pieces, index):
    low, high = (index & 1) == 1, (index & 2) == 2
    swapped = [pick(low, pieces[j ^ 1], pieces[j]) for j in range(4)]
    return [pick(high, swapped[j ^ 2], swapped[j]) for j in range(4)]


def local_plane(
    inputs,
    cotangent,
    seq_counts,
    seq_bucket,
    attn_norm_gain,
    q_norm_gain,
    k_norm_gain,
    w_query,
    w_key,
    w_value,
    w_headgate,
    w_out,
    ffn_norm_gain,
    w_gate,
    w_up,
    w_down,
):
    micro_batches, row_count, model_width = inputs.shape
    n_dp = lax.axis_size("dp")
    head_idx = lax.axis_index("head")
    mp_idx = lax.axis_index("mp")
    dp_idx = lax.axis_index("dp")
    core = head_idx & 1
    plane_idx = head_idx * 2 + mp_idx
    seq_len = row_count * 8
    ffn_cols = w_gate.shape[1] // 4
    slot_ids = jnp.arange(micro_batches * n_dp, dtype=jnp.int32)
    slot_count = jnp.sum(
        jnp.where(seq_bucket[None, :] == slot_ids[:, None], seq_counts[None, :], 0), axis=1
    )
    own_pos = plane_idx * row_count + jnp.arange(row_count, dtype=jnp.int32)
    apart = jnp.arange(8, dtype=jnp.int32) ^ plane_idx
    along_x, along_y, across = apart & 1, apart >> 2, (apart >> 1) & 1
    x_first = (core ^ across) == 0
    slots = across * 4 + jnp.where(x_first, along_x + 2 * along_y, along_y + 2 * along_x)
    table_cos, table_sin = rope_tables(jnp.arange(seq_len, dtype=jnp.int32), 64)
    table_cos, table_sin = table_cos[:, 0, :], table_sin[:, 0, :]
    cosine = jnp.concatenate([table_cos, table_cos], axis=1)
    sine = jnp.concatenate([-table_sin, table_sin], axis=1)
    q_gain, k_gain = q_norm_gain[None, :], k_norm_gain[None, :]

    def after(value, *ahead):
        return lax.optimization_barrier((value, ahead))[0]

    spare = jnp.zeros((row_count, 126), BF16)
    halves = [
        jnp.concatenate(
            [
                w_query[:, k * 256 : (k + 1) * 256],
                w_key[:, k * 128 : (k + 1) * 128],
                w_value[:, k * 128 : (k + 1) * 128],
                w_headgate[:, k * 2 : (k + 1) * 2],
                spare,
                w_out[k * 256 : (k + 1) * 256, :].T,
            ],
            axis=1,
        )
        for k in range(2)
    ]
    is_first = mp_idx == 0
    kept = pick(is_first, halves[0], halves[1])
    came = swap(pick(is_first, halves[1], halves[0]), BIT_X)
    attn_rows = jnp.concatenate([pick(is_first, kept, came), pick(is_first, came, kept)], axis=0)
    attn_full = lax.all_gather(attn_rows, "dp", axis=0, tiled=True)
    w_proj, w_out_t = attn_full[:, :640], attn_full[:, 640:]

    first_batch, second_batch = range(micro_batches)
    half = seq_len // 2
    live_counts = [slot_count[n * n_dp + dp_idx] for n in range(micro_batches)]
    tables = [jnp.concatenate([slots, live[None]]).astype(jnp.int32) for live in live_counts]
    x_float = [inputs[n].astype(F32) for n in range(micro_batches)]
    scale1 = [rms_scale(x) for x in x_float]
    normed1 = [x * scale for x, scale in zip(x_float, scale1)]
    xn1_own = [(n * attn_norm_gain).astype(BF16) for n in normed1]
    cot_live = [
        cotangent[n].astype(F32) * (own_pos < live_counts[n]).astype(F32)[:, None]
        for n in range(micro_batches)
    ]
    xn1 = [Gather(xn1_own[0]), None]
    pair = xn1[0].second()

    down_t = w_down.T
    quarters = jnp.stack(
        [
            jnp.concatenate(
                [w[:, k * ffn_cols : (k + 1) * ffn_cols] for w in (w_gate, w_up, down_t)], axis=1
            )
            for k in range(4)
        ]
    )
    traded = [lax.dynamic_index_in_dim(quarters, head_idx, 0, False)] + [
        swap(lax.dynamic_index_in_dim(quarters, head_idx ^ r, 0, False), r * 2) for r in (1, 2, 3)
    ]
    ffn_rows = jnp.concatenate(reorder_by(traded, head_idx), axis=0)
    ffn_rows = after(ffn_rows, attn_rows)
    w_down_t = lax.all_gather(ffn_rows[:, 2 * ffn_cols :], "dp", axis=0, tiled=True)
    w_gate_up = lax.all_gather(ffn_rows[:, : 2 * ffn_cols], "dp", axis=0, tiled=True)

    xn1[1] = Gather(after(xn1_own[1], pair))
    order = Order()
    project = lambda rows, w: dot(rows, w)
    project_t = lambda rows, w: dot(rows, w, NT).astype(BF16)
    add_t = lambda rows, w, came: (dot(rows, w, NT) + came.astype(F32)).astype(BF16)
    weight_grad = lambda rows, grads: dot(rows, grads, TN)
    add_grad = lambda rows, grads, total: dot(rows, grads, TN) + total

    def attend(n, proj):
        return attend_forward_call(tables[n], proj, cosine, sine, q_gain, k_gain)

    order.need(xn1[0].third(), xn1[1].second(), ffn_rows)
    proj, att, cot = ([None, None] for _ in range(3))
    proj_a = order.run(project, xn1[0].mine, w_proj)
    proj_b = order.run(project, xn1[0].other, w_proj)
    proj[0] = jnp.concatenate([proj_a, proj_b], axis=0)
    cot[0] = Gather(after(cot_live[0].astype(BF16), proj_a))
    att[0] = order.run(lambda p: attend(0, p), proj[0])
    order.need(xn1[1].third(), cot[0].second())
    out_sum = [None, None]
    out_sum[0] = Scatter(order.run(project_t, att[0][0][half:], w_out_t))
    proj_a = order.run(project, xn1[1].mine, w_proj)
    proj_b = order.run(project, xn1[1].other, w_proj)
    proj[1] = jnp.concatenate([proj_a, proj_b], axis=0)
    out_sum[0].second(order.run(add_t, att[0][0][:half], w_out_t, out_sum[0].came))
    order.need(cot[0].third())
    att[1] = order.run(lambda p: attend(1, p), proj[1])
    order.need(out_sum[0].third())
    out_sum[1] = Scatter(order.run(project_t, att[1][0][half:], w_out_t))
    d_hidden = [[None, None], [None, None]]
    d_hidden[0][1] = order.run(project, cot[0].other, w_down_t)

    hidden1, scale2, normed2, xn2 = ([None, None] for _ in range(4))

    def middle(n):
        hidden1[n] = x_float[n] + out_sum[n].result()
        scale2[n] = rms_scale(hidden1[n])
        normed2[n] = hidden1[n] * scale2[n]
        rows = (normed2[n] * ffn_norm_gain).astype(BF16)
        xn2[n] = Gather(rows)
        return rows

    order.need(middle(0))
    out_sum[1].second(order.run(add_t, att[1][0][:half], w_out_t, out_sum[1].came))
    order.need(xn2[0].second())
    d_hidden[0][0] = order.run(project, cot[0].mine, w_down_t)
    cot[1] = Gather(after(cot_live[1].astype(BF16), d_hidden[0][0]))
    order.need(out_sum[1].third(), xn2[0].third())

    down, back = ([None, None] for _ in range(2))
    feed_o, feed_m = ([None, None] for _ in range(2))

    def feed_other(n):
        feed_o[n] = order.run(
            feed_forward_call, xn2[n].other, d_hidden[n][1], w_gate_up, w_down_t
        )
        back[n] = Scatter(feed_o[n][3])
        down[n] = Scatter(feed_o[n][2])

    def feed_mine(n):
        feed_m[n] = order.run(
            feed_forward_call,
            xn2[n].mine,
            d_hidden[n][0],
            w_gate_up,
            w_down_t,
            down[n].came,
            back[n].came,
        )
        back[n].second(feed_m[n][3])

    feed_other(0)
    order.need(middle(1), cot[1].second())
    feed_mine(0)
    order.need(xn2[1].second(), cot[1].third())
    d_hidden[1][1] = order.run(project, cot[1].other, w_down_t)
    d_hidden[1][0] = order.run(project, cot[1].mine, w_down_t)
    order.need(back[0].third(), xn2[1].third())

    d_hidden1, d_attn = ([None, None] for _ in range(2))
    gain_ffn = []

    def turn(n):
        d_xn2 = back[n].result()
        gain_ffn.append(jnp.sum(d_xn2 * normed2[n], axis=0))
        d_hidden1[n] = cot_live[n] + norm_back(d_xn2, normed2[n], scale2[n], ffn_norm_gain)
        rows = d_hidden1[n].astype(BF16)
        d_attn[n] = Gather(rows)
        return rows

    grad_gate_up = order.run(weight_grad, xn2[0].other, feed_o[0][1])
    order.need(turn(0))
    feed_other(1)
    order.need(d_attn[0].second())
    feed_mine(1)
    order.need(d_attn[0].third())
    grad_gate_up = order.run(add_grad, xn2[0].mine, feed_m[0][1], grad_gate_up)
    grad_gate_up = order.run(add_grad, xn2[1].other, feed_o[1][1], grad_gate_up)
    order.need(back[1].third())
    grad_gate_up = order.run(add_grad, xn2[1].mine, feed_m[1][1], grad_gate_up)
    order.need(turn(1))
    grad_down_t = order.run(weight_grad, cot[0].other, feed_o[0][0])
    down[0].second(after(feed_m[0][2], grad_down_t))
    grad_down_t = order.run(add_grad, cot[0].mine, feed_m[0][0], grad_down_t)
    order.need(d_attn[1].second())
    grad_down_t = order.run(add_grad, cot[1].other, feed_o[1][0], grad_down_t)
    grad_down_t = order.run(add_grad, cot[1].mine, feed_m[1][0], grad_down_t)
    order.need(down[0].third())

    d_proj, gain_parts, rows_sum = ([None, None] for _ in range(3))
    outputs, input_grads = ([None, None] for _ in range(2))

    def back_attend(n):
        d_a = order.run(project, d_attn[n].mine, w_out_t)
        d_b = order.run(project, d_attn[n].other, w_out_t)
        d_gated = jnp.concatenate([d_a, d_b], axis=0)
        d_proj[n], part_q, part_k = order.run(
            lambda *v: attend_backward_call(tables[n], *v, cosine, sine, q_gain, k_gain),
            proj[n],
            d_gated,
            att[n][1],
            att[n][2],
        )
        gain_parts[n] = (part_q[0], part_k[0])

    def finish(n):
        d_xn1 = rows_sum[n].result()
        input_grads[n] = (
            d_hidden1[n] + norm_back(d_xn1, normed1[n], scale1[n], attn_norm_gain)
        ).astype(BF16)

    back_attend(0)
    order.need(d_attn[1].third())
    rows_sum[0] = Scatter(order.run(project_t, d_proj[0][half:], w_proj))
    outputs[0] = (hidden1[0] + down[0].result()).astype(BF16)
    grad_out_t = order.run(weight_grad, d_attn[0].mine, att[0][0][:half])
    grad_out_t = order.run(add_grad, d_attn[0].other, att[0][0][half:], grad_out_t)
    rows_sum[0].second(order.run(add_t, d_proj[0][:half], w_proj, rows_sum[0].came))
    down[1].second(after(feed_m[1][2], outputs[0]))
    back_attend(1)
    order.need(rows_sum[0].third(), down[1].third())
    rows_sum[1] = Scatter(order.run(project_t, d_proj[1][half:], w_proj))
    grad_proj = order.run(weight_grad, xn1[0].mine, d_proj[0][:half])
    rows_sum[1].second(order.run(add_t, d_proj[1][:half], w_proj, rows_sum[1].came))
    grad_proj = order.run(add_grad, xn1[0].other, d_proj[0][half:], grad_proj)
    grad_proj = order.run(add_grad, xn1[1].mine, d_proj[1][:half], grad_proj)
    grad_proj = order.run(add_grad, xn1[1].other, d_proj[1][half:], grad_proj)
    order.need(rows_sum[1].third())
    grad_out_t = order.run(add_grad, d_attn[1].mine, att[1][0][:half], grad_out_t)
    grad_out_t = order.run(add_grad, d_attn[1].other, att[1][0][half:], grad_out_t)
    finish(0)
    finish(1)
    outputs[1] = (hidden1[1] + down[1].result()).astype(BF16)

    gain_attn = jnp.sum(grad_proj * w_proj.astype(F32), axis=1) / attn_norm_gain
    gains = jnp.concatenate(
        [gain_attn, gain_ffn[0] + gain_ffn[1]]
        + [gain_parts[0][k] + gain_parts[1][k] for k in range(2)]
    ).reshape(-1, 128)
    for bits in (BIT_C, BIT_X, BIT_Y):
        gains = gains + swap(gains, bits)
    for step in (1, 2):
        gains = gains + lax.ppermute(gains, "dp", [(i, i ^ step) for i in range(4)])
    gains = gains.reshape(-1)
    sum_attn, sum_gain_ffn = gains[:model_width], gains[model_width : 2 * model_width]
    sum_query, sum_key = gains[-256:-128], gains[-128:]

    sum_ffn = [
        lax.psum_scatter(g.astype(BF16), "dp", scatter_dimension=0, tiled=True)
        for g in (grad_gate_up, grad_down_t)
    ]
    ffn_sum = jnp.concatenate(sum_ffn, axis=1).reshape(4, -1, 3 * ffn_cols)
    back = [lax.dynamic_index_in_dim(ffn_sum, head_idx, 0, False)] + [
        swap(lax.dynamic_index_in_dim(ffn_sum, head_idx ^ r, 0, False), r * 2) for r in (1, 2, 3)
    ]
    back = reorder_by(back, head_idx)
    grad_gate, grad_up, grad_down = [
        jnp.concatenate([b[:, k * ffn_cols : (k + 1) * ffn_cols] for b in back], axis=1).astype(F32)
        for k in range(3)
    ]
    grad_down = grad_down.T
    attn_grads = jnp.concatenate([grad_proj, grad_out_t], axis=1).astype(BF16)
    attn_sum = lax.psum_scatter(attn_grads, "dp", scatter_dimension=0, tiled=True)
    upper, lower = attn_sum[:row_count], attn_sum[row_count:]
    kept = pick(is_first, upper, lower)
    came = swap(pick(is_first, lower, upper), BIT_X)
    by_half = [v.astype(F32) for v in (pick(is_first, kept, came), pick(is_first, came, kept))]
    grad_query = jnp.concatenate([v[:, 0:256] for v in by_half], axis=1)
    grad_key = jnp.concatenate([v[:, 256:384] for v in by_half], axis=1)
    grad_value = jnp.concatenate([v[:, 384:512] for v in by_half], axis=1)
    grad_headgate = jnp.concatenate([v[:, 512:514] for v in by_half], axis=1)
    grad_out = jnp.concatenate([v[:, 640:896].T for v in by_half], axis=0)
    return (
        jnp.stack(outputs),
        jnp.stack(input_grads),
        sum_attn,
        sum_query,
        sum_key,
        grad_query,
        grad_key,
        grad_value,
        grad_headgate,
        grad_out,
        sum_gain_ffn,
        grad_gate,
        grad_up,
        grad_down,
    )


def choose_local(mesh):
    if mesh.shape["head"] == 4 and mesh.shape["mp"] == 2 and mesh.shape["dp"] == 4:
        return local_plane
    return local


def solution(mesh):
    placed = (
        P(None, ("dp", "head", "mp"), None),
        P(None, ("dp", "head", "mp"), None),
        P(),
        P(),
        P(),
        P(),
        P(),
        P(("dp", "mp"), "head"),
        P(("dp", "mp"), "head"),
        P(("dp", "mp"), "head"),
        P(("dp", "mp"), "head"),
        P("head", ("dp", "mp")),
        P(),
        P(("dp", "head"), "mp"),
        P(("dp", "head"), "mp"),
        P("mp", ("dp", "head")),
    )
    return jax.shard_map(
        choose_local(mesh),
        mesh=mesh,
        in_specs=placed,
        out_specs=(
            P(None, ("dp", "head", "mp"), None),
            P(None, ("dp", "head", "mp"), None),
            P(),
            P(),
            P(),
            P(("dp", "mp"), "head"),
            P(("dp", "mp"), "head"),
            P(("dp", "mp"), "head"),
            P(("dp", "mp"), "head"),
            P("head", ("dp", "mp")),
            P(),
            P(("dp", "head"), "mp"),
            P(("dp", "head"), "mp"),
            P("mp", ("dp", "head")),
        ),
        check_vma=False,
    )
```

```python
import functools

import jax
import jax.numpy as jnp
from jax import lax
from jax.experimental import pallas as pl
from jax.experimental.pallas import tpu as pltpu
from jax.sharding import PartitionSpec as P

EPS = 1e-06
ROPE_BASE = 1000000.0
NEG_FILL = -1e30


def rms_scale(values):
    return lax.rsqrt(jnp.mean(values * values, axis=-1, keepdims=True) + EPS)


def norm_back(grad_out, normed, scale_rows, gain):
    d_normed = grad_out * gain
    return scale_rows * (d_normed - normed * jnp.mean(d_normed * normed, axis=-1, keepdims=True))


def rope_tables(positions, half):
    freq = jnp.power(ROPE_BASE, -jnp.arange(half, dtype=jnp.float32) / half)
    angle = positions.astype(jnp.float32)[:, None] * freq[None, :]
    return (jnp.cos(angle)[:, None, :], jnp.sin(angle)[:, None, :])


def rotate(values, cosine, sine):
    half = values.shape[-1] // 2
    first = values[..., :half]
    second = values[..., half:]
    return jnp.concatenate(
        [first * cosine - second * sine, second * cosine + first * sine], axis=-1
    )


def rotate_back(grads, cosine, sine):
    half = grads.shape[-1] // 2
    first = grads[..., :half]
    second = grads[..., half:]
    return jnp.concatenate(
        [first * cosine + second * sine, second * cosine - first * sine], axis=-1
    )


def masked_scores(q_group, key_piece, query_pos, key_pos, live_count):
    scores = jnp.einsum("qhgd,khd->hgqk", q_group, key_piece, preferred_element_type=jnp.float32)
    allowed = (key_pos[None, :] <= query_pos[:, None]) & (key_pos[None, :] < live_count)
    return (scores, allowed)


def split_keys(keys, values, key_pos, key_block):
    n_blocks = keys.shape[0] // key_block
    key_pieces = keys.reshape(n_blocks, key_block, keys.shape[1], keys.shape[2])
    value_pieces = values.reshape(n_blocks, key_block, values.shape[1], values.shape[2])
    return (key_pieces, value_pieces, key_pos.reshape(n_blocks, key_block))


def attend_forward(q_group, keys, values, query_pos, key_pos, live_count, key_block):
    n_query, kv_here, group_size, head_dim = q_group.shape
    key_pieces, value_pieces, pos_pieces = split_keys(keys, values, key_pos, key_block)

    def stats(carry, piece):
        row_max, row_total = carry
        key_piece, piece_pos = piece
        scores, allowed = masked_scores(q_group, key_piece, query_pos, piece_pos, live_count)
        scores = jnp.where(allowed, scores, NEG_FILL)
        new_max = jnp.maximum(row_max, jnp.max(scores, axis=-1))
        kept_exp = jnp.where(allowed, jnp.exp(scores - new_max[..., None]), 0.0)
        row_total = row_total * jnp.exp(row_max - new_max) + jnp.sum(kept_exp, axis=-1)
        return ((new_max, row_total), None)

    start = (
        jnp.full((kv_here, group_size, n_query), NEG_FILL, jnp.float32),
        jnp.zeros((kv_here, group_size, n_query), jnp.float32),
    )
    (row_max, row_total), unused = lax.scan(stats, start, (key_pieces, pos_pieces))
    log_total = row_max + jnp.log(row_total)

    def weigh(acc, piece):
        key_piece, value_piece, piece_pos = piece
        scores, allowed = masked_scores(q_group, key_piece, query_pos, piece_pos, live_count)
        prob_low = jnp.where(allowed, jnp.exp(scores - log_total[..., None]), 0.0).astype(
            jnp.bfloat16
        )
        acc = acc + jnp.einsum(
            "hgqk,khd->qhgd", prob_low, value_piece, preferred_element_type=jnp.float32
        )
        return (acc, None)

    attn_o, unused = lax.scan(
        weigh, jnp.zeros(q_group.shape, jnp.float32), (key_pieces, value_pieces, pos_pieces)
    )
    return (attn_o, log_total)


def attend_backward(
    q_group, keys, values, query_pos, key_pos, live_count, key_block, log_total, d_out, delta
):
    kv_here = keys.shape[1]
    head_dim = keys.shape[2]
    key_pieces, value_pieces, pos_pieces = split_keys(keys, values, key_pos, key_block)

    def backstep(d_query, piece):
        key_piece, value_piece, piece_pos = piece
        scores, allowed = masked_scores(q_group, key_piece, query_pos, piece_pos, live_count)
        probs = jnp.where(allowed, jnp.exp(scores - log_total[..., None]), 0.0)
        d_probs = jnp.einsum(
            "qhgd,khd->hgqk", d_out, value_piece, preferred_element_type=jnp.float32
        )
        d_scores = (probs * (d_probs - delta[..., None])).astype(jnp.bfloat16)
        d_query = d_query + jnp.einsum(
            "hgqk,khd->qhgd", d_scores, key_piece, preferred_element_type=jnp.float32
        )
        d_key = jnp.einsum("hgqk,qhgd->khd", d_scores, q_group, preferred_element_type=jnp.float32)
        d_value = jnp.einsum(
            "hgqk,qhgd->khd", probs.astype(jnp.bfloat16), d_out, preferred_element_type=jnp.float32
        )
        return (d_query, (d_key, d_value))

    d_query, (d_key, d_value) = lax.scan(
        backstep, jnp.zeros(q_group.shape, jnp.float32), (key_pieces, value_pieces, pos_pieces)
    )
    return (d_query, d_key.reshape(-1, kv_here * head_dim), d_value.reshape(-1, kv_here * head_dim))


def gather_weights(w_query, w_key, w_value, w_headgate, w_out, w_gate, w_up, w_down):
    attn_parts = (
        lax.all_gather(w_query, ("dp", "mp"), axis=0, tiled=True),
        lax.all_gather(w_key, ("dp", "mp"), axis=0, tiled=True),
        lax.all_gather(w_value, ("dp", "mp"), axis=0, tiled=True),
        lax.all_gather(w_headgate, ("dp", "mp"), axis=0, tiled=True),
        lax.all_gather(w_out, ("dp", "mp"), axis=1, tiled=True),
    )
    ffn_parts = (
        lax.all_gather(w_gate, ("dp", "head"), axis=0, tiled=True),
        lax.all_gather(w_up, ("dp", "head"), axis=0, tiled=True),
        lax.all_gather(w_down, ("dp", "head"), axis=1, tiled=True),
    )
    return tuple(attn_parts) + tuple(ffn_parts)


def reduce_grads(g_query, g_key, g_value, g_headgate, g_out, g_gate, g_up, g_down):
    attn_parts = (
        lax.psum_scatter(
            g_query.astype(jnp.bfloat16), ("dp", "mp"), scatter_dimension=0, tiled=True
        ).astype(jnp.float32),
        lax.psum_scatter(
            g_key.astype(jnp.bfloat16), ("dp", "mp"), scatter_dimension=0, tiled=True
        ).astype(jnp.float32),
        lax.psum_scatter(
            g_value.astype(jnp.bfloat16), ("dp", "mp"), scatter_dimension=0, tiled=True
        ).astype(jnp.float32),
        lax.psum_scatter(
            g_headgate.astype(jnp.bfloat16), ("dp", "mp"), scatter_dimension=0, tiled=True
        ).astype(jnp.float32),
        lax.psum_scatter(
            g_out.astype(jnp.bfloat16), ("dp", "mp"), scatter_dimension=1, tiled=True
        ).astype(jnp.float32),
    )
    ffn_parts = (
        lax.psum_scatter(
            g_gate.astype(jnp.bfloat16), ("dp", "head"), scatter_dimension=0, tiled=True
        ).astype(jnp.float32),
        lax.psum_scatter(
            g_up.astype(jnp.bfloat16), ("dp", "head"), scatter_dimension=0, tiled=True
        ).astype(jnp.float32),
        lax.psum_scatter(
            g_down.astype(jnp.bfloat16), ("dp", "head"), scatter_dimension=1, tiled=True
        ).astype(jnp.float32),
    )
    return tuple(attn_parts) + tuple(ffn_parts)


def local(
    inputs,
    cotangent,
    seq_counts,
    seq_bucket,
    attn_norm_gain,
    q_norm_gain,
    k_norm_gain,
    w_query,
    w_key,
    w_value,
    w_headgate,
    w_out,
    ffn_norm_gain,
    w_gate,
    w_up,
    w_down,
):
    micro_batches, row_count, model_width = inputs.shape
    n_head = lax.axis_size("head")
    n_mp = lax.axis_size("mp")
    n_dp = lax.axis_size("dp")
    head_idx = lax.axis_index("head")
    mp_idx = lax.axis_index("mp")
    dp_idx = lax.axis_index("dp")
    head_dim = q_norm_gain.shape[0]
    q_heads = w_query.shape[1] // head_dim
    kv_heads = w_key.shape[1] // head_dim
    group_size = q_heads // kv_heads
    q_scale = head_dim ** (-0.5)
    seq_len = row_count * n_head * n_mp
    key_block = min(512, seq_len)
    n_query = n_head * row_count
    slot_ids = jnp.arange(micro_batches * n_dp, dtype=jnp.int32)
    slot_count = jnp.sum(
        jnp.where(seq_bucket[None, :] == slot_ids[:, None], seq_counts[None, :], 0), axis=1
    )
    local_idx = jnp.arange(row_count, dtype=jnp.int32)
    own_pos = head_idx * n_mp * row_count + mp_idx * row_count + local_idx
    query_idx = jnp.arange(n_query, dtype=jnp.int32)
    query_pos = (
        query_idx // row_count * n_mp * row_count + mp_idx * row_count + query_idx % row_count
    )
    key_idx = jnp.arange(seq_len, dtype=jnp.int32)
    key_pos = (
        key_idx % n_query // row_count * n_mp * row_count
        + key_idx // n_query * row_count
        + key_idx % row_count
    )
    rope_cos, rope_sin = rope_tables(query_pos, head_dim // 2)
    grad_total = None
    gain_attn = jnp.zeros((model_width,), jnp.float32)
    gain_query = jnp.zeros((head_dim,), jnp.float32)
    gain_key = jnp.zeros((head_dim,), jnp.float32)
    gain_ffn = jnp.zeros((model_width,), jnp.float32)
    outputs = []
    input_grads = []
    for micro_batch in range(micro_batches):
        weights = gather_weights(w_query, w_key, w_value, w_headgate, w_out, w_gate, w_up, w_down)
        wq_full, wk_full, wv_full, wg_full, wo_full, wgate_full, wup_full, wdown_full = weights
        live_count = slot_count[micro_batch * n_dp + dp_idx]
        x_float = inputs[micro_batch].astype(jnp.float32)
        scale1 = rms_scale(x_float)
        normed1 = x_float * scale1
        xn1 = (normed1 * attn_norm_gain).astype(jnp.bfloat16)
        gathered_rows = lax.all_gather(xn1, "head", axis=0, tiled=True)
        q_raw = jnp.dot(gathered_rows, wq_full, preferred_element_type=jnp.float32).reshape(
            n_query, q_heads, head_dim
        )
        k_raw = jnp.dot(gathered_rows, wk_full, preferred_element_type=jnp.float32).reshape(
            n_query, kv_heads, head_dim
        )
        value_low = jnp.dot(gathered_rows, wv_full, preferred_element_type=jnp.float32).astype(
            jnp.bfloat16
        )
        gate_logit = jnp.dot(gathered_rows, wg_full, preferred_element_type=jnp.float32)
        q_rms = rms_scale(q_raw)
        q_hat = q_raw * q_rms
        query_low = (rotate(q_hat * q_norm_gain, rope_cos, rope_sin) * q_scale).astype(jnp.bfloat16)
        k_rms = rms_scale(k_raw)
        k_hat = k_raw * k_rms
        key_low = rotate(k_hat * k_norm_gain, rope_cos, rope_sin).astype(jnp.bfloat16)
        all_keys, all_values = (
            lax.all_gather(key_low.reshape(n_query, kv_heads * head_dim), "mp", axis=0, tiled=True),
            lax.all_gather(value_low, "mp", axis=0, tiled=True),
        )
        all_keys = all_keys.reshape(seq_len, kv_heads, head_dim)
        all_values = all_values.reshape(seq_len, kv_heads, head_dim)
        q_group = query_low.reshape(n_query, kv_heads, group_size, head_dim)
        attn_o, log_total = attend_forward(
            q_group, all_keys, all_values, query_pos, key_pos, live_count, key_block
        )
        gate_prob = jax.nn.sigmoid(gate_logit)
        attn_heads = attn_o.reshape(n_query, q_heads, head_dim)
        gated = (
            (attn_heads * gate_prob[..., None])
            .reshape(n_query, q_heads * head_dim)
            .astype(jnp.bfloat16)
        )
        attn_sum = lax.psum_scatter(
            jnp.dot(gated, wo_full, preferred_element_type=jnp.float32).astype(jnp.bfloat16),
            "head",
            scatter_dimension=0,
            tiled=True,
        ).astype(jnp.float32)
        hidden1 = x_float + attn_sum
        scale2 = rms_scale(hidden1)
        normed2 = hidden1 * scale2
        xn2 = (normed2 * ffn_norm_gain).astype(jnp.bfloat16)
        live = (own_pos < live_count).astype(jnp.float32)[:, None]
        cot_live = cotangent[micro_batch].astype(jnp.float32) * live
        ffn_in, cot_rows = (
            lax.all_gather(xn2, "mp", axis=0, tiled=True),
            lax.all_gather(cot_live.astype(jnp.bfloat16), "mp", axis=0, tiled=True),
        )
        gate_pre = jnp.dot(ffn_in, wgate_full, preferred_element_type=jnp.float32)
        up_pre = jnp.dot(ffn_in, wup_full, preferred_element_type=jnp.float32)
        gate_sig = jax.nn.sigmoid(gate_pre)
        gate_act = gate_pre * gate_sig
        hidden = (gate_act * up_pre).astype(jnp.bfloat16)
        ffn_sum = lax.psum_scatter(
            jnp.dot(hidden, wdown_full, preferred_element_type=jnp.float32).astype(jnp.bfloat16),
            "mp",
            scatter_dimension=0,
            tiled=True,
        ).astype(jnp.float32)
        outputs.append((hidden1 + ffn_sum).astype(jnp.bfloat16))
        d_hidden = jnp.einsum("rd,fd->rf", cot_rows, wdown_full, preferred_element_type=jnp.float32)
        grad_down = jnp.einsum("rf,rd->fd", hidden, cot_rows, preferred_element_type=jnp.float32)
        d_up = (d_hidden * gate_act).astype(jnp.bfloat16)
        d_gate = (d_hidden * up_pre * gate_sig * (1.0 + gate_pre * (1.0 - gate_sig))).astype(
            jnp.bfloat16
        )
        grad_gate = jnp.einsum("rd,rf->df", ffn_in, d_gate, preferred_element_type=jnp.float32)
        grad_up = jnp.einsum("rd,rf->df", ffn_in, d_up, preferred_element_type=jnp.float32)
        ffn_term = jnp.einsum(
            "rf,df->rd", d_gate, wgate_full, preferred_element_type=jnp.float32
        ) + jnp.einsum("rf,df->rd", d_up, wup_full, preferred_element_type=jnp.float32)
        d_xn2 = lax.psum_scatter(
            ffn_term.astype(jnp.bfloat16), "mp", scatter_dimension=0, tiled=True
        ).astype(jnp.float32)
        gain_ffn = gain_ffn + jnp.sum(d_xn2 * normed2, axis=0)
        d_hidden1 = cot_live + norm_back(d_xn2, normed2, scale2, ffn_norm_gain)
        d_attn = lax.all_gather(d_hidden1.astype(jnp.bfloat16), "head", axis=0, tiled=True)
        d_gated = jnp.einsum(
            "rd,cd->rc", d_attn, wo_full, preferred_element_type=jnp.float32
        ).reshape(n_query, q_heads, head_dim)
        grad_out = jnp.einsum("rc,rd->cd", gated, d_attn, preferred_element_type=jnp.float32)
        d_out_low = (d_gated * gate_prob[..., None]).astype(jnp.bfloat16)
        d_gate_logit = (
            jnp.sum(d_gated * attn_heads, axis=-1) * gate_prob * (1.0 - gate_prob)
        ).astype(jnp.bfloat16)
        grad_headgate = jnp.einsum(
            "rd,rc->dc", gathered_rows, d_gate_logit, preferred_element_type=jnp.float32
        )
        d_out_group = d_out_low.reshape(n_query, kv_heads, group_size, head_dim)
        delta = jnp.transpose(jnp.sum(d_out_group.astype(jnp.float32) * attn_o, axis=-1), (1, 2, 0))
        d_query, d_key_all, d_value_all = attend_backward(
            q_group,
            all_keys,
            all_values,
            query_pos,
            key_pos,
            live_count,
            key_block,
            log_total,
            d_out_group,
            delta,
        )
        d_key_own, d_value_own = (
            lax.psum_scatter(
                d_key_all.astype(jnp.bfloat16), "mp", scatter_dimension=0, tiled=True
            ).astype(jnp.float32),
            lax.psum_scatter(
                d_value_all.astype(jnp.bfloat16), "mp", scatter_dimension=0, tiled=True
            ).astype(jnp.float32),
        )
        dq_norm = rotate_back(
            (d_query * q_scale).reshape(n_query, q_heads, head_dim), rope_cos, rope_sin
        )
        gain_query = gain_query + jnp.sum(dq_norm * q_hat, axis=(0, 1))
        d_q_raw = (
            norm_back(dq_norm, q_hat, q_rms, q_norm_gain)
            .reshape(n_query, q_heads * head_dim)
            .astype(jnp.bfloat16)
        )
        dk_norm = rotate_back(d_key_own.reshape(n_query, kv_heads, head_dim), rope_cos, rope_sin)
        gain_key = gain_key + jnp.sum(dk_norm * k_hat, axis=(0, 1))
        d_k_raw = (
            norm_back(dk_norm, k_hat, k_rms, k_norm_gain)
            .reshape(n_query, kv_heads * head_dim)
            .astype(jnp.bfloat16)
        )
        d_value_low = d_value_own.astype(jnp.bfloat16)
        grad_query = jnp.einsum(
            "rd,rc->dc", gathered_rows, d_q_raw, preferred_element_type=jnp.float32
        )
        grad_key = jnp.einsum(
            "rd,rc->dc", gathered_rows, d_k_raw, preferred_element_type=jnp.float32
        )
        grad_value = jnp.einsum(
            "rd,rc->dc", gathered_rows, d_value_low, preferred_element_type=jnp.float32
        )
        attn_term = jnp.einsum("rc,dc->rd", d_q_raw, wq_full, preferred_element_type=jnp.float32)
        attn_term = attn_term + jnp.einsum(
            "rc,dc->rd", d_k_raw, wk_full, preferred_element_type=jnp.float32
        )
        attn_term = attn_term + jnp.einsum(
            "rc,dc->rd", d_value_low, wv_full, preferred_element_type=jnp.float32
        )
        attn_term = attn_term + jnp.einsum(
            "rc,dc->rd", d_gate_logit, wg_full, preferred_element_type=jnp.float32
        )
        d_xn1 = lax.psum_scatter(
            attn_term.astype(jnp.bfloat16), "head", scatter_dimension=0, tiled=True
        ).astype(jnp.float32)
        gain_attn = gain_attn + jnp.sum(d_xn1 * normed1, axis=0)
        input_grads.append(
            (d_hidden1 + norm_back(d_xn1, normed1, scale1, attn_norm_gain)).astype(jnp.bfloat16)
        )
        batch_grads = reduce_grads(
            grad_query, grad_key, grad_value, grad_headgate, grad_out, grad_gate, grad_up, grad_down
        )
        if grad_total is None:
            grad_total = batch_grads
        else:
            grad_total = tuple((a + b for a, b in zip(grad_total, batch_grads)))
    sum_attn, sum_query, sum_key, sum_ffn = lax.psum(
        (gain_attn, gain_query, gain_key, gain_ffn), ("dp", "head", "mp")
    )
    return (
        jnp.stack(outputs),
        jnp.stack(input_grads),
        sum_attn,
        sum_query,
        sum_key,
        grad_total[0],
        grad_total[1],
        grad_total[2],
        grad_total[3],
        grad_total[4],
        sum_ffn,
        grad_total[5],
        grad_total[6],
        grad_total[7],
    )


PLANE = ("head", "mp")
BIT_X, BIT_C, BIT_Y = 1, 2, 4
NT = (((1,), (1,)), ((), ()))
NN = (((1,), (0,)), ((), ()))
TN = (((0,), (0,)), ((), ()))
F32 = jnp.float32
BF16 = jnp.bfloat16
COST_SHARE = 0.4
LATE_SHARE = 0.4


def dot(left, right, dims=NN):
    return lax.dot_general(left, right, dims, preferred_element_type=F32)


def swap(values, bits):
    return lax.ppermute(values, PLANE, [(i, i ^ bits) for i in range(8)])


def swap_mixed(values, core0, core1):
    return lax.ppermute(
        values, PLANE, [(i, i ^ (core1 if i & BIT_C else core0)) for i in range(8)]
    )


class Order:
    def __init__(self):
        self.ahead = []
        self.last = None

    def need(self, *values):
        self.ahead.extend(values)

    def pin(self, value):
        if self.last is None:
            return value
        return lax.optimization_barrier((value, self.last))[0]

    def run(self, op, *operands):
        if self.ahead:
            operands = lax.optimization_barrier((tuple(operands), tuple(self.ahead)))[0]
        out = op(*operands)
        self.last = out[0] if isinstance(out, (tuple, list)) else out
        self.ahead = [self.last]
        return out


class Gather:
    def __init__(self, order, rows):
        self.order = order
        self.rows = rows
        self.came = swap_mixed(rows, BIT_X, BIT_Y)

    def second(self):
        came = self.order.pin(self.came)
        near = jnp.concatenate([self.rows, came], axis=0)
        self.came = swap_mixed(near, BIT_Y, BIT_X)
        self.pieces = [near, None, swap(near, BIT_C), None]
        return near

    def third(self):
        far = self.order.pin(self.came)
        self.pieces[1], self.pieces[3] = far, swap(far, BIT_C)
        return far


class Scatter:
    def __init__(self, order, near, far):
        self.order = order
        self.came = (swap(near, BIT_C), swap(far, BIT_C))

    def add(self, near, far):
        near_came, far_came = self.order.pin(self.came)
        far = (far.astype(F32) + far_came.astype(F32)).astype(BF16)
        near = (near.astype(F32) + near_came.astype(F32)).astype(BF16)
        return self.second(near, far)

    def second(self, near, far):
        self.kept = near
        self.came = swap_mixed(far, BIT_Y, BIT_X)
        return (near, far)

    def third(self):
        came = self.order.pin(self.came)
        half = came.shape[0] // 2
        sent = (self.kept[half:].astype(F32) + came[half:].astype(F32)).astype(BF16)
        self.kept = self.kept[:half].astype(F32) + came[:half].astype(F32)
        self.came = swap_mixed(sent, BIT_X, BIT_Y)
        return sent

    def result(self):
        return self.kept + self.order.pin(self.came).astype(F32)


def norm_rope(raw, gain, cosine, sine):
    scale_rows = lax.rsqrt(jnp.mean(raw * raw, axis=-1, keepdims=True) + EPS)
    hat = raw * scale_rows
    turned = hat * gain
    return (turned * cosine + pltpu.roll(turned, 64, 1) * sine, hat, scale_rows)


def norm_rope_back(grad, hat, scale_rows, gain, cosine, sine):
    grad_n = grad * cosine - pltpu.roll(grad, 64, 1) * sine
    gain_part = jnp.sum(grad_n * hat, axis=0, keepdims=True)
    scaled = grad_n * gain
    raw = scale_rows * (scaled - hat * jnp.mean(scaled * hat, axis=-1, keepdims=True))
    return (raw, gain_part)


def two_lanes(first, second, shape):
    lane = lax.broadcasted_iota(jnp.int32, shape, 1)
    return jnp.where(lane == 0, first, jnp.where(lane == 1, second, 0.0))


def cost(flops, traffic, transcendentals=0, share=COST_SHARE):
    return pl.CostEstimate(
        flops=int(flops / share),
        bytes_accessed=int(traffic / share),
        transcendentals=int(transcendentals / share),
    )


SLOT, LIVE, BLOCK, PLACE = 0, 8, 9, 41


def attend_table(plane_idx, core, live_count):
    slot = jnp.arange(8, dtype=jnp.int32)
    across, low, high = slot >> 2, slot & 1, (slot >> 1) & 1
    x_first = (core ^ across) == 0
    apart = across * 2 + jnp.where(x_first, low + 4 * high, high + 4 * low)
    place = apart ^ plane_idx
    slots = jnp.sum(jnp.where(place[None, :] == slot[:, None], slot[None, :], 0), axis=1)
    steps = jnp.arange(8, dtype=jnp.int32)
    blocks = []
    for piece in range(4):
        one, two = place[2 * piece], place[2 * piece + 1]
        first = jnp.where(one < two, 0, 1)
        blocks.append(jnp.where(steps >= jnp.maximum(one, two), 1 - first, first))
    return jnp.concatenate([slots, live_count[None]] + blocks + [place]).astype(jnp.int32)


def take_piece(slot, pieces):
    near = jnp.where(slot < 2, pieces[0][...], pieces[1][...])
    far = jnp.where(slot < 6, pieces[2][...], pieces[3][...])
    return jnp.where(slot < 4, near, far)


def attend_forward_kernel(table, *refs):
    x_pieces, (weights, cosine, sine, q_gain, k_gain) = refs[:4], refs[4:9]
    proj, attn_o, lse, gated = refs[9:13]
    out_pieces, (keys, values, acc) = refs[13:17], refs[17:]
    step = pl.program_id(0)
    rows = proj.shape[0]
    live, slot = table[LIVE], table[SLOT + step]
    cos_b, sin_b = cosine[...], sine[...]
    here = pl.multiple_of(step * rows, rows)
    proj[...] = dot(take_piece(slot, x_pieces), weights[:, 0:640])
    key, _, _ = norm_rope(proj[:, 256:384], k_gain[...], cos_b, sin_b)
    keys[pl.ds(here, rows), :] = key.astype(BF16)
    values[pl.ds(here, rows), 0:128] = proj[:, 384:512].astype(BF16)
    values[pl.ds(here, rows), 128:256] = jnp.ones((rows, 128), BF16)
    q_scale = 128**-0.5
    first, _, _ = norm_rope(proj[:, 0:128], q_gain[...], cos_b, sin_b)
    second, _, _ = norm_rope(proj[:, 128:256], q_gain[...], cos_b, sin_b)
    query = (jnp.concatenate([first, second], axis=0) * q_scale).astype(BF16)

    def add_block(index, mask_of):
        there = pl.multiple_of(index * rows, rows)
        weight = jnp.exp(dot(query, keys[pl.ds(there, rows), :], NT))
        if mask_of is not None:
            weight = jnp.where(mask_of(there), weight, 0.0)
        acc[...] += dot(weight.astype(BF16), values[pl.ds(there, rows), :])

    def column():
        return lax.broadcasted_iota(jnp.int32, (2 * rows, rows), 1)

    def causal(there):
        row = lax.broadcasted_iota(jnp.int32, (2 * rows, rows), 0)
        return (column() <= jnp.where(row >= rows, row - rows, row)) & (column() + there < live)

    acc[...] = jnp.zeros_like(acc)
    whole = jnp.minimum(step, live // rows)

    def block(index, carry):
        add_block(index, None)
        return carry

    lax.fori_loop(0, whole, block, 0)

    @pl.when((whole < step) & (whole * rows < live))
    def _():
        add_block(whole, lambda there: column() + there < live)

    @pl.when(here < live)
    def _():
        add_block(step, causal)

    total = acc[:, 128:129]
    out = acc[:, 0:128] / total
    log_total = jnp.log(total)
    gate0 = jax.nn.sigmoid(proj[:, 512:513])
    gate1 = jax.nn.sigmoid(proj[:, 513:514])
    attn_o[:, 0:128] = out[:rows]
    attn_o[:, 128:256] = out[rows:]
    gated[:, 0:128] = (out[:rows] * gate0).astype(BF16)
    gated[:, 128:256] = (out[rows:] * gate1).astype(BF16)
    lse[...] = two_lanes(log_total[:rows], log_total[rows:], (rows, 128))
    part = dot(gated[...], weights[:, 640:896], NT).astype(BF16)
    for piece in range(4):

        @pl.when(slot // 2 == piece)
        def _():
            out_pieces[piece][...] = part


def attend_backward_kernel(table, *refs):
    d_pieces = refs[:4]
    weights, proj, attn_o, lse, cosine, sine, q_gain, k_gain = refs[4:12]
    d_proj, gain_q, gain_k = refs[12:15]
    back_pieces = refs[15:19]
    keys, keys_t, values, k_raw, d_keys, d_values, d_query, d_held = refs[19:]
    step = pl.program_id(0)
    rows = proj.shape[0]
    live = table[LIVE]
    q_scale = 128**-0.5

    @pl.when(step == 0)
    def _():
        gain_q[...] = jnp.zeros_like(gain_q)
        gain_k[...] = jnp.zeros_like(gain_k)

    @pl.when(step < 8)
    def _():
        here = pl.multiple_of(step * rows, rows)
        slot = table[SLOT + step]
        cos_b, sin_b = cosine[pl.ds(here, rows), :], sine[pl.ds(here, rows), :]
        raw_key = proj[:, 256:384]
        k_raw[pl.ds(here, rows), :] = raw_key
        key, _, _ = norm_rope(raw_key, k_gain[...], cos_b, sin_b)
        key = key.astype(BF16)
        keys[pl.ds(here, rows), :] = key
        keys_t[step] = key.T
        values[pl.ds(here, rows), :] = proj[:, 384:512].astype(BF16)
        d_keys[pl.ds(here, rows), :] = jnp.zeros((rows, 128), F32)
        d_values[pl.ds(here, rows), :] = jnp.zeros((rows, 128), F32)
        d_query[...] = jnp.zeros_like(d_query)
        first, hat0, scale0 = norm_rope(proj[:, 0:128], q_gain[...], cos_b, sin_b)
        second, hat1, scale1 = norm_rope(proj[:, 128:256], q_gain[...], cos_b, sin_b)
        query = (jnp.concatenate([first, second], axis=0) * q_scale).astype(BF16)
        gate0 = jax.nn.sigmoid(proj[:, 512:513])
        gate1 = jax.nn.sigmoid(proj[:, 513:514])
        d_gated = dot(take_piece(slot, d_pieces), weights[:, 640:896])
        dg0, dg1 = d_gated[:, 0:128], d_gated[:, 128:256]
        out0, out1 = attn_o[:, 0:128], attn_o[:, 128:256]
        do0, do1 = (dg0 * gate0).astype(BF16), (dg1 * gate1).astype(BF16)
        logit0 = jnp.sum(dg0 * out0, axis=-1, keepdims=True) * gate0 * (1.0 - gate0)
        logit1 = jnp.sum(dg1 * out1, axis=-1, keepdims=True) * gate1 * (1.0 - gate1)
        d_held[pl.ds(here, rows), 512:640] = two_lanes(logit0, logit1, (rows, 128)).astype(BF16)
        delta0 = jnp.sum(do0.astype(F32) * out0, axis=-1, keepdims=True)
        delta1 = jnp.sum(do1.astype(F32) * out1, axis=-1, keepdims=True)
        delta_t = two_lanes(delta0, delta1, (rows, 128)).T
        delta = jnp.concatenate([delta_t[0:1], delta_t[1:2]], axis=1)
        lse_t = lse[...].T
        log_total = jnp.concatenate([lse_t[0:1], lse_t[1:2]], axis=1)
        d_out = jnp.concatenate([do0, do1], axis=0)

        def add_block(index, mask_of):
            there = pl.multiple_of(index * rows, rows)
            scores = dot(keys[pl.ds(there, rows), :], query, NT)
            probs = jnp.exp(scores - log_total)
            if mask_of is not None:
                probs = jnp.where(mask_of(there), probs, 0.0)
            d_probs = dot(values[pl.ds(there, rows), :], d_out, NT)
            d_scores = (probs * (d_probs - delta)).astype(BF16)
            d_values[pl.ds(there, rows), :] += dot(probs.astype(BF16), d_out)
            d_keys[pl.ds(there, rows), :] += dot(d_scores, query)
            d_query[...] += dot(keys_t[index], d_scores)

        def key_row():
            return lax.broadcasted_iota(jnp.int32, (rows, 2 * rows), 0)

        def causal(there):
            q_col = lax.broadcasted_iota(jnp.int32, (rows, 2 * rows), 1)
            q_col = jnp.where(q_col >= rows, q_col - rows, q_col)
            return (key_row() <= q_col) & (key_row() + there < live)

        whole = jnp.minimum(step, live // rows)

        def block(index, carry):
            add_block(index, None)
            return carry

        lax.fori_loop(0, whole, block, 0)

        @pl.when((whole < step) & (whole * rows < live))
        def _():
            add_block(whole, lambda there: key_row() + there < live)

        @pl.when(here < live)
        def _():
            add_block(step, causal)

        grads = d_query[...].T * q_scale
        raw0, part0 = norm_rope_back(grads[:rows], hat0, scale0, q_gain[...], cos_b, sin_b)
        raw1, part1 = norm_rope_back(grads[rows:], hat1, scale1, q_gain[...], cos_b, sin_b)
        d_held[pl.ds(here, rows), 0:128] = raw0.astype(BF16)
        d_held[pl.ds(here, rows), 128:256] = raw1.astype(BF16)
        gain_q[0:1, :] += part0 + part1

    @pl.when(step >= 8)
    def _():
        slot = (step - 4) % 8
        there = pl.multiple_of(table[PLACE + slot] * rows, rows)
        cos_k, sin_k = cosine[pl.ds(there, rows), :], sine[pl.ds(there, rows), :]
        _, hat, scale_rows = norm_rope(k_raw[pl.ds(there, rows), :], k_gain[...], cos_k, sin_k)
        raw, part = norm_rope_back(
            d_keys[pl.ds(there, rows), :], hat, scale_rows, k_gain[...], cos_k, sin_k
        )
        gain_k[0:1, :] += part
        d_held[pl.ds(there, rows), 256:384] = raw.astype(BF16)
        d_held[pl.ds(there, rows), 384:512] = d_values[pl.ds(there, rows), :].astype(BF16)
        d_block = d_held[pl.ds(there, rows), :]
        d_proj[...] = d_block
        back = dot(d_block, weights[:, 0:640], NT).astype(BF16)
        for piece in range(4):

            @pl.when(slot // 2 == piece)
            def _():
                back_pieces[piece][...] = back


def attend_forward_call(table, pieces, weights, cosine, sine, q_gain, k_gain):
    seq_len, width = cosine.shape[0], weights.shape[0]
    rows = seq_len // 8
    by_slot = lambda i, t: (t[SLOT + i], 0)
    by_place = lambda i, t: (i, 0)
    fixed = lambda i, t: (0, 0)
    whole = [
        pl.BlockSpec((rows, width), lambda i, t, k=k: (t[BLOCK + 8 * k + i], 0)) for k in range(4)
    ]
    pairs = seq_len * (seq_len + rows)
    return pl.pallas_call(
        attend_forward_kernel,
        grid_spec=pltpu.PrefetchScalarGridSpec(
            num_scalar_prefetch=1,
            grid=(8,),
            in_specs=whole
            + [
                pl.BlockSpec(weights.shape, fixed, pipeline_mode=pl.Buffered(1)),
                pl.BlockSpec((rows, 128), by_place),
                pl.BlockSpec((rows, 128), by_place),
                pl.BlockSpec((1, 128), fixed),
                pl.BlockSpec((1, 128), fixed),
            ],
            out_specs=[
                pl.BlockSpec((rows, 640), by_slot),
                pl.BlockSpec((rows, 256), by_slot),
                pl.BlockSpec((rows, 128), by_slot),
                pl.BlockSpec((rows, 256), by_slot),
            ]
            + whole,
            scratch_shapes=[
                pltpu.VMEM((seq_len, 128), BF16),
                pltpu.VMEM((seq_len, 256), BF16),
                pltpu.VMEM((2 * rows, 256), F32),
            ],
        ),
        out_shape=[
            jax.ShapeDtypeStruct((seq_len, 640), F32),
            jax.ShapeDtypeStruct((seq_len, 256), F32),
            jax.ShapeDtypeStruct((seq_len, 128), F32),
            jax.ShapeDtypeStruct((seq_len, 256), BF16),
        ]
        + [jax.ShapeDtypeStruct((2 * rows, width), BF16)] * 4,
        compiler_params=pltpu.CompilerParams(
            dimension_semantics=("arbitrary",), vmem_limit_bytes=62 << 20
        ),
        cost_estimate=cost(
            2 * seq_len * width * 896 + 4 * pairs * 128, 2 * seq_len * (2 * width + 2200), pairs
        ),
        name="attend_forward",
    )(table, *pieces, weights, cosine, sine, q_gain, k_gain)


def attend_backward_call(table, pieces, weights, proj, attn_o, lse, cosine, sine, q_gain, k_gain):
    seq_len, width = cosine.shape[0], weights.shape[0]
    rows = seq_len // 8
    by_slot = lambda i, t: (t[SLOT + jnp.minimum(i, 7)], 0)
    last_slot = lambda i, t: (jnp.where(i < 8, 4, (i - 4) % 8), 0)
    fixed = lambda i, t: (0, 0)
    pairs = seq_len * (seq_len + rows)
    return pl.pallas_call(
        attend_backward_kernel,
        grid_spec=pltpu.PrefetchScalarGridSpec(
            num_scalar_prefetch=1,
            grid=(16,),
            in_specs=[
                pl.BlockSpec(
                    (rows, width), lambda i, t, k=k: (t[BLOCK + 8 * k + jnp.minimum(i, 7)], 0)
                )
                for k in range(4)
            ]
            + [
                pl.BlockSpec(weights.shape, fixed, pipeline_mode=pl.Buffered(1)),
                pl.BlockSpec((rows, 640), by_slot),
                pl.BlockSpec((rows, 256), by_slot),
                pl.BlockSpec((rows, 128), by_slot),
                pl.BlockSpec((seq_len, 128), fixed, pipeline_mode=pl.Buffered(1)),
                pl.BlockSpec((seq_len, 128), fixed, pipeline_mode=pl.Buffered(1)),
                pl.BlockSpec((1, 128), fixed),
                pl.BlockSpec((1, 128), fixed),
            ],
            out_specs=[
                pl.BlockSpec((rows, 640), last_slot),
                pl.BlockSpec((8, 128), fixed),
                pl.BlockSpec((8, 128), fixed),
            ]
            + [
                pl.BlockSpec(
                    (rows, width), lambda i, t, k=k: (jnp.clip(i - 8 - (2 * k + 4) % 8, 0, 1), 0)
                )
                for k in range(4)
            ],
            scratch_shapes=[
                pltpu.VMEM((seq_len, 128), BF16),
                pltpu.VMEM((8, 128, rows), BF16),
                pltpu.VMEM((seq_len, 128), BF16),
                pltpu.VMEM((seq_len, 128), F32),
                pltpu.VMEM((seq_len, 128), F32),
                pltpu.VMEM((seq_len, 128), F32),
                pltpu.VMEM((128, 2 * rows), F32),
                pltpu.VMEM((seq_len, 640), BF16),
            ],
        ),
        out_shape=[
            jax.ShapeDtypeStruct((seq_len, 640), BF16),
            jax.ShapeDtypeStruct((8, 128), F32),
            jax.ShapeDtypeStruct((8, 128), F32),
        ]
        + [jax.ShapeDtypeStruct((2 * rows, width), BF16)] * 4,
        compiler_params=pltpu.CompilerParams(
            dimension_semantics=("arbitrary",), vmem_limit_bytes=62 << 20
        ),
        cost_estimate=cost(
            2 * seq_len * width * 896 + 10 * pairs * 128,
            2 * seq_len * (2 * width + 2200),
            pairs,
            LATE_SHARE,
        ),
        name="attend_backward",
    )(table, *pieces, weights, proj, attn_o, lse, cosine, sine, q_gain, k_gain)


def feed_forward_kernel(*refs):
    rows_near, rows_far, cot_near, cot_far, w_down_t, w_inner = refs[:6]
    sums = refs[6:-6]
    hidden_out, d_pre_out, down_near, down_far, back_near, back_far = refs[-6:]
    near = pl.program_id(0) < 2
    units = hidden_out.shape[1]
    pre = dot(jnp.where(near, rows_near[...], rows_far[...]), w_inner[...])
    d_hidden = dot(jnp.where(near, cot_near[...], cot_far[...]), w_down_t[...])
    gate_pre, up_pre = pre[:, :units], pre[:, units:]
    gate_sig = jax.nn.sigmoid(gate_pre)
    gate_act = gate_pre * gate_sig
    hidden_out[...] = (gate_act * up_pre).astype(BF16)
    d_pre_out[:, units:] = (d_hidden * gate_act).astype(BF16)
    d_pre_out[:, :units] = (
        d_hidden * up_pre * gate_sig * (1.0 + gate_pre * (1.0 - gate_sig))
    ).astype(BF16)
    back = dot(d_pre_out[...], w_inner[...], NT)
    down = dot(hidden_out[...], w_down_t[...], NT)
    if sums:
        back = back + jnp.where(near, sums[0][...], sums[1][...]).astype(F32)

    @pl.when(near)
    def _():
        back_near[...] = back.astype(BF16)
        down_near[...] = down.astype(BF16)

    @pl.when(jnp.logical_not(near))
    def _():
        back_far[...] = back.astype(BF16)
        down_far[...] = down.astype(BF16)


def feed_forward_call(rows, cots, w_down_t, w_inner, backs=()):
    count, width = rows[0].shape
    units = w_down_t.shape[1]
    tile = count // 2
    by_row = lambda i: (i, 0)
    fixed = lambda i: (0, 0)
    near = pl.BlockSpec((tile, width), lambda i: (jnp.minimum(i, 1), 0))
    far = pl.BlockSpec((tile, width), lambda i: (jnp.maximum(i - 2, 0), 0))
    wide = jax.ShapeDtypeStruct((count, width), BF16)
    out = pl.pallas_call(
        feed_forward_kernel,
        grid=(4,),
        in_specs=[near, far, near, far]
        + [pl.BlockSpec(w.shape, fixed, pipeline_mode=pl.Buffered(1)) for w in (w_down_t, w_inner)]
        + [near, far] * (len(backs) // 2),
        out_specs=[
            pl.BlockSpec((tile, units), by_row),
            pl.BlockSpec((tile, 2 * units), by_row),
            near,
            far,
            near,
            far,
        ],
        out_shape=[
            jax.ShapeDtypeStruct((2 * count, units), BF16),
            jax.ShapeDtypeStruct((2 * count, 2 * units), BF16),
            wide,
            wide,
            wide,
            wide,
        ],
        compiler_params=pltpu.CompilerParams(
            dimension_semantics=("arbitrary",), vmem_limit_bytes=52 << 20
        ),
        cost_estimate=cost(24 * count * width * units, 2 * width * (8 * count + 3 * units)),
        name="feed_forward",
    )(*rows, *cots, w_down_t, w_inner, *backs)
    return (out[0], out[1], (out[2], out[3]), (out[4], out[5]))


def weight_grad_call(n_parts, lefts, terms, weights=None):
    n_pieces = len(lefts[0])
    rows, width = lefts[0][0].shape
    columns = [pieces[0][0].shape[1] for _, pieces in terms]
    starts = [sum(columns[:k]) for k in range(len(terms))]
    total = sum(columns)
    arrays, place = ([], {})
    for _, pieces in terms:
        for array, _ in pieces:
            if id(array) not in place:
                place[id(array)] = len(arrays)
                arrays.append(array)
    n_left, n_terms = len(lefts), len(terms)

    def kernel(*refs):
        left_refs = refs[: n_left * n_pieces]
        right_refs = refs[len(left_refs) : len(left_refs) + len(arrays)]
        rest = list(refs[len(left_refs) + len(arrays) :])
        if weights is not None:
            weights_ref = rest.pop(0)
        out = rest.pop(0)
        if weights is not None:
            gain = rest.pop(0)
        left_buf, right_buf = rest[:n_left], rest[n_left : n_left + n_terms]
        accs, sems = rest[n_left + n_terms : -1], rest[-1]

        def copies(piece, slot):
            made = [
                pltpu.make_async_copy(
                    left_refs[k * n_pieces + piece], left_buf[k].at[slot], sems.at[slot, k]
                )
                for k in range(n_left)
            ]
            for k, (_, pieces) in enumerate(terms):
                array, first = pieces[piece]
                made.append(
                    pltpu.make_async_copy(
                        right_refs[place[id(array)]].at[pl.ds(first, rows)],
                        right_buf[k].at[slot],
                        sems.at[slot, n_left + k],
                    )
                )
            return made

        for copy in copies(0, 0):
            copy.start()
        for acc in accs:
            acc[...] = jnp.zeros_like(acc)

        def body(index, carry):
            slot = lax.rem(index, 2)
            for piece in range(1, n_pieces):

                @pl.when(index + 1 == piece)
                def _():
                    for copy in copies(piece, piece % 2):
                        copy.start()

            for copy in copies(0, slot):
                copy.wait()
            for k, (left, _) in enumerate(terms):
                for first in range(0, columns[k], 256):
                    some = slice(first, min(first + 256, columns[k]))
                    accs[k][some, :] += dot(right_buf[k][slot, :, some], left_buf[left][slot], TN)
            return carry

        lax.fori_loop(0, n_pieces, body, 0)
        part = width // n_parts
        for p in range(n_parts):
            for k in range(n_terms):
                start = p * total + starts[k]
                out[start : start + columns[k], :] = accs[k][:, p * part : (p + 1) * part].astype(
                    BF16
                )
        if weights is not None:
            scaled = accs[0][...] * weights_ref[:, : columns[0]].T.astype(F32)
            gain[...] = jnp.broadcast_to(jnp.sum(scaled, axis=0, keepdims=True), gain.shape)

    out_shape = [jax.ShapeDtypeStruct((n_parts * total, width // n_parts), BF16)]
    vmem = pl.BlockSpec(memory_space=pltpu.VMEM)
    operands = [piece for pieces in lefts for piece in pieces] + arrays
    in_specs = [pl.BlockSpec(memory_space=pl.ANY)] * len(operands)
    if weights is not None:
        operands.append(weights)
        in_specs.append(vmem)
        out_shape.append(jax.ShapeDtypeStruct((8, width), F32))
    return pl.pallas_call(
        kernel,
        in_specs=in_specs,
        out_specs=[vmem] * len(out_shape),
        out_shape=out_shape,
        scratch_shapes=[pltpu.VMEM((2, rows, width), BF16)] * n_left
        + [pltpu.VMEM((2, rows, c), BF16) for c in columns]
        + [pltpu.VMEM((c, width), F32) for c in columns]
        + [pltpu.SemaphoreType.DMA((2, n_left + n_terms))],
        compiler_params=pltpu.CompilerParams(vmem_limit_bytes=56 << 20),
        cost_estimate=cost(
            2 * n_pieces * rows * width * total,
            2 * n_pieces * rows * (n_left * width + total) + 2 * width * total,
            0,
            LATE_SHARE,
        ),
        name="weight_grad",
    )(*operands)


def pack_attention_kernel(index, query, key, value, headgate, out, packed):
    half = pl.program_id(0) ^ index[0]
    packed[0, :, 0:256] = query[...]
    packed[0, :, 256:384] = key[...]
    packed[0, :, 384:512] = value[...]
    gates = headgate[...].astype(F32)
    first = jnp.where(half == 0, gates[:, 0:1], gates[:, 2:3])
    second = jnp.where(half == 0, gates[:, 1:2], gates[:, 3:4])
    packed[0, :, 512:640] = two_lanes(first, second, (packed.shape[1], 128)).astype(BF16)
    packed[0, :, 640:896] = out[...].T


def pack_attention(index, query, key, value, headgate, out):
    rows = query.shape[0]
    half = lambda i, t: (0, i ^ t[0])
    return pl.pallas_call(
        pack_attention_kernel,
        grid_spec=pltpu.PrefetchScalarGridSpec(
            num_scalar_prefetch=1,
            grid=(2,),
            in_specs=[
                pl.BlockSpec((rows, 256), half),
                pl.BlockSpec((rows, 128), half),
                pl.BlockSpec((rows, 128), half),
                pl.BlockSpec(headgate.shape, lambda i, t: (0, 0)),
                pl.BlockSpec((256, out.shape[1]), lambda i, t: (i ^ t[0], 0)),
            ],
            out_specs=pl.BlockSpec((1, rows, 896), lambda i, t: (i, 0, 0)),
        ),
        out_shape=jax.ShapeDtypeStruct((2, rows, 896), BF16),
        cost_estimate=cost(0, 4 * rows * 896 * 2),
        name="pack_attention",
    )(index, query, key, value, headgate, out)


def unpack_attention_kernel(index, kept, came, out_kept, out_came, query, key, value, headgate, out):
    flip = index[0] == 1

    def ordered(mine, other):
        return [
            jnp.where(flip, other[...], mine[...]).astype(F32),
            jnp.where(flip, mine[...], other[...]).astype(F32),
        ]

    for k, part in enumerate(ordered(kept, came)):
        query[:, 256 * k : 256 * k + 256] = part[0:256].T
        key[:, 128 * k : 128 * k + 128] = part[256:384].T
        value[:, 128 * k : 128 * k + 128] = part[384:512].T
        headgate[:, 2 * k : 2 * k + 2] = part[512:640].T[:, 0:2]
    for k, part in enumerate(ordered(out_kept, out_came)):
        out[256 * k : 256 * k + 256, :] = part


def unpack_attention(index, kept, came, out_kept, out_came):
    rows = kept.shape[1]
    vmem = pl.BlockSpec(memory_space=pltpu.VMEM)
    shapes = [(rows, 512), (rows, 256), (rows, 256), (rows, 4), (512, rows)]
    return pl.pallas_call(
        unpack_attention_kernel,
        in_specs=[pl.BlockSpec(memory_space=pltpu.SMEM)] + [vmem] * 4,
        out_specs=[vmem] * 5,
        out_shape=[jax.ShapeDtypeStruct(shape, F32) for shape in shapes],
        cost_estimate=cost(0, 8 * rows * 896),
        name="unpack_attention",
    )(index, kept, came, out_kept, out_came)


def pack_feed_forward_kernel(index, gate, up, down, packed):
    units = gate.shape[1]
    packed[0, :, :units] = down[...].T
    packed[0, :, units : 2 * units] = gate[...]
    packed[0, :, 2 * units :] = up[...]


def pack_feed_forward(index, gate, up, down):
    rows, units = gate.shape[0], gate.shape[1] // 4
    quarter = pl.BlockSpec((rows, units), lambda i, t: (0, i ^ t[0]))
    return pl.pallas_call(
        pack_feed_forward_kernel,
        grid_spec=pltpu.PrefetchScalarGridSpec(
            num_scalar_prefetch=1,
            grid=(4,),
            in_specs=[
                quarter,
                quarter,
                pl.BlockSpec((units, rows), lambda i, t: (i ^ t[0], 0)),
            ],
            out_specs=pl.BlockSpec((1, rows, 3 * units), lambda i, t: (i, 0, 0)),
        ),
        out_shape=jax.ShapeDtypeStruct((4, rows, 3 * units), BF16),
        cost_estimate=cost(0, 8 * rows * units * 6),
        name="pack_feed_forward",
    )(index, gate, up, down)


def unpack_feed_forward_kernel(index, *refs):
    pieces, (gate, up, down) = refs[:8], refs[8:]
    units = gate.shape[1]
    apart = pl.program_id(0) ^ index[0]

    def of_piece(group):
        low = jnp.where(apart == 0, group[0][...], group[1][...])
        high = jnp.where(apart == 2, group[2][...], group[3][...])
        return jnp.where(apart < 2, low, high).astype(F32)

    inner = of_piece(pieces[:4])
    gate[...] = inner[:units].T
    up[...] = inner[units:].T
    down[...] = of_piece(pieces[4:])


def unpack_feed_forward(index, inners, downs):
    units, rows = downs[0].shape
    quarter = pl.BlockSpec((rows, units), lambda i, t: (0, i))
    whole = [pl.BlockSpec(v.shape, lambda i, t: (0, 0)) for v in (*inners, *downs)]
    wide = jax.ShapeDtypeStruct((rows, 4 * units), F32)
    return pl.pallas_call(
        unpack_feed_forward_kernel,
        grid_spec=pltpu.PrefetchScalarGridSpec(
            num_scalar_prefetch=1,
            grid=(4,),
            in_specs=whole,
            out_specs=[quarter, quarter, pl.BlockSpec((units, rows), lambda i, t: (i, 0))],
        ),
        out_shape=[wide, wide, jax.ShapeDtypeStruct((4 * units, rows), F32)],
        cost_estimate=cost(0, 24 * rows * units * 4),
        name="unpack_feed_forward",
    )(index, *inners, *downs)


def pick(flag, first, second):
    return jnp.where(flag, first, second)


def reorder_by(pieces, index):
    low, high = (index & 1) == 1, (index & 2) == 2
    swapped = [pick(low, pieces[j ^ 1], pieces[j]) for j in range(4)]
    return [pick(high, swapped[j ^ 2], swapped[j]) for j in range(4)]


def local_plane(
    inputs,
    cotangent,
    seq_counts,
    seq_bucket,
    attn_norm_gain,
    q_norm_gain,
    k_norm_gain,
    w_query,
    w_key,
    w_value,
    w_headgate,
    w_out,
    ffn_norm_gain,
    w_gate,
    w_up,
    w_down,
):
    micro_batches, row_count, model_width = inputs.shape
    both = range(micro_batches)
    n_dp = lax.axis_size("dp")
    head_idx = lax.axis_index("head")
    mp_idx = lax.axis_index("mp")
    dp_idx = lax.axis_index("dp")
    core = head_idx & 1
    plane_idx = head_idx * 2 + mp_idx
    seq_len = row_count * 8
    units = w_gate.shape[1] // 4
    head_at = head_idx[None].astype(jnp.int32)
    mp_at = mp_idx[None].astype(jnp.int32)
    order = Order()

    def after(value, *ahead):
        return lax.optimization_barrier((value, ahead))[0]

    halves = pack_attention(mp_at, w_query, w_key, w_value, w_headgate, w_out)
    attn_came = swap(halves[1], BIT_X)

    slot_ids = jnp.arange(micro_batches * n_dp, dtype=jnp.int32)
    slot_count = jnp.sum(
        jnp.where(seq_bucket[None, :] == slot_ids[:, None], seq_counts[None, :], 0), axis=1
    )
    own_pos = plane_idx * row_count + jnp.arange(row_count, dtype=jnp.int32)
    live = [slot_count[n * n_dp + dp_idx] for n in both]
    x_float = [inputs[n].astype(F32) for n in both]
    scale1 = [rms_scale(x) for x in x_float]
    normed1 = [x * scale for x, scale in zip(x_float, scale1)]
    xn1_own = [(n * attn_norm_gain).astype(BF16) for n in normed1]
    cot_live = [
        cotangent[n].astype(F32) * (own_pos < live[n]).astype(F32)[:, None] for n in both
    ]
    cot_own = [c.astype(BF16) for c in cot_live]
    xn1, xn2, cot, d_attn = ([None] * micro_batches for _ in range(4))
    xn1[0] = Gather(order, xn1_own[0])
    is_first = mp_idx == 0
    attn_rows = jnp.concatenate(
        [pick(is_first, halves[0], attn_came), pick(is_first, attn_came, halves[0])], axis=0
    )
    w_attn = lax.all_gather(attn_rows, "dp", axis=0, tiled=True)

    quarters = pack_feed_forward(head_at, w_gate, w_up, w_down)
    traded = [quarters[0]] + [swap(quarters[r], r * 2) for r in (1, 2, 3)]
    near = xn1[0].second()
    parts = [[t[:, :units] for t in traded], [t[:, units:] for t in traded]]
    ffn_rows = [jnp.concatenate(reorder_by(part, head_idx), axis=0) for part in parts]
    ffn_rows = after(tuple(ffn_rows), attn_rows)
    w_ffn = [lax.all_gather(rows, "dp", axis=0, tiled=True) for rows in ffn_rows]

    xn1[1] = Gather(order, after(xn1_own[1], traded[1]))
    tables = [attend_table(plane_idx, core, count) for count in live]
    table_cos, table_sin = rope_tables(jnp.arange(seq_len, dtype=jnp.int32), 64)
    table_cos, table_sin = table_cos[:, 0, :], table_sin[:, 0, :]
    cosine = jnp.concatenate([table_cos, table_cos], axis=1)
    sine = jnp.concatenate([-table_sin, table_sin], axis=1)
    fixed = (cosine, sine, q_norm_gain[None, :], k_norm_gain[None, :])
    att, out_sum = ([None] * micro_batches for _ in range(2))

    def attend(n):
        att[n] = order.run(
            lambda *pieces: attend_forward_call(tables[n], pieces, w_attn, *fixed), *xn1[n].pieces
        )
        out_sum[n] = Scatter(order, att[n][6], att[n][7])

    cot[0] = Gather(order, after(cot_own[0], xn1[1].second()))
    order.need(xn1[0].third(), cot[0].second())
    attend(0)
    order.need(xn1[1].third(), cot[0].third())
    order.need(*out_sum[0].add(att[0][4], att[0][5]), w_ffn[0])
    attend(1)
    order.need(out_sum[0].third())

    hidden1, scale2, normed2 = ([None] * micro_batches for _ in range(3))

    def middle(n):
        hidden1[n] = x_float[n] + out_sum[n].result()
        scale2[n] = rms_scale(hidden1[n])
        normed2[n] = hidden1[n] * scale2[n]
        rows = (normed2[n] * ffn_norm_gain).astype(BF16)
        xn2[n] = Gather(order, rows)
        return rows

    rows = middle(0)
    order.need(*out_sum[1].add(after(att[1][4], rows), att[1][5]))
    order.need(xn2[0].second(), out_sum[1].third())
    order.need(xn2[0].third(), middle(1))
    cot[1] = Gather(order, after(cot_own[1], xn2[0].pieces[1]))

    feed = {}
    down, back = ([None] * micro_batches for _ in range(2))

    def feed_other(n):
        feed[n, 1] = order.run(
            lambda *v: feed_forward_call(v[0:2], v[2:4], *w_ffn), *xn2[n].pieces[2:], *cot[n].pieces[2:]
        )
        back[n] = Scatter(order, *feed[n, 1][3])

    def feed_mine(n):
        feed[n, 0] = order.run(
            lambda *v: feed_forward_call(v[0:2], v[2:4], *w_ffn, order.pin(back[n].came)),
            *xn2[n].pieces[:2],
            *cot[n].pieces[:2],
        )
        back[n].second(*feed[n, 0][3])
        down[n] = Scatter(order, *after(feed[n, 1][2], feed[n, 0][0]))

    d_hidden1 = [None] * micro_batches
    gain_ffn = []

    def turn(n):
        d_xn2 = back[n].result()
        gain_ffn.append(jnp.sum(d_xn2 * normed2[n], axis=0))
        d_hidden1[n] = cot_live[n] + norm_back(d_xn2, normed2[n], scale2[n], ffn_norm_gain)
        rows = d_hidden1[n].astype(BF16)
        d_attn[n] = Gather(order, rows)
        return rows

    def row_pieces(array):
        count = array.shape[0] // (2 * row_count)
        return [(array, 2 * row_count * k) for k in range(count)]

    def of_feed(which):
        return [p for n in both for side in (0, 1) for p in row_pieces(feed[n, side][which])]

    def rows_of(gathers):
        return [piece for gather in gathers for piece in gather.pieces]

    def grad_call(lefts, terms, weights=None):
        count = [len(left) for left in lefts]
        return order.run(
            lambda *v: weight_grad_call(
                n_dp,
                [list(v[sum(count[:k]) : sum(count[: k + 1])]) for k in range(len(lefts))],
                terms,
                weights,
            ),
            *[piece for left in lefts for piece in left],
        )

    def sum_over_dp(values):
        return lax.psum_scatter(values, "dp", scatter_dimension=0, tiled=True)

    def quarters_of(values):
        width = values.shape[1] // 4
        quarter = lambda k: lax.dynamic_slice_in_dim(values, k * width, width, 1)
        return [quarter(head_idx)] + [swap(quarter(head_idx ^ r), r * 2) for r in (1, 2, 3)]

    feed_other(0)
    order.need(xn2[1].second(), cot[1].second())
    feed_mine(0)
    order.need(cot[1].third(), xn2[1].third())
    feed_other(1)
    order.need(back[0].third(), *down[0].add(*feed[0, 0][2]))
    feed_mine(1)
    order.need(turn(0))
    grads_inner = sum_over_dp(grad_call([rows_of(xn2)], [(0, of_feed(1))])[0])
    order.need(d_attn[0].second(), down[0].third())
    grads_down = sum_over_dp(grad_call([rows_of(cot)], [(0, of_feed(0))])[0])
    order.need(back[1].third(), d_attn[0].third(), turn(1))

    d_proj, gain_parts, rows_sum = ([None] * micro_batches for _ in range(3))

    def attend_back(n):
        out = order.run(
            lambda *v: attend_backward_call(
                tables[n], v, w_attn, att[n][0], att[n][1], att[n][2], *fixed
            ),
            *d_attn[n].pieces,
        )
        d_proj[n] = out[0]
        gain_parts[n] = (out[1][0], out[2][0])
        rows_sum[n] = Scatter(order, out[5], out[6])
        return out

    def finish(n):
        d_xn1 = rows_sum[n].result()
        return (d_hidden1[n] + norm_back(d_xn1, normed1[n], scale1[n], attn_norm_gain)).astype(BF16)

    outputs, input_grads = ([None] * micro_batches for _ in range(2))
    back_0 = attend_back(0)
    order.need(d_attn[1].second(), *down[1].add(*feed[1, 0][2]))
    order.need(*rows_sum[0].add(back_0[3], back_0[4]), d_attn[1].third())
    grads_out = sum_over_dp(
        grad_call(
            [rows_of(d_attn)], [(0, [p for n in both for p in row_pieces(att[n][3])])]
        )[0]
    )
    inner_quarters = quarters_of(grads_inner)
    order.need(grads_inner)
    back_1 = attend_back(1)
    outputs[0] = (hidden1[0] + down[0].result()).astype(BF16)
    order.need(rows_sum[0].third(), down[1].third(), *inner_quarters)
    order.need(*rows_sum[1].add(back_1[3], back_1[4]))
    down_quarters = quarters_of(grads_down)
    order.need(grads_down)
    grads_proj, gain_rows = grad_call(
        [rows_of(xn1)], [(0, [p for n in both for p in row_pieces(d_proj[n])])], w_attn
    )
    grads_proj = sum_over_dp(grads_proj)
    input_grads[0] = finish(0)
    order.need(rows_sum[1].third(), *down_quarters)
    grad_gate, grad_up, grad_down = order.run(
        lambda *v: unpack_feed_forward(head_at, v[:4], v[4:]), *inner_quarters, *down_quarters
    )
    outputs[1] = (hidden1[1] + down[1].result()).astype(BF16)
    input_grads[1] = finish(1)

    gains = jnp.concatenate(
        [gain_rows[0] / attn_norm_gain, gain_ffn[0] + gain_ffn[1]]
        + [gain_parts[0][k] + gain_parts[1][k] for k in range(2)]
    ).reshape(-1, 128)
    for bits in (BIT_C, BIT_X, BIT_Y):
        gains = gains + swap(gains, bits)
    for step in (1, 2):
        gains = gains + lax.ppermute(gains, "dp", [(i, i ^ step) for i in range(4)])
    gains = gains.reshape(-1)
    sum_attn, sum_gain_ffn = gains[:model_width], gains[model_width : 2 * model_width]
    sum_query, sum_key = gains[-256:-128], gains[-128:]

    def halves_of(values):
        left, right = values[:, :row_count], values[:, row_count:]
        return pick(is_first, left, right), swap(pick(is_first, right, left), BIT_X)

    grad_query, grad_key, grad_value, grad_headgate, grad_out = unpack_attention(
        mp_at, *halves_of(grads_proj), *halves_of(grads_out)
    )
    return (
        jnp.stack(outputs),
        jnp.stack(input_grads),
        sum_attn,
        sum_query,
        sum_key,
        grad_query,
        grad_key,
        grad_value,
        grad_headgate,
        grad_out,
        sum_gain_ffn,
        grad_gate,
        grad_up,
        grad_down,
    )


def choose_local(mesh):
    if mesh.shape["head"] == 4 and mesh.shape["mp"] == 2 and mesh.shape["dp"] == 4:
        return local_plane
    return local


def solution(mesh):
    placed = (
        P(None, ("dp", "head", "mp"), None),
        P(None, ("dp", "head", "mp"), None),
        P(),
        P(),
        P(),
        P(),
        P(),
        P(("dp", "mp"), "head"),
        P(("dp", "mp"), "head"),
        P(("dp", "mp"), "head"),
        P(("dp", "mp"), "head"),
        P("head", ("dp", "mp")),
        P(),
        P(("dp", "head"), "mp"),
        P(("dp", "head"), "mp"),
        P("mp", ("dp", "head")),
    )
    return jax.shard_map(
        choose_local(mesh),
        mesh=mesh,
        in_specs=placed,
        out_specs=(
            P(None, ("dp", "head", "mp"), None),
            P(None, ("dp", "head", "mp"), None),
            P(),
            P(),
            P(),
            P(("dp", "mp"), "head"),
            P(("dp", "mp"), "head"),
            P(("dp", "mp"), "head"),
            P(("dp", "mp"), "head"),
            P("head", ("dp", "mp")),
            P(),
            P(("dp", "head"), "mp"),
            P(("dp", "head"), "mp"),
            P("mp", ("dp", "head")),
        ),
        check_vma=False,
    )
```

```python
import functools

import jax
import jax.numpy as jnp
from jax import lax
from jax.experimental import pallas as pl
from jax.experimental.pallas import tpu as pltpu
from jax.sharding import PartitionSpec as P

EPS = 1e-06
ROPE_BASE = 1000000.0
NEG_FILL = -1e30


def rms_scale(values):
    return lax.rsqrt(jnp.mean(values * values, axis=-1, keepdims=True) + EPS)


def norm_back(grad_out, normed, scale_rows, gain):
    d_normed = grad_out * gain
    return scale_rows * (d_normed - normed * jnp.mean(d_normed * normed, axis=-1, keepdims=True))


def rope_tables(positions, half):
    freq = jnp.power(ROPE_BASE, -jnp.arange(half, dtype=jnp.float32) / half)
    angle = positions.astype(jnp.float32)[:, None] * freq[None, :]
    return (jnp.cos(angle)[:, None, :], jnp.sin(angle)[:, None, :])


def rotate(values, cosine, sine):
    half = values.shape[-1] // 2
    first = values[..., :half]
    second = values[..., half:]
    return jnp.concatenate(
        [first * cosine - second * sine, second * cosine + first * sine], axis=-1
    )


def rotate_back(grads, cosine, sine):
    half = grads.shape[-1] // 2
    first = grads[..., :half]
    second = grads[..., half:]
    return jnp.concatenate(
        [first * cosine + second * sine, second * cosine - first * sine], axis=-1
    )


def masked_scores(q_group, key_piece, query_pos, key_pos, live_count):
    scores = jnp.einsum("qhgd,khd->hgqk", q_group, key_piece, preferred_element_type=jnp.float32)
    allowed = (key_pos[None, :] <= query_pos[:, None]) & (key_pos[None, :] < live_count)
    return (scores, allowed)


def split_keys(keys, values, key_pos, key_block):
    n_blocks = keys.shape[0] // key_block
    key_pieces = keys.reshape(n_blocks, key_block, keys.shape[1], keys.shape[2])
    value_pieces = values.reshape(n_blocks, key_block, values.shape[1], values.shape[2])
    return (key_pieces, value_pieces, key_pos.reshape(n_blocks, key_block))


def attend_forward(q_group, keys, values, query_pos, key_pos, live_count, key_block):
    n_query, kv_here, group_size, head_dim = q_group.shape
    key_pieces, value_pieces, pos_pieces = split_keys(keys, values, key_pos, key_block)

    def stats(carry, piece):
        row_max, row_total = carry
        key_piece, piece_pos = piece
        scores, allowed = masked_scores(q_group, key_piece, query_pos, piece_pos, live_count)
        scores = jnp.where(allowed, scores, NEG_FILL)
        new_max = jnp.maximum(row_max, jnp.max(scores, axis=-1))
        kept_exp = jnp.where(allowed, jnp.exp(scores - new_max[..., None]), 0.0)
        row_total = row_total * jnp.exp(row_max - new_max) + jnp.sum(kept_exp, axis=-1)
        return ((new_max, row_total), None)

    start = (
        jnp.full((kv_here, group_size, n_query), NEG_FILL, jnp.float32),
        jnp.zeros((kv_here, group_size, n_query), jnp.float32),
    )
    (row_max, row_total), unused = lax.scan(stats, start, (key_pieces, pos_pieces))
    log_total = row_max + jnp.log(row_total)

    def weigh(acc, piece):
        key_piece, value_piece, piece_pos = piece
        scores, allowed = masked_scores(q_group, key_piece, query_pos, piece_pos, live_count)
        prob_low = jnp.where(allowed, jnp.exp(scores - log_total[..., None]), 0.0).astype(
            jnp.bfloat16
        )
        acc = acc + jnp.einsum(
            "hgqk,khd->qhgd", prob_low, value_piece, preferred_element_type=jnp.float32
        )
        return (acc, None)

    attn_o, unused = lax.scan(
        weigh, jnp.zeros(q_group.shape, jnp.float32), (key_pieces, value_pieces, pos_pieces)
    )
    return (attn_o, log_total)


def attend_backward(
    q_group, keys, values, query_pos, key_pos, live_count, key_block, log_total, d_out, delta
):
    kv_here = keys.shape[1]
    head_dim = keys.shape[2]
    key_pieces, value_pieces, pos_pieces = split_keys(keys, values, key_pos, key_block)

    def backstep(d_query, piece):
        key_piece, value_piece, piece_pos = piece
        scores, allowed = masked_scores(q_group, key_piece, query_pos, piece_pos, live_count)
        probs = jnp.where(allowed, jnp.exp(scores - log_total[..., None]), 0.0)
        d_probs = jnp.einsum(
            "qhgd,khd->hgqk", d_out, value_piece, preferred_element_type=jnp.float32
        )
        d_scores = (probs * (d_probs - delta[..., None])).astype(jnp.bfloat16)
        d_query = d_query + jnp.einsum(
            "hgqk,khd->qhgd", d_scores, key_piece, preferred_element_type=jnp.float32
        )
        d_key = jnp.einsum("hgqk,qhgd->khd", d_scores, q_group, preferred_element_type=jnp.float32)
        d_value = jnp.einsum(
            "hgqk,qhgd->khd", probs.astype(jnp.bfloat16), d_out, preferred_element_type=jnp.float32
        )
        return (d_query, (d_key, d_value))

    d_query, (d_key, d_value) = lax.scan(
        backstep, jnp.zeros(q_group.shape, jnp.float32), (key_pieces, value_pieces, pos_pieces)
    )
    return (d_query, d_key.reshape(-1, kv_here * head_dim), d_value.reshape(-1, kv_here * head_dim))


def gather_weights(w_query, w_key, w_value, w_headgate, w_out, w_gate, w_up, w_down):
    attn_parts = (
        lax.all_gather(w_query, ("dp", "mp"), axis=0, tiled=True),
        lax.all_gather(w_key, ("dp", "mp"), axis=0, tiled=True),
        lax.all_gather(w_value, ("dp", "mp"), axis=0, tiled=True),
        lax.all_gather(w_headgate, ("dp", "mp"), axis=0, tiled=True),
        lax.all_gather(w_out, ("dp", "mp"), axis=1, tiled=True),
    )
    ffn_parts = (
        lax.all_gather(w_gate, ("dp", "head"), axis=0, tiled=True),
        lax.all_gather(w_up, ("dp", "head"), axis=0, tiled=True),
        lax.all_gather(w_down, ("dp", "head"), axis=1, tiled=True),
    )
    return tuple(attn_parts) + tuple(ffn_parts)


def reduce_grads(g_query, g_key, g_value, g_headgate, g_out, g_gate, g_up, g_down):
    attn_parts = (
        lax.psum_scatter(
            g_query.astype(jnp.bfloat16), ("dp", "mp"), scatter_dimension=0, tiled=True
        ).astype(jnp.float32),
        lax.psum_scatter(
            g_key.astype(jnp.bfloat16), ("dp", "mp"), scatter_dimension=0, tiled=True
        ).astype(jnp.float32),
        lax.psum_scatter(
            g_value.astype(jnp.bfloat16), ("dp", "mp"), scatter_dimension=0, tiled=True
        ).astype(jnp.float32),
        lax.psum_scatter(
            g_headgate.astype(jnp.bfloat16), ("dp", "mp"), scatter_dimension=0, tiled=True
        ).astype(jnp.float32),
        lax.psum_scatter(
            g_out.astype(jnp.bfloat16), ("dp", "mp"), scatter_dimension=1, tiled=True
        ).astype(jnp.float32),
    )
    ffn_parts = (
        lax.psum_scatter(
            g_gate.astype(jnp.bfloat16), ("dp", "head"), scatter_dimension=0, tiled=True
        ).astype(jnp.float32),
        lax.psum_scatter(
            g_up.astype(jnp.bfloat16), ("dp", "head"), scatter_dimension=0, tiled=True
        ).astype(jnp.float32),
        lax.psum_scatter(
            g_down.astype(jnp.bfloat16), ("dp", "head"), scatter_dimension=1, tiled=True
        ).astype(jnp.float32),
    )
    return tuple(attn_parts) + tuple(ffn_parts)


def local(
    inputs,
    cotangent,
    seq_counts,
    seq_bucket,
    attn_norm_gain,
    q_norm_gain,
    k_norm_gain,
    w_query,
    w_key,
    w_value,
    w_headgate,
    w_out,
    ffn_norm_gain,
    w_gate,
    w_up,
    w_down,
):
    micro_batches, row_count, model_width = inputs.shape
    n_head = lax.axis_size("head")
    n_mp = lax.axis_size("mp")
    n_dp = lax.axis_size("dp")
    head_idx = lax.axis_index("head")
    mp_idx = lax.axis_index("mp")
    dp_idx = lax.axis_index("dp")
    head_dim = q_norm_gain.shape[0]
    q_heads = w_query.shape[1] // head_dim
    kv_heads = w_key.shape[1] // head_dim
    group_size = q_heads // kv_heads
    q_scale = head_dim ** (-0.5)
    seq_len = row_count * n_head * n_mp
    key_block = min(512, seq_len)
    n_query = n_head * row_count
    slot_ids = jnp.arange(micro_batches * n_dp, dtype=jnp.int32)
    slot_count = jnp.sum(
        jnp.where(seq_bucket[None, :] == slot_ids[:, None], seq_counts[None, :], 0), axis=1
    )
    local_idx = jnp.arange(row_count, dtype=jnp.int32)
    own_pos = head_idx * n_mp * row_count + mp_idx * row_count + local_idx
    query_idx = jnp.arange(n_query, dtype=jnp.int32)
    query_pos = (
        query_idx // row_count * n_mp * row_count + mp_idx * row_count + query_idx % row_count
    )
    key_idx = jnp.arange(seq_len, dtype=jnp.int32)
    key_pos = (
        key_idx % n_query // row_count * n_mp * row_count
        + key_idx // n_query * row_count
        + key_idx % row_count
    )
    rope_cos, rope_sin = rope_tables(query_pos, head_dim // 2)
    grad_total = None
    gain_attn = jnp.zeros((model_width,), jnp.float32)
    gain_query = jnp.zeros((head_dim,), jnp.float32)
    gain_key = jnp.zeros((head_dim,), jnp.float32)
    gain_ffn = jnp.zeros((model_width,), jnp.float32)
    outputs = []
    input_grads = []
    for micro_batch in range(micro_batches):
        weights = gather_weights(w_query, w_key, w_value, w_headgate, w_out, w_gate, w_up, w_down)
        wq_full, wk_full, wv_full, wg_full, wo_full, wgate_full, wup_full, wdown_full = weights
        live_count = slot_count[micro_batch * n_dp + dp_idx]
        x_float = inputs[micro_batch].astype(jnp.float32)
        scale1 = rms_scale(x_float)
        normed1 = x_float * scale1
        xn1 = (normed1 * attn_norm_gain).astype(jnp.bfloat16)
        gathered_rows = lax.all_gather(xn1, "head", axis=0, tiled=True)
        q_raw = jnp.dot(gathered_rows, wq_full, preferred_element_type=jnp.float32).reshape(
            n_query, q_heads, head_dim
        )
        k_raw = jnp.dot(gathered_rows, wk_full, preferred_element_type=jnp.float32).reshape(
            n_query, kv_heads, head_dim
        )
        value_low = jnp.dot(gathered_rows, wv_full, preferred_element_type=jnp.float32).astype(
            jnp.bfloat16
        )
        gate_logit = jnp.dot(gathered_rows, wg_full, preferred_element_type=jnp.float32)
        q_rms = rms_scale(q_raw)
        q_hat = q_raw * q_rms
        query_low = (rotate(q_hat * q_norm_gain, rope_cos, rope_sin) * q_scale).astype(jnp.bfloat16)
        k_rms = rms_scale(k_raw)
        k_hat = k_raw * k_rms
        key_low = rotate(k_hat * k_norm_gain, rope_cos, rope_sin).astype(jnp.bfloat16)
        all_keys, all_values = (
            lax.all_gather(key_low.reshape(n_query, kv_heads * head_dim), "mp", axis=0, tiled=True),
            lax.all_gather(value_low, "mp", axis=0, tiled=True),
        )
        all_keys = all_keys.reshape(seq_len, kv_heads, head_dim)
        all_values = all_values.reshape(seq_len, kv_heads, head_dim)
        q_group = query_low.reshape(n_query, kv_heads, group_size, head_dim)
        attn_o, log_total = attend_forward(
            q_group, all_keys, all_values, query_pos, key_pos, live_count, key_block
        )
        gate_prob = jax.nn.sigmoid(gate_logit)
        attn_heads = attn_o.reshape(n_query, q_heads, head_dim)
        gated = (
            (attn_heads * gate_prob[..., None])
            .reshape(n_query, q_heads * head_dim)
            .astype(jnp.bfloat16)
        )
        attn_sum = lax.psum_scatter(
            jnp.dot(gated, wo_full, preferred_element_type=jnp.float32).astype(jnp.bfloat16),
            "head",
            scatter_dimension=0,
            tiled=True,
        ).astype(jnp.float32)
        hidden1 = x_float + attn_sum
        scale2 = rms_scale(hidden1)
        normed2 = hidden1 * scale2
        xn2 = (normed2 * ffn_norm_gain).astype(jnp.bfloat16)
        live = (own_pos < live_count).astype(jnp.float32)[:, None]
        cot_live = cotangent[micro_batch].astype(jnp.float32) * live
        ffn_in, cot_rows = (
            lax.all_gather(xn2, "mp", axis=0, tiled=True),
            lax.all_gather(cot_live.astype(jnp.bfloat16), "mp", axis=0, tiled=True),
        )
        gate_pre = jnp.dot(ffn_in, wgate_full, preferred_element_type=jnp.float32)
        up_pre = jnp.dot(ffn_in, wup_full, preferred_element_type=jnp.float32)
        gate_sig = jax.nn.sigmoid(gate_pre)
        gate_act = gate_pre * gate_sig
        hidden = (gate_act * up_pre).astype(jnp.bfloat16)
        ffn_sum = lax.psum_scatter(
            jnp.dot(hidden, wdown_full, preferred_element_type=jnp.float32).astype(jnp.bfloat16),
            "mp",
            scatter_dimension=0,
            tiled=True,
        ).astype(jnp.float32)
        outputs.append((hidden1 + ffn_sum).astype(jnp.bfloat16))
        d_hidden = jnp.einsum("rd,fd->rf", cot_rows, wdown_full, preferred_element_type=jnp.float32)
        grad_down = jnp.einsum("rf,rd->fd", hidden, cot_rows, preferred_element_type=jnp.float32)
        d_up = (d_hidden * gate_act).astype(jnp.bfloat16)
        d_gate = (d_hidden * up_pre * gate_sig * (1.0 + gate_pre * (1.0 - gate_sig))).astype(
            jnp.bfloat16
        )
        grad_gate = jnp.einsum("rd,rf->df", ffn_in, d_gate, preferred_element_type=jnp.float32)
        grad_up = jnp.einsum("rd,rf->df", ffn_in, d_up, preferred_element_type=jnp.float32)
        ffn_term = jnp.einsum(
            "rf,df->rd", d_gate, wgate_full, preferred_element_type=jnp.float32
        ) + jnp.einsum("rf,df->rd", d_up, wup_full, preferred_element_type=jnp.float32)
        d_xn2 = lax.psum_scatter(
            ffn_term.astype(jnp.bfloat16), "mp", scatter_dimension=0, tiled=True
        ).astype(jnp.float32)
        gain_ffn = gain_ffn + jnp.sum(d_xn2 * normed2, axis=0)
        d_hidden1 = cot_live + norm_back(d_xn2, normed2, scale2, ffn_norm_gain)
        d_attn = lax.all_gather(d_hidden1.astype(jnp.bfloat16), "head", axis=0, tiled=True)
        d_gated = jnp.einsum(
            "rd,cd->rc", d_attn, wo_full, preferred_element_type=jnp.float32
        ).reshape(n_query, q_heads, head_dim)
        grad_out = jnp.einsum("rc,rd->cd", gated, d_attn, preferred_element_type=jnp.float32)
        d_out_low = (d_gated * gate_prob[..., None]).astype(jnp.bfloat16)
        d_gate_logit = (
            jnp.sum(d_gated * attn_heads, axis=-1) * gate_prob * (1.0 - gate_prob)
        ).astype(jnp.bfloat16)
        grad_headgate = jnp.einsum(
            "rd,rc->dc", gathered_rows, d_gate_logit, preferred_element_type=jnp.float32
        )
        d_out_group = d_out_low.reshape(n_query, kv_heads, group_size, head_dim)
        delta = jnp.transpose(jnp.sum(d_out_group.astype(jnp.float32) * attn_o, axis=-1), (1, 2, 0))
        d_query, d_key_all, d_value_all = attend_backward(
            q_group,
            all_keys,
            all_values,
            query_pos,
            key_pos,
            live_count,
            key_block,
            log_total,
            d_out_group,
            delta,
        )
        d_key_own, d_value_own = (
            lax.psum_scatter(
                d_key_all.astype(jnp.bfloat16), "mp", scatter_dimension=0, tiled=True
            ).astype(jnp.float32),
            lax.psum_scatter(
                d_value_all.astype(jnp.bfloat16), "mp", scatter_dimension=0, tiled=True
            ).astype(jnp.float32),
        )
        dq_norm = rotate_back(
            (d_query * q_scale).reshape(n_query, q_heads, head_dim), rope_cos, rope_sin
        )
        gain_query = gain_query + jnp.sum(dq_norm * q_hat, axis=(0, 1))
        d_q_raw = (
            norm_back(dq_norm, q_hat, q_rms, q_norm_gain)
            .reshape(n_query, q_heads * head_dim)
            .astype(jnp.bfloat16)
        )
        dk_norm = rotate_back(d_key_own.reshape(n_query, kv_heads, head_dim), rope_cos, rope_sin)
        gain_key = gain_key + jnp.sum(dk_norm * k_hat, axis=(0, 1))
        d_k_raw = (
            norm_back(dk_norm, k_hat, k_rms, k_norm_gain)
            .reshape(n_query, kv_heads * head_dim)
            .astype(jnp.bfloat16)
        )
        d_value_low = d_value_own.astype(jnp.bfloat16)
        grad_query = jnp.einsum(
            "rd,rc->dc", gathered_rows, d_q_raw, preferred_element_type=jnp.float32
        )
        grad_key = jnp.einsum(
            "rd,rc->dc", gathered_rows, d_k_raw, preferred_element_type=jnp.float32
        )
        grad_value = jnp.einsum(
            "rd,rc->dc", gathered_rows, d_value_low, preferred_element_type=jnp.float32
        )
        attn_term = jnp.einsum("rc,dc->rd", d_q_raw, wq_full, preferred_element_type=jnp.float32)
        attn_term = attn_term + jnp.einsum(
            "rc,dc->rd", d_k_raw, wk_full, preferred_element_type=jnp.float32
        )
        attn_term = attn_term + jnp.einsum(
            "rc,dc->rd", d_value_low, wv_full, preferred_element_type=jnp.float32
        )
        attn_term = attn_term + jnp.einsum(
            "rc,dc->rd", d_gate_logit, wg_full, preferred_element_type=jnp.float32
        )
        d_xn1 = lax.psum_scatter(
            attn_term.astype(jnp.bfloat16), "head", scatter_dimension=0, tiled=True
        ).astype(jnp.float32)
        gain_attn = gain_attn + jnp.sum(d_xn1 * normed1, axis=0)
        input_grads.append(
            (d_hidden1 + norm_back(d_xn1, normed1, scale1, attn_norm_gain)).astype(jnp.bfloat16)
        )
        batch_grads = reduce_grads(
            grad_query, grad_key, grad_value, grad_headgate, grad_out, grad_gate, grad_up, grad_down
        )
        if grad_total is None:
            grad_total = batch_grads
        else:
            grad_total = tuple((a + b for a, b in zip(grad_total, batch_grads)))
    sum_attn, sum_query, sum_key, sum_ffn = lax.psum(
        (gain_attn, gain_query, gain_key, gain_ffn), ("dp", "head", "mp")
    )
    return (
        jnp.stack(outputs),
        jnp.stack(input_grads),
        sum_attn,
        sum_query,
        sum_key,
        grad_total[0],
        grad_total[1],
        grad_total[2],
        grad_total[3],
        grad_total[4],
        sum_ffn,
        grad_total[5],
        grad_total[6],
        grad_total[7],
    )


PLANE = ("head", "mp")
BIT_X, BIT_C, BIT_Y = 1, 2, 4
NT = (((1,), (1,)), ((), ()))
NN = (((1,), (0,)), ((), ()))
TN = (((0,), (0,)), ((), ()))
F32 = jnp.float32
BF16 = jnp.bfloat16
COST_SHARE = 0.2
LATE_SHARE = 0.1


def dot(left, right, dims=NN):
    return lax.dot_general(left, right, dims, preferred_element_type=F32)


def swap(values, bits):
    return lax.ppermute(values, PLANE, [(i, i ^ bits) for i in range(8)])


def swap_mixed(values, core0, core1):
    return lax.ppermute(
        values, PLANE, [(i, i ^ (core1 if i & BIT_C else core0)) for i in range(8)]
    )


class Order:
    def __init__(self):
        self.ahead = []
        self.last = None

    def need(self, *values):
        self.ahead.extend(values)

    def pin(self, value):
        if self.last is None:
            return value
        return lax.optimization_barrier((value, self.last))[0]

    def run(self, op, *operands):
        if self.ahead:
            operands = lax.optimization_barrier((tuple(operands), tuple(self.ahead)))[0]
        out = op(*operands)
        self.last = out[0] if isinstance(out, (tuple, list)) else out
        self.ahead = [self.last]
        return out


class Gather:
    def __init__(self, order, rows):
        self.order = order
        self.rows = rows
        self.came = swap_mixed(rows, BIT_X, BIT_Y)

    def second(self):
        came = self.order.pin(self.came)
        near = jnp.concatenate([self.rows, came], axis=0)
        self.came = swap_mixed(near, BIT_Y, BIT_X)
        self.pieces = [near, None, swap(near, BIT_C), None]
        return near

    def third(self):
        far = self.order.pin(self.came)
        self.pieces[1], self.pieces[3] = far, swap(far, BIT_C)
        return far


def add_pieces_kernel(*refs):
    for k in range(2):
        refs[4 + k][...] = (refs[k][...].astype(F32) + refs[2 + k][...].astype(F32)).astype(BF16)


def add_pieces(near, far, near_came, far_came):
    count, width = near.shape
    block = pl.BlockSpec((count // 4, width), lambda i: (i, 0))
    return pl.pallas_call(
        add_pieces_kernel,
        grid=(4,),
        in_specs=[block] * 4,
        out_specs=[block] * 2,
        out_shape=[jax.ShapeDtypeStruct((count, width), BF16)] * 2,
        cost_estimate=pl.CostEstimate(
            flops=2 * count * width, bytes_accessed=12 * count * width, transcendentals=0
        ),
        name="add_pieces",
    )(near, far, near_came, far_came)


class Scatter:
    def __init__(self, order, near, far):
        self.order = order
        self.came = (swap(near, BIT_C), swap(far, BIT_C))

    def add(self, near, far):
        near_came, far_came = self.order.pin(self.came)
        self.near, self.far = add_pieces(near, far, near_came, far_came)
        return (self.near, self.far)

    def send_far(self):
        self.came = swap_mixed(self.order.pin(self.far), BIT_Y, BIT_X)

    def take(self):
        came = self.order.pin(self.came)
        half = came.shape[0] // 2
        self.sent = (self.near[half:].astype(F32) + came[half:].astype(F32)).astype(BF16)
        self.kept = self.near[:half].astype(F32) + came[:half].astype(F32)
        return self.sent

    def send_near(self):
        self.came = swap_mixed(self.order.pin(self.sent), BIT_X, BIT_Y)

    def result(self):
        return self.kept + self.order.pin(self.came).astype(F32)


def norm_rope(raw, gain, cosine, sine):
    scale_rows = lax.rsqrt(jnp.mean(raw * raw, axis=-1, keepdims=True) + EPS)
    hat = raw * scale_rows
    turned = hat * gain
    return (turned * cosine + pltpu.roll(turned, 64, 1) * sine, hat, scale_rows)


def norm_rope_back(grad, hat, scale_rows, gain, cosine, sine):
    grad_n = grad * cosine - pltpu.roll(grad, 64, 1) * sine
    gain_part = jnp.sum(grad_n * hat, axis=0, keepdims=True)
    scaled = grad_n * gain
    raw = scale_rows * (scaled - hat * jnp.mean(scaled * hat, axis=-1, keepdims=True))
    return (raw, gain_part)


def two_lanes(first, second, shape):
    lane = lax.broadcasted_iota(jnp.int32, shape, 1)
    return jnp.where(lane == 0, first, jnp.where(lane == 1, second, 0.0))


def cost(flops, traffic, transcendentals=0, share=COST_SHARE):
    return pl.CostEstimate(
        flops=int(flops / share),
        bytes_accessed=int(traffic / share),
        transcendentals=int(transcendentals / share),
    )


SLOT, LIVE, BLOCK, PLACE = 0, 8, 9, 41


def attend_table(plane_idx, core, live_count):
    slot = jnp.arange(8, dtype=jnp.int32)
    across, low, high = slot >> 2, slot & 1, (slot >> 1) & 1
    x_first = (core ^ across) == 0
    apart = across * 2 + jnp.where(x_first, low + 4 * high, high + 4 * low)
    place = apart ^ plane_idx
    slots = jnp.sum(jnp.where(place[None, :] == slot[:, None], slot[None, :], 0), axis=1)
    steps = jnp.arange(8, dtype=jnp.int32)
    blocks = []
    for piece in range(4):
        one, two = place[2 * piece], place[2 * piece + 1]
        first = jnp.where(one < two, 0, 1)
        blocks.append(jnp.where(steps >= jnp.maximum(one, two), 1 - first, first))
    return jnp.concatenate([slots, live_count[None]] + blocks + [place]).astype(jnp.int32)


def take_piece(slot, pieces):
    near = jnp.where(slot < 2, pieces[0][...], pieces[1][...])
    far = jnp.where(slot < 6, pieces[2][...], pieces[3][...])
    return jnp.where(slot < 4, near, far)


def walk_tiles(step, rows, live, add_tile):
    pairs = step // 2
    whole = jnp.minimum(pairs, live // (2 * rows))

    def tile(index, carry):
        add_tile(pl.multiple_of(index * 2 * rows, 2 * rows), 2 * rows, False)
        return carry

    lax.fori_loop(0, whole, tile, 0)
    odd = step % 2 == 1
    edge = pl.multiple_of(pairs * 2 * rows, 2 * rows)

    @pl.when((whole < pairs) & (whole * 2 * rows < live))
    def _():
        add_tile(pl.multiple_of(whole * 2 * rows, 2 * rows), 2 * rows, True)

    @pl.when(odd & (edge < live))
    def _():
        add_tile(edge, 2 * rows, True)

    @pl.when(jnp.logical_not(odd) & (edge < live))
    def _():
        add_tile(edge, rows, True)


def attend_forward_kernel(table, *refs):
    x_pieces, (weights, cosine, sine, q_gain, k_gain) = refs[:4], refs[4:9]
    proj, attn_o, lse, gated = refs[9:13]
    out_pieces, (keys, values, acc) = refs[13:17], refs[17:]
    step = pl.program_id(0)
    rows = proj.shape[0]
    live, slot = table[LIVE], table[SLOT + step]
    cos_b, sin_b = cosine[...], sine[...]
    here = pl.multiple_of(step * rows, rows)
    proj[...] = dot(take_piece(slot, x_pieces), weights[:, 0:640])
    key, _, _ = norm_rope(proj[:, 256:384], k_gain[...], cos_b, sin_b)
    keys[pl.ds(here, rows), :] = key.astype(BF16)
    values[pl.ds(here, rows), 0:128] = proj[:, 384:512].astype(BF16)
    values[pl.ds(here, rows), 128:256] = jnp.ones((rows, 128), BF16)
    q_scale = 128**-0.5
    first, _, _ = norm_rope(proj[:, 0:128], q_gain[...], cos_b, sin_b)
    second, _, _ = norm_rope(proj[:, 128:256], q_gain[...], cos_b, sin_b)
    query = (jnp.concatenate([first, second], axis=0) * q_scale).astype(BF16)

    def add_tile(there, count, masked):
        weight = jnp.exp(dot(query, keys[pl.ds(there, count), :], NT))
        if masked:
            row = lax.broadcasted_iota(jnp.int32, (2 * rows, count), 0)
            place = there + lax.broadcasted_iota(jnp.int32, (2 * rows, count), 1)
            allowed = (place <= here + jnp.where(row >= rows, row - rows, row)) & (place < live)
            weight = jnp.where(allowed, weight, 0.0)
        acc[...] += dot(weight.astype(BF16), values[pl.ds(there, count), :])

    acc[...] = jnp.zeros_like(acc)
    walk_tiles(step, rows, live, add_tile)
    total = acc[:, 128:129]
    out = acc[:, 0:128] / total
    log_total = jnp.log(total)
    gate0 = jax.nn.sigmoid(proj[:, 512:513])
    gate1 = jax.nn.sigmoid(proj[:, 513:514])
    attn_o[:, 0:128] = out[:rows]
    attn_o[:, 128:256] = out[rows:]
    gated[:, 0:128] = (out[:rows] * gate0).astype(BF16)
    gated[:, 128:256] = (out[rows:] * gate1).astype(BF16)
    lse[...] = two_lanes(log_total[:rows], log_total[rows:], (rows, 128))
    part = dot(gated[...], weights[:, 640:896], NT).astype(BF16)
    for piece in range(4):

        @pl.when(slot // 2 == piece)
        def _():
            out_pieces[piece][...] = part


def attend_backward_kernel(table, *refs):
    d_pieces = refs[:4]
    weights, proj, attn_o, lse, cosine, sine, q_gain, k_gain = refs[4:12]
    d_proj, gain_q, gain_k = refs[12:15]
    back_pieces = refs[15:19]
    keys, keys_t, values, k_raw, d_keys, d_values, d_query, d_held = refs[19:]
    step = pl.program_id(0)
    rows = proj.shape[0]
    live = table[LIVE]
    q_scale = 128**-0.5

    @pl.when(step == 0)
    def _():
        gain_q[...] = jnp.zeros_like(gain_q)
        gain_k[...] = jnp.zeros_like(gain_k)

    @pl.when(step < 8)
    def _():
        here = pl.multiple_of(step * rows, rows)
        slot = table[SLOT + step]
        cos_b, sin_b = cosine[pl.ds(here, rows), :], sine[pl.ds(here, rows), :]
        raw_key = proj[:, 256:384]
        k_raw[pl.ds(here, rows), :] = raw_key
        key, _, _ = norm_rope(raw_key, k_gain[...], cos_b, sin_b)
        key = key.astype(BF16)
        keys[pl.ds(here, rows), :] = key
        keys_t[:, pl.ds(here, rows)] = key.T
        values[pl.ds(here, rows), :] = proj[:, 384:512].astype(BF16)
        d_keys[pl.ds(here, rows), :] = jnp.zeros((rows, 128), F32)
        d_values[pl.ds(here, rows), :] = jnp.zeros((rows, 128), F32)
        d_query[...] = jnp.zeros_like(d_query)
        first, hat0, scale0 = norm_rope(proj[:, 0:128], q_gain[...], cos_b, sin_b)
        second, hat1, scale1 = norm_rope(proj[:, 128:256], q_gain[...], cos_b, sin_b)
        query = (jnp.concatenate([first, second], axis=0) * q_scale).astype(BF16)
        gate0 = jax.nn.sigmoid(proj[:, 512:513])
        gate1 = jax.nn.sigmoid(proj[:, 513:514])
        d_gated = dot(take_piece(slot, d_pieces), weights[:, 640:896])
        dg0, dg1 = d_gated[:, 0:128], d_gated[:, 128:256]
        out0, out1 = attn_o[:, 0:128], attn_o[:, 128:256]
        do0, do1 = (dg0 * gate0).astype(BF16), (dg1 * gate1).astype(BF16)
        logit0 = jnp.sum(dg0 * out0, axis=-1, keepdims=True) * gate0 * (1.0 - gate0)
        logit1 = jnp.sum(dg1 * out1, axis=-1, keepdims=True) * gate1 * (1.0 - gate1)
        d_held[pl.ds(here, rows), 512:640] = two_lanes(logit0, logit1, (rows, 128)).astype(BF16)
        delta0 = jnp.sum(do0.astype(F32) * out0, axis=-1, keepdims=True)
        delta1 = jnp.sum(do1.astype(F32) * out1, axis=-1, keepdims=True)
        delta_t = two_lanes(delta0, delta1, (rows, 128)).T
        delta = jnp.concatenate([delta_t[0:1], delta_t[1:2]], axis=1)
        lse_t = lse[...].T
        log_total = jnp.concatenate([lse_t[0:1], lse_t[1:2]], axis=1)
        d_out = jnp.concatenate([do0, do1], axis=0)

        def add_tile(there, count, masked):
            here_keys = pl.ds(there, count)
            scores = dot(keys[here_keys, :], query, NT)
            probs = jnp.exp(scores - log_total)
            if masked:
                place = there + lax.broadcasted_iota(jnp.int32, (count, 2 * rows), 0)
                q_col = lax.broadcasted_iota(jnp.int32, (count, 2 * rows), 1)
                q_place = here + jnp.where(q_col >= rows, q_col - rows, q_col)
                probs = jnp.where((place <= q_place) & (place < live), probs, 0.0)
            d_probs = dot(values[here_keys, :], d_out, NT)
            d_scores = (probs * (d_probs - delta)).astype(BF16)
            d_values[here_keys, :] += dot(probs.astype(BF16), d_out)
            d_keys[here_keys, :] += dot(d_scores, query)
            d_query[...] += dot(keys_t[:, here_keys], d_scores)

        walk_tiles(step, rows, live, add_tile)
        grads = d_query[...].T * q_scale
        raw0, part0 = norm_rope_back(grads[:rows], hat0, scale0, q_gain[...], cos_b, sin_b)
        raw1, part1 = norm_rope_back(grads[rows:], hat1, scale1, q_gain[...], cos_b, sin_b)
        d_held[pl.ds(here, rows), 0:128] = raw0.astype(BF16)
        d_held[pl.ds(here, rows), 128:256] = raw1.astype(BF16)
        gain_q[0:1, :] += part0 + part1

    @pl.when(step >= 8)
    def _():
        slot = (step - 4) % 8
        there = pl.multiple_of(table[PLACE + slot] * rows, rows)
        cos_k, sin_k = cosine[pl.ds(there, rows), :], sine[pl.ds(there, rows), :]
        _, hat, scale_rows = norm_rope(k_raw[pl.ds(there, rows), :], k_gain[...], cos_k, sin_k)
        raw, part = norm_rope_back(
            d_keys[pl.ds(there, rows), :], hat, scale_rows, k_gain[...], cos_k, sin_k
        )
        gain_k[0:1, :] += part
        d_held[pl.ds(there, rows), 256:384] = raw.astype(BF16)
        d_held[pl.ds(there, rows), 384:512] = d_values[pl.ds(there, rows), :].astype(BF16)
        d_block = d_held[pl.ds(there, rows), :]
        d_proj[...] = d_block
        back = dot(d_block, weights[:, 0:640], NT).astype(BF16)
        for piece in range(4):

            @pl.when(slot // 2 == piece)
            def _():
                back_pieces[piece][...] = back


def attend_forward_call(table, pieces, weights, cosine, sine, q_gain, k_gain):
    seq_len, width = cosine.shape[0], weights.shape[0]
    rows = seq_len // 8
    by_slot = lambda i, t: (t[SLOT + i], 0)
    by_place = lambda i, t: (i, 0)
    fixed = lambda i, t: (0, 0)
    whole = [
        pl.BlockSpec((rows, width), lambda i, t, k=k: (t[BLOCK + 8 * k + i], 0)) for k in range(4)
    ]
    pairs = seq_len * (seq_len + rows)
    return pl.pallas_call(
        attend_forward_kernel,
        grid_spec=pltpu.PrefetchScalarGridSpec(
            num_scalar_prefetch=1,
            grid=(8,),
            in_specs=whole
            + [
                pl.BlockSpec(weights.shape, fixed, pipeline_mode=pl.Buffered(1)),
                pl.BlockSpec((rows, 128), by_place),
                pl.BlockSpec((rows, 128), by_place),
                pl.BlockSpec((1, 128), fixed),
                pl.BlockSpec((1, 128), fixed),
            ],
            out_specs=[
                pl.BlockSpec((rows, 640), by_slot),
                pl.BlockSpec((rows, 256), by_slot),
                pl.BlockSpec((rows, 128), by_slot),
                pl.BlockSpec((rows, 256), by_slot),
            ]
            + whole,
            scratch_shapes=[
                pltpu.VMEM((seq_len, 128), BF16),
                pltpu.VMEM((seq_len, 256), BF16),
                pltpu.VMEM((2 * rows, 256), F32),
            ],
        ),
        out_shape=[
            jax.ShapeDtypeStruct((seq_len, 640), F32),
            jax.ShapeDtypeStruct((seq_len, 256), F32),
            jax.ShapeDtypeStruct((seq_len, 128), F32),
            jax.ShapeDtypeStruct((seq_len, 256), BF16),
        ]
        + [jax.ShapeDtypeStruct((2 * rows, width), BF16)] * 4,
        compiler_params=pltpu.CompilerParams(
            dimension_semantics=("arbitrary",), vmem_limit_bytes=62 << 20
        ),
        cost_estimate=cost(
            2 * seq_len * width * 896 + 4 * pairs * 128, 2 * seq_len * (2 * width + 2200), pairs
        ),
        name="attend_forward",
    )(table, *pieces, weights, cosine, sine, q_gain, k_gain)


def attend_backward_call(table, pieces, weights, proj, attn_o, lse, cosine, sine, q_gain, k_gain):
    seq_len, width = cosine.shape[0], weights.shape[0]
    rows = seq_len // 8
    by_slot = lambda i, t: (t[SLOT + jnp.minimum(i, 7)], 0)
    last_slot = lambda i, t: (jnp.where(i < 8, 4, (i - 4) % 8), 0)
    fixed = lambda i, t: (0, 0)
    pairs = seq_len * (seq_len + rows)
    return pl.pallas_call(
        attend_backward_kernel,
        grid_spec=pltpu.PrefetchScalarGridSpec(
            num_scalar_prefetch=1,
            grid=(16,),
            in_specs=[
                pl.BlockSpec(
                    (rows, width), lambda i, t, k=k: (t[BLOCK + 8 * k + jnp.minimum(i, 7)], 0)
                )
                for k in range(4)
            ]
            + [
                pl.BlockSpec(weights.shape, fixed, pipeline_mode=pl.Buffered(1)),
                pl.BlockSpec((rows, 640), by_slot),
                pl.BlockSpec((rows, 256), by_slot),
                pl.BlockSpec((rows, 128), by_slot),
                pl.BlockSpec((seq_len, 128), fixed, pipeline_mode=pl.Buffered(1)),
                pl.BlockSpec((seq_len, 128), fixed, pipeline_mode=pl.Buffered(1)),
                pl.BlockSpec((1, 128), fixed),
                pl.BlockSpec((1, 128), fixed),
            ],
            out_specs=[
                pl.BlockSpec((rows, 640), last_slot),
                pl.BlockSpec((8, 128), fixed),
                pl.BlockSpec((8, 128), fixed),
            ]
            + [
                pl.BlockSpec(
                    (rows, width), lambda i, t, k=k: (jnp.clip(i - 8 - (2 * k + 4) % 8, 0, 1), 0)
                )
                for k in range(4)
            ],
            scratch_shapes=[
                pltpu.VMEM((seq_len, 128), BF16),
                pltpu.VMEM((128, seq_len), BF16),
                pltpu.VMEM((seq_len, 128), BF16),
                pltpu.VMEM((seq_len, 128), F32),
                pltpu.VMEM((seq_len, 128), F32),
                pltpu.VMEM((seq_len, 128), F32),
                pltpu.VMEM((128, 2 * rows), F32),
                pltpu.VMEM((seq_len, 640), BF16),
            ],
        ),
        out_shape=[
            jax.ShapeDtypeStruct((seq_len, 640), BF16),
            jax.ShapeDtypeStruct((8, 128), F32),
            jax.ShapeDtypeStruct((8, 128), F32),
        ]
        + [jax.ShapeDtypeStruct((2 * rows, width), BF16)] * 4,
        compiler_params=pltpu.CompilerParams(
            dimension_semantics=("arbitrary",), vmem_limit_bytes=62 << 20
        ),
        cost_estimate=cost(
            2 * seq_len * width * 896 + 10 * pairs * 128,
            2 * seq_len * (2 * width + 2200),
            pairs,
            LATE_SHARE,
        ),
        name="attend_backward",
    )(table, *pieces, weights, proj, attn_o, lse, cosine, sine, q_gain, k_gain)


def feed_forward_kernel(*refs):
    rows_near, rows_far, cot_near, cot_far, w_down_t, w_inner = refs[:6]
    hidden_out, d_pre_out, down_near, down_far, back_near, back_far = refs[-6:]
    near = pl.program_id(0) < 2
    units = hidden_out.shape[1]
    pre = dot(jnp.where(near, rows_near[...], rows_far[...]), w_inner[...])
    d_hidden = dot(jnp.where(near, cot_near[...], cot_far[...]), w_down_t[...])
    gate_pre, up_pre = pre[:, :units], pre[:, units:]
    gate_sig = jax.nn.sigmoid(gate_pre)
    gate_act = gate_pre * gate_sig
    hidden_out[...] = (gate_act * up_pre).astype(BF16)
    d_pre_out[:, units:] = (d_hidden * gate_act).astype(BF16)
    d_pre_out[:, :units] = (
        d_hidden * up_pre * gate_sig * (1.0 + gate_pre * (1.0 - gate_sig))
    ).astype(BF16)
    back = dot(d_pre_out[...], w_inner[...], NT)
    down = dot(hidden_out[...], w_down_t[...], NT)

    @pl.when(near)
    def _():
        back_near[...] = back.astype(BF16)
        down_near[...] = down.astype(BF16)

    @pl.when(jnp.logical_not(near))
    def _():
        back_far[...] = back.astype(BF16)
        down_far[...] = down.astype(BF16)


def feed_forward_call(rows, cots, w_down_t, w_inner):
    count, width = rows[0].shape
    units = w_down_t.shape[1]
    tile = count // 2
    by_row = lambda i: (i, 0)
    fixed = lambda i: (0, 0)
    near = pl.BlockSpec((tile, width), lambda i: (jnp.minimum(i, 1), 0))
    far = pl.BlockSpec((tile, width), lambda i: (jnp.maximum(i - 2, 0), 0))
    wide = jax.ShapeDtypeStruct((count, width), BF16)
    out = pl.pallas_call(
        feed_forward_kernel,
        grid=(4,),
        in_specs=[near, far, near, far]
        + [pl.BlockSpec(w.shape, fixed, pipeline_mode=pl.Buffered(1)) for w in (w_down_t, w_inner)],
        out_specs=[
            pl.BlockSpec((tile, units), by_row),
            pl.BlockSpec((tile, 2 * units), by_row),
            near,
            far,
            near,
            far,
        ],
        out_shape=[
            jax.ShapeDtypeStruct((2 * count, units), BF16),
            jax.ShapeDtypeStruct((2 * count, 2 * units), BF16),
            wide,
            wide,
            wide,
            wide,
        ],
        compiler_params=pltpu.CompilerParams(
            dimension_semantics=("arbitrary",), vmem_limit_bytes=52 << 20
        ),
        cost_estimate=cost(24 * count * width * units, 2 * width * (8 * count + 3 * units)),
        name="feed_forward",
    )(*rows, *cots, w_down_t, w_inner)
    return (out[0], out[1], (out[2], out[3]), (out[4], out[5]))


def weight_grad_call(n_parts, lefts, terms, weights=None, carried=None, final=True):
    n_pieces = len(lefts[0])
    rows, width = lefts[0][0].shape
    columns = [pieces[0][0].shape[1] for _, pieces in terms]
    starts = [sum(columns[:k]) for k in range(len(terms))]
    total = sum(columns)
    arrays, place = ([], {})
    for _, pieces in terms:
        for array, _ in pieces:
            if id(array) not in place:
                place[id(array)] = len(arrays)
                arrays.append(array)
    n_left, n_terms = len(lefts), len(terms)

    def kernel(*refs):
        left_refs = refs[: n_left * n_pieces]
        right_refs = refs[len(left_refs) : len(left_refs) + len(arrays)]
        rest = list(refs[len(left_refs) + len(arrays) :])
        if weights is not None:
            weights_ref = rest.pop(0)
        if carried is not None:
            carried_ref = rest.pop(0)
        out = rest.pop(0)
        if weights is not None:
            gain = rest.pop(0)
        left_buf, right_buf = rest[:n_left], rest[n_left : n_left + n_terms]
        accs, sems = rest[n_left + n_terms : -1], rest[-1]

        def copies(piece, slot):
            made = [
                pltpu.make_async_copy(
                    left_refs[k * n_pieces + piece], left_buf[k].at[slot], sems.at[slot, k]
                )
                for k in range(n_left)
            ]
            for k, (_, pieces) in enumerate(terms):
                array, first = pieces[piece]
                made.append(
                    pltpu.make_async_copy(
                        right_refs[place[id(array)]].at[pl.ds(first, rows)],
                        right_buf[k].at[slot],
                        sems.at[slot, n_left + k],
                    )
                )
            return made

        for copy in copies(0, 0):
            copy.start()
        if not final:
            accs = [out]
        for acc in accs:
            acc[...] = jnp.zeros_like(acc) if carried is None else carried_ref[...]

        def body(index, carry):
            slot = lax.rem(index, 2)
            for piece in range(1, n_pieces):

                @pl.when(index + 1 == piece)
                def _():
                    for copy in copies(piece, piece % 2):
                        copy.start()

            for copy in copies(0, slot):
                copy.wait()
            for k, (left, _) in enumerate(terms):
                for first in range(0, columns[k], 256):
                    some = slice(first, min(first + 256, columns[k]))
                    accs[k][some, :] += dot(right_buf[k][slot, :, some], left_buf[left][slot], TN)
            return carry

        lax.fori_loop(0, n_pieces, body, 0)
        if not final:
            return
        part = width // n_parts
        for p in range(n_parts):
            for k in range(n_terms):
                start = p * total + starts[k]
                out[start : start + columns[k], :] = accs[k][:, p * part : (p + 1) * part].astype(
                    BF16
                )
        if weights is not None:
            scaled = accs[0][...] * weights_ref[:, : columns[0]].T.astype(F32)
            gain[...] = jnp.broadcast_to(jnp.sum(scaled, axis=0, keepdims=True), gain.shape)

    out_shape = [jax.ShapeDtypeStruct((n_parts * total, width // n_parts), BF16)]
    if not final:
        out_shape = [jax.ShapeDtypeStruct((total, width), F32)]
    vmem = pl.BlockSpec(memory_space=pltpu.VMEM)
    operands = [piece for pieces in lefts for piece in pieces] + arrays
    in_specs = [pl.BlockSpec(memory_space=pl.ANY)] * len(operands)
    if weights is not None:
        operands.append(weights)
        in_specs.append(vmem)
        out_shape.append(jax.ShapeDtypeStruct((8, width), F32))
    if carried is not None:
        operands.append(carried)
        in_specs.append(vmem)
    return pl.pallas_call(
        kernel,
        in_specs=in_specs,
        out_specs=[vmem] * len(out_shape),
        out_shape=out_shape,
        scratch_shapes=[pltpu.VMEM((2, rows, width), BF16)] * n_left
        + [pltpu.VMEM((2, rows, c), BF16) for c in columns]
        + [pltpu.VMEM((c, width), F32) for c in columns if final]
        + [pltpu.SemaphoreType.DMA((2, n_left + n_terms))],
        compiler_params=pltpu.CompilerParams(vmem_limit_bytes=56 << 20),
        cost_estimate=cost(
            2 * n_pieces * rows * width * total,
            2 * n_pieces * rows * (n_left * width + total) + 2 * width * total,
            0,
            LATE_SHARE,
        ),
        name="weight_grad",
    )(*operands)


def pack_attention_kernel(index, query, key, value, headgate, out, packed):
    half = pl.program_id(0) ^ index[0]
    packed[0, :, 0:256] = query[...]
    packed[0, :, 256:384] = key[...]
    packed[0, :, 384:512] = value[...]
    gates = headgate[...].astype(F32)
    first = jnp.where(half == 0, gates[:, 0:1], gates[:, 2:3])
    second = jnp.where(half == 0, gates[:, 1:2], gates[:, 3:4])
    packed[0, :, 512:640] = two_lanes(first, second, (packed.shape[1], 128)).astype(BF16)
    packed[0, :, 640:896] = out[...].T


def pack_attention(index, query, key, value, headgate, out):
    rows = query.shape[0]
    half = lambda i, t: (0, i ^ t[0])
    return pl.pallas_call(
        pack_attention_kernel,
        grid_spec=pltpu.PrefetchScalarGridSpec(
            num_scalar_prefetch=1,
            grid=(2,),
            in_specs=[
                pl.BlockSpec((rows, 256), half),
                pl.BlockSpec((rows, 128), half),
                pl.BlockSpec((rows, 128), half),
                pl.BlockSpec(headgate.shape, lambda i, t: (0, 0)),
                pl.BlockSpec((256, out.shape[1]), lambda i, t: (i ^ t[0], 0)),
            ],
            out_specs=pl.BlockSpec((1, rows, 896), lambda i, t: (i, 0, 0)),
        ),
        out_shape=jax.ShapeDtypeStruct((2, rows, 896), BF16),
        cost_estimate=cost(0, 4 * rows * 896 * 2),
        name="pack_attention",
    )(index, query, key, value, headgate, out)


def unpack_attention_kernel(index, kept, came, out_kept, out_came, query, key, value, headgate, out):
    flip = index[0] == 1

    def ordered(mine, other):
        return [
            jnp.where(flip, other[...], mine[...]).astype(F32),
            jnp.where(flip, mine[...], other[...]).astype(F32),
        ]

    for k, part in enumerate(ordered(kept, came)):
        query[:, 256 * k : 256 * k + 256] = part[0:256].T
        key[:, 128 * k : 128 * k + 128] = part[256:384].T
        value[:, 128 * k : 128 * k + 128] = part[384:512].T
        headgate[:, 2 * k : 2 * k + 2] = part[512:640].T[:, 0:2]
    for k, part in enumerate(ordered(out_kept, out_came)):
        out[256 * k : 256 * k + 256, :] = part


def unpack_attention(index, kept, came, out_kept, out_came):
    rows = kept.shape[1]
    vmem = pl.BlockSpec(memory_space=pltpu.VMEM)
    shapes = [(rows, 512), (rows, 256), (rows, 256), (rows, 4), (512, rows)]
    return pl.pallas_call(
        unpack_attention_kernel,
        in_specs=[pl.BlockSpec(memory_space=pltpu.SMEM)] + [vmem] * 4,
        out_specs=[vmem] * 5,
        out_shape=[jax.ShapeDtypeStruct(shape, F32) for shape in shapes],
        cost_estimate=cost(0, 8 * rows * 896),
        name="unpack_attention",
    )(index, kept, came, out_kept, out_came)


def pack_feed_forward_kernel(index, gate, up, down, packed):
    units = gate.shape[1]
    packed[0, :, :units] = down[...].T
    packed[0, :, units : 2 * units] = gate[...]
    packed[0, :, 2 * units :] = up[...]


def pack_feed_forward(index, gate, up, down):
    rows, units = gate.shape[0], gate.shape[1] // 4
    quarter = pl.BlockSpec((rows, units), lambda i, t: (0, i ^ t[0]))
    return pl.pallas_call(
        pack_feed_forward_kernel,
        grid_spec=pltpu.PrefetchScalarGridSpec(
            num_scalar_prefetch=1,
            grid=(4,),
            in_specs=[
                quarter,
                quarter,
                pl.BlockSpec((units, rows), lambda i, t: (i ^ t[0], 0)),
            ],
            out_specs=pl.BlockSpec((1, rows, 3 * units), lambda i, t: (i, 0, 0)),
        ),
        out_shape=jax.ShapeDtypeStruct((4, rows, 3 * units), BF16),
        cost_estimate=cost(0, 8 * rows * units * 6),
        name="pack_feed_forward",
    )(index, gate, up, down)


def unpack_feed_forward_kernel(index, *refs):
    pieces, (gate, up, down) = refs[:8], refs[8:]
    units = gate.shape[1]
    apart = pl.program_id(0) ^ index[0]

    def of_piece(group):
        low = jnp.where(apart == 0, group[0][...], group[1][...])
        high = jnp.where(apart == 2, group[2][...], group[3][...])
        return jnp.where(apart < 2, low, high).astype(F32)

    inner = of_piece(pieces[:4])
    gate[...] = inner[:units].T
    up[...] = inner[units:].T
    down[...] = of_piece(pieces[4:])


def unpack_feed_forward(index, inners, downs):
    units, rows = downs[0].shape
    quarter = pl.BlockSpec((rows, units), lambda i, t: (0, i))
    whole = [pl.BlockSpec(v.shape, lambda i, t: (0, 0)) for v in (*inners, *downs)]
    wide = jax.ShapeDtypeStruct((rows, 4 * units), F32)
    return pl.pallas_call(
        unpack_feed_forward_kernel,
        grid_spec=pltpu.PrefetchScalarGridSpec(
            num_scalar_prefetch=1,
            grid=(4,),
            in_specs=whole,
            out_specs=[quarter, quarter, pl.BlockSpec((units, rows), lambda i, t: (i, 0))],
        ),
        out_shape=[wide, wide, jax.ShapeDtypeStruct((4 * units, rows), F32)],
        cost_estimate=cost(0, 24 * rows * units * 4),
        name="unpack_feed_forward",
    )(index, *inners, *downs)


def pick(flag, first, second):
    return jnp.where(flag, first, second)


def reorder_by(pieces, index):
    low, high = (index & 1) == 1, (index & 2) == 2
    swapped = [pick(low, pieces[j ^ 1], pieces[j]) for j in range(4)]
    return [pick(high, swapped[j ^ 2], swapped[j]) for j in range(4)]


def local_plane(
    inputs,
    cotangent,
    seq_counts,
    seq_bucket,
    attn_norm_gain,
    q_norm_gain,
    k_norm_gain,
    w_query,
    w_key,
    w_value,
    w_headgate,
    w_out,
    ffn_norm_gain,
    w_gate,
    w_up,
    w_down,
):
    micro_batches, row_count, model_width = inputs.shape
    both = range(micro_batches)
    n_dp = lax.axis_size("dp")
    head_idx = lax.axis_index("head")
    mp_idx = lax.axis_index("mp")
    dp_idx = lax.axis_index("dp")
    core = head_idx & 1
    plane_idx = head_idx * 2 + mp_idx
    seq_len = row_count * 8
    units = w_gate.shape[1] // 4
    head_at = head_idx[None].astype(jnp.int32)
    mp_at = mp_idx[None].astype(jnp.int32)
    order = Order()

    def after(value, *ahead):
        return lax.optimization_barrier((value, ahead))[0]

    halves = pack_attention(mp_at, w_query, w_key, w_value, w_headgate, w_out)
    attn_came = swap(halves[1], BIT_X)

    slot_ids = jnp.arange(micro_batches * n_dp, dtype=jnp.int32)
    slot_count = jnp.sum(
        jnp.where(seq_bucket[None, :] == slot_ids[:, None], seq_counts[None, :], 0), axis=1
    )
    own_pos = plane_idx * row_count + jnp.arange(row_count, dtype=jnp.int32)
    live = [slot_count[n * n_dp + dp_idx] for n in both]
    x_float = [inputs[n].astype(F32) for n in both]
    scale1 = [rms_scale(x) for x in x_float]
    normed1 = [x * scale for x, scale in zip(x_float, scale1)]
    xn1_own = [(n * attn_norm_gain).astype(BF16) for n in normed1]
    cot_live = [
        cotangent[n].astype(F32) * (own_pos < live[n]).astype(F32)[:, None] for n in both
    ]
    cot_own = [c.astype(BF16) for c in cot_live]
    xn1, xn2, cot, d_attn = ([None] * micro_batches for _ in range(4))
    xn1[0] = Gather(order, xn1_own[0])
    is_first = mp_idx == 0
    attn_rows = jnp.concatenate(
        [pick(is_first, halves[0], attn_came), pick(is_first, attn_came, halves[0])], axis=0
    )
    attn_rows = after(attn_rows, xn1[0].came)
    w_attn = lax.all_gather(attn_rows, "dp", axis=0, tiled=True)
    xn1[0].second()
    xn1[0].third()

    quarters = after(pack_feed_forward(head_at, w_gate, w_up, w_down), xn1[0].pieces[1])
    traded = [quarters[0]] + [swap(quarters[r], r * 2) for r in (1, 2, 3)]
    parts = [[t[:, :units] for t in traded], [t[:, units:] for t in traded]]
    ffn_rows = [jnp.concatenate(reorder_by(part, head_idx), axis=0) for part in parts]
    ffn_rows = after(tuple(ffn_rows), attn_rows)
    w_ffn = [lax.all_gather(rows, "dp", axis=0, tiled=True) for rows in ffn_rows]

    xn1[1] = Gather(order, after(xn1_own[1], xn1[0].pieces[1]))
    tables = [attend_table(plane_idx, core, count) for count in live]
    table_cos, table_sin = rope_tables(jnp.arange(seq_len, dtype=jnp.int32), 64)
    table_cos, table_sin = table_cos[:, 0, :], table_sin[:, 0, :]
    cosine = jnp.concatenate([table_cos, table_cos], axis=1)
    sine = jnp.concatenate([-table_sin, table_sin], axis=1)
    fixed = (cosine, sine, q_norm_gain[None, :], k_norm_gain[None, :])
    att, out_sum = ([None] * micro_batches for _ in range(2))

    def attend(n):
        att[n] = order.run(
            lambda *pieces: attend_forward_call(tables[n], pieces, w_attn, *fixed), *xn1[n].pieces
        )

    order.need(xn1[1].second())
    cot[0] = Gather(order, after(cot_own[0], xn1[1].pieces[0]))
    attend(0)
    done = (xn1[1].third(), cot[0].second())
    out_sum[0] = Scatter(order, *after((att[0][6], att[0][7]), *done))
    order.need(*out_sum[0].add(att[0][4], att[0][5]), *done, w_ffn[0])
    out_sum[0].send_far()
    attend(1)
    done = (out_sum[0].take(), cot[0].third())
    out_sum[0].send_near()
    out_sum[1] = Scatter(order, *after((att[1][6], att[1][7]), *done))
    order.need(*done)

    hidden1, scale2, normed2 = ([None] * micro_batches for _ in range(3))

    def middle(n):
        hidden1[n] = x_float[n] + out_sum[n].result()
        scale2[n] = rms_scale(hidden1[n])
        normed2[n] = hidden1[n] * scale2[n]
        rows = (normed2[n] * ffn_norm_gain).astype(BF16)
        xn2[n] = Gather(order, rows)
        return rows

    rows = middle(0)
    order.need(*out_sum[1].add(after(att[1][4], rows), att[1][5]))
    out_sum[1].send_far()
    order.need(xn2[0].second(), out_sum[1].take())
    out_sum[1].send_near()
    order.need(xn2[0].third(), middle(1))
    cot[1] = Gather(order, after(cot_own[1], xn2[0].pieces[1]))

    feed = {}
    down, back = ([None] * micro_batches for _ in range(2))

    def feed_other(n):
        feed[n, 1] = order.run(
            lambda *v: feed_forward_call(v[0:2], v[2:4], *w_ffn), *xn2[n].pieces[2:], *cot[n].pieces[2:]
        )

    def feed_mine(n):
        feed[n, 0] = order.run(
            lambda *v: feed_forward_call(v[0:2], v[2:4], *w_ffn), *xn2[n].pieces[:2], *cot[n].pieces[:2]
        )
        return back[n].add(*feed[n, 0][3])

    d_hidden1 = [None] * micro_batches
    gain_ffn = []

    def turn(n):
        d_xn2 = back[n].result()
        gain_ffn.append(jnp.sum(d_xn2 * normed2[n], axis=0))
        d_hidden1[n] = cot_live[n] + norm_back(d_xn2, normed2[n], scale2[n], ffn_norm_gain)
        rows = d_hidden1[n].astype(BF16)
        d_attn[n] = Gather(order, rows)
        return rows

    def row_pieces(array):
        count = array.shape[0] // (2 * row_count)
        return [(array, 2 * row_count * k) for k in range(count)]

    def of_feed(which):
        return [p for n in both for side in (0, 1) for p in row_pieces(feed[n, side][which])]

    def rows_of(gathers):
        return [piece for gather in gathers for piece in gather.pieces]

    def grad_call(lefts, terms, *more):
        count = [len(left) for left in lefts]
        return order.run(
            lambda *v: weight_grad_call(
                n_dp,
                [list(v[sum(count[:k]) : sum(count[: k + 1])]) for k in range(len(lefts))],
                terms,
                *more,
            ),
            *[piece for left in lefts for piece in left],
        )

    def sum_over_dp(values):
        return lax.psum_scatter(values, "dp", scatter_dimension=0, tiled=True)

    def quarters_of(values):
        width = values.shape[1] // 4
        quarter = lambda k: lax.dynamic_slice_in_dim(values, k * width, width, 1)
        return [quarter(head_idx)] + [swap(quarter(head_idx ^ r), r * 2) for r in (1, 2, 3)]

    feed_other(0)
    done = (xn2[1].second(), cot[1].second())
    back[0] = Scatter(order, *after(feed[0, 1][3], *done))
    order.need(*done)
    sums = feed_mine(0)
    done = (xn2[1].third(), cot[1].third())
    down[0] = Scatter(order, *after(feed[0, 1][2], *done, *sums))
    back[0].send_far()
    order.need(*sums, *done)
    feed_other(1)
    done = (back[0].take(), *down[0].add(*feed[0, 0][2]))
    back[0].send_near()
    down[0].send_far()
    back[1] = Scatter(order, *after(feed[1, 1][3], *done))
    order.need(*done)
    order.need(*feed_mine(1), turn(0), down[0].take())
    back[1].send_far()
    grad_inner = grad_call([rows_of(xn2)], [(0, of_feed(1))])[0]
    done = (d_attn[0].second(), back[1].take())
    back[1].send_near()
    down[1] = Scatter(order, *after(feed[1, 1][2], *done))
    order.need(*done)
    grad_down = grad_call([rows_of(cot)], [(0, of_feed(0))])[0]
    grads_inner = sum_over_dp(order.pin(grad_inner))
    order.need(d_attn[0].third(), turn(1), *down[1].add(*feed[1, 0][2]))
    down[0].send_near()
    down[1].send_far()

    d_proj, gain_parts, rows_sum = ([None] * micro_batches for _ in range(3))

    def attend_back(n):
        out = order.run(
            lambda *v: attend_backward_call(
                tables[n], v, w_attn, att[n][0], att[n][1], att[n][2], *fixed
            ),
            *d_attn[n].pieces,
        )
        d_proj[n] = out[0]
        gain_parts[n] = (out[1][0], out[2][0])
        return out

    def finish(n):
        d_xn1 = rows_sum[n].result()
        return (d_hidden1[n] + norm_back(d_xn1, normed1[n], scale1[n], attn_norm_gain)).astype(BF16)

    outputs, input_grads = ([None] * micro_batches for _ in range(2))
    back_0 = attend_back(0)
    grads_down = sum_over_dp(order.pin(grad_down))
    done = (d_attn[1].second(), down[1].take())
    outputs[0] = (hidden1[0] + down[0].result()).astype(BF16)
    rows_sum[0] = Scatter(order, *after((back_0[5], back_0[6]), *done, outputs[0]))
    order.need(*done, outputs[0], *rows_sum[0].add(back_0[3], back_0[4]))
    grads_proj = grad_call([xn1[0].pieces], [(0, row_pieces(d_proj[0]))], None, None, False)[0]
    order.need(d_attn[1].third())
    grads_out = sum_over_dp(
        grad_call(
            [rows_of(d_attn)], [(0, [p for n in both for p in row_pieces(att[n][3])])]
        )[0]
    )
    rows_sum[0].send_far()
    down[1].send_near()
    inner_quarters = quarters_of(order.pin(grads_inner))
    order.need(grads_inner)
    back_1 = attend_back(1)
    done = (rows_sum[0].take(), *inner_quarters)
    rows_sum[0].send_near()
    rows_sum[1] = Scatter(order, *after((back_1[5], back_1[6]), *done))
    down_quarters = quarters_of(order.pin(grads_down))
    order.need(*done, grads_down)
    grads_proj, gain_rows = grad_call(
        [xn1[1].pieces], [(0, row_pieces(d_proj[1]))], w_attn, grads_proj
    )
    grads_proj = sum_over_dp(grads_proj)
    outputs[1] = (hidden1[1] + down[1].result()).astype(BF16)
    input_grads[0] = finish(0)
    order.need(*rows_sum[1].add(*after((back_1[3], back_1[4]), outputs[1], input_grads[0])))
    rows_sum[1].send_far()
    order.need(*down_quarters)
    grad_gate, grad_up, grad_down = order.run(
        lambda *v: unpack_feed_forward(head_at, v[:4], v[4:]), *inner_quarters, *down_quarters
    )
    rows_sum[1].take()
    rows_sum[1].send_near()
    input_grads[1] = finish(1)

    gains = jnp.concatenate(
        [gain_rows[0] / attn_norm_gain, gain_ffn[0] + gain_ffn[1]]
        + [gain_parts[0][k] + gain_parts[1][k] for k in range(2)]
    ).reshape(-1, 128)
    gains = gains + swap(gains, BIT_C)
    for step in (1, 2):
        gains = gains + lax.ppermute(gains, "dp", [(i, i ^ step) for i in range(4)])
    gains = after(gains, rows_sum[1].sent)
    for bits in (BIT_X, BIT_Y):
        gains = gains + swap(gains, bits)
    gains = gains.reshape(-1)
    sum_attn, sum_gain_ffn = gains[:model_width], gains[model_width : 2 * model_width]
    sum_query, sum_key = gains[-256:-128], gains[-128:]

    def halves_of(values):
        left, right = values[:, :row_count], values[:, row_count:]
        return pick(is_first, left, right), swap(pick(is_first, right, left), BIT_X)

    grad_query, grad_key, grad_value, grad_headgate, grad_out = unpack_attention(
        mp_at, *halves_of(grads_proj), *halves_of(grads_out)
    )
    return (
        jnp.stack(outputs),
        jnp.stack(input_grads),
        sum_attn,
        sum_query,
        sum_key,
        grad_query,
        grad_key,
        grad_value,
        grad_headgate,
        grad_out,
        sum_gain_ffn,
        grad_gate,
        grad_up,
        grad_down,
    )


def choose_local(mesh):
    if mesh.shape["head"] == 4 and mesh.shape["mp"] == 2 and mesh.shape["dp"] == 4:
        return local_plane
    return local


def solution(mesh):
    placed = (
        P(None, ("dp", "head", "mp"), None),
        P(None, ("dp", "head", "mp"), None),
        P(),
        P(),
        P(),
        P(),
        P(),
        P(("dp", "mp"), "head"),
        P(("dp", "mp"), "head"),
        P(("dp", "mp"), "head"),
        P(("dp", "mp"), "head"),
        P("head", ("dp", "mp")),
        P(),
        P(("dp", "head"), "mp"),
        P(("dp", "head"), "mp"),
        P("mp", ("dp", "head")),
    )
    return jax.shard_map(
        choose_local(mesh),
        mesh=mesh,
        in_specs=placed,
        out_specs=(
            P(None, ("dp", "head", "mp"), None),
            P(None, ("dp", "head", "mp"), None),
            P(),
            P(),
            P(),
            P(("dp", "mp"), "head"),
            P(("dp", "mp"), "head"),
            P(("dp", "mp"), "head"),
            P(("dp", "mp"), "head"),
            P("head", ("dp", "mp")),
            P(),
            P(("dp", "head"), "mp"),
            P(("dp", "head"), "mp"),
            P("mp", ("dp", "head")),
        ),
        check_vma=False,
    )
```

```python
import functools

import jax
import jax.numpy as jnp
from jax import lax
from jax.experimental import pallas as pl
from jax.experimental.pallas import tpu as pltpu
from jax.sharding import PartitionSpec as P

EPS = 1e-06
ROPE_BASE = 1000000.0
NEG_FILL = -1e30


def rms_scale(values):
    return lax.rsqrt(jnp.mean(values * values, axis=-1, keepdims=True) + EPS)


def norm_back(grad_out, normed, scale_rows, gain):
    d_normed = grad_out * gain
    return scale_rows * (d_normed - normed * jnp.mean(d_normed * normed, axis=-1, keepdims=True))


def rope_tables(positions, half):
    freq = jnp.power(ROPE_BASE, -jnp.arange(half, dtype=jnp.float32) / half)
    angle = positions.astype(jnp.float32)[:, None] * freq[None, :]
    return (jnp.cos(angle)[:, None, :], jnp.sin(angle)[:, None, :])


def rotate(values, cosine, sine):
    half = values.shape[-1] // 2
    first = values[..., :half]
    second = values[..., half:]
    return jnp.concatenate(
        [first * cosine - second * sine, second * cosine + first * sine], axis=-1
    )


def rotate_back(grads, cosine, sine):
    half = grads.shape[-1] // 2
    first = grads[..., :half]
    second = grads[..., half:]
    return jnp.concatenate(
        [first * cosine + second * sine, second * cosine - first * sine], axis=-1
    )


def masked_scores(q_group, key_piece, query_pos, key_pos, live_count):
    scores = jnp.einsum("qhgd,khd->hgqk", q_group, key_piece, preferred_element_type=jnp.float32)
    allowed = (key_pos[None, :] <= query_pos[:, None]) & (key_pos[None, :] < live_count)
    return (scores, allowed)


def split_keys(keys, values, key_pos, key_block):
    n_blocks = keys.shape[0] // key_block
    key_pieces = keys.reshape(n_blocks, key_block, keys.shape[1], keys.shape[2])
    value_pieces = values.reshape(n_blocks, key_block, values.shape[1], values.shape[2])
    return (key_pieces, value_pieces, key_pos.reshape(n_blocks, key_block))


def attend_forward(q_group, keys, values, query_pos, key_pos, live_count, key_block):
    n_query, kv_here, group_size, head_dim = q_group.shape
    key_pieces, value_pieces, pos_pieces = split_keys(keys, values, key_pos, key_block)

    def stats(carry, piece):
        row_max, row_total = carry
        key_piece, piece_pos = piece
        scores, allowed = masked_scores(q_group, key_piece, query_pos, piece_pos, live_count)
        scores = jnp.where(allowed, scores, NEG_FILL)
        new_max = jnp.maximum(row_max, jnp.max(scores, axis=-1))
        kept_exp = jnp.where(allowed, jnp.exp(scores - new_max[..., None]), 0.0)
        row_total = row_total * jnp.exp(row_max - new_max) + jnp.sum(kept_exp, axis=-1)
        return ((new_max, row_total), None)

    start = (
        jnp.full((kv_here, group_size, n_query), NEG_FILL, jnp.float32),
        jnp.zeros((kv_here, group_size, n_query), jnp.float32),
    )
    (row_max, row_total), unused = lax.scan(stats, start, (key_pieces, pos_pieces))
    log_total = row_max + jnp.log(row_total)

    def weigh(acc, piece):
        key_piece, value_piece, piece_pos = piece
        scores, allowed = masked_scores(q_group, key_piece, query_pos, piece_pos, live_count)
        prob_low = jnp.where(allowed, jnp.exp(scores - log_total[..., None]), 0.0).astype(
            jnp.bfloat16
        )
        acc = acc + jnp.einsum(
            "hgqk,khd->qhgd", prob_low, value_piece, preferred_element_type=jnp.float32
        )
        return (acc, None)

    attn_o, unused = lax.scan(
        weigh, jnp.zeros(q_group.shape, jnp.float32), (key_pieces, value_pieces, pos_pieces)
    )
    return (attn_o, log_total)


def attend_backward(
    q_group, keys, values, query_pos, key_pos, live_count, key_block, log_total, d_out, delta
):
    kv_here = keys.shape[1]
    head_dim = keys.shape[2]
    key_pieces, value_pieces, pos_pieces = split_keys(keys, values, key_pos, key_block)

    def backstep(d_query, piece):
        key_piece, value_piece, piece_pos = piece
        scores, allowed = masked_scores(q_group, key_piece, query_pos, piece_pos, live_count)
        probs = jnp.where(allowed, jnp.exp(scores - log_total[..., None]), 0.0)
        d_probs = jnp.einsum(
            "qhgd,khd->hgqk", d_out, value_piece, preferred_element_type=jnp.float32
        )
        d_scores = (probs * (d_probs - delta[..., None])).astype(jnp.bfloat16)
        d_query = d_query + jnp.einsum(
            "hgqk,khd->qhgd", d_scores, key_piece, preferred_element_type=jnp.float32
        )
        d_key = jnp.einsum("hgqk,qhgd->khd", d_scores, q_group, preferred_element_type=jnp.float32)
        d_value = jnp.einsum(
            "hgqk,qhgd->khd", probs.astype(jnp.bfloat16), d_out, preferred_element_type=jnp.float32
        )
        return (d_query, (d_key, d_value))

    d_query, (d_key, d_value) = lax.scan(
        backstep, jnp.zeros(q_group.shape, jnp.float32), (key_pieces, value_pieces, pos_pieces)
    )
    return (d_query, d_key.reshape(-1, kv_here * head_dim), d_value.reshape(-1, kv_here * head_dim))


def gather_weights(w_query, w_key, w_value, w_headgate, w_out, w_gate, w_up, w_down):
    attn_parts = (
        lax.all_gather(w_query, ("dp", "mp"), axis=0, tiled=True),
        lax.all_gather(w_key, ("dp", "mp"), axis=0, tiled=True),
        lax.all_gather(w_value, ("dp", "mp"), axis=0, tiled=True),
        lax.all_gather(w_headgate, ("dp", "mp"), axis=0, tiled=True),
        lax.all_gather(w_out, ("dp", "mp"), axis=1, tiled=True),
    )
    ffn_parts = (
        lax.all_gather(w_gate, ("dp", "head"), axis=0, tiled=True),
        lax.all_gather(w_up, ("dp", "head"), axis=0, tiled=True),
        lax.all_gather(w_down, ("dp", "head"), axis=1, tiled=True),
    )
    return tuple(attn_parts) + tuple(ffn_parts)


def reduce_grads(g_query, g_key, g_value, g_headgate, g_out, g_gate, g_up, g_down):
    attn_parts = (
        lax.psum_scatter(
            g_query.astype(jnp.bfloat16), ("dp", "mp"), scatter_dimension=0, tiled=True
        ).astype(jnp.float32),
        lax.psum_scatter(
            g_key.astype(jnp.bfloat16), ("dp", "mp"), scatter_dimension=0, tiled=True
        ).astype(jnp.float32),
        lax.psum_scatter(
            g_value.astype(jnp.bfloat16), ("dp", "mp"), scatter_dimension=0, tiled=True
        ).astype(jnp.float32),
        lax.psum_scatter(
            g_headgate.astype(jnp.bfloat16), ("dp", "mp"), scatter_dimension=0, tiled=True
        ).astype(jnp.float32),
        lax.psum_scatter(
            g_out.astype(jnp.bfloat16), ("dp", "mp"), scatter_dimension=1, tiled=True
        ).astype(jnp.float32),
    )
    ffn_parts = (
        lax.psum_scatter(
            g_gate.astype(jnp.bfloat16), ("dp", "head"), scatter_dimension=0, tiled=True
        ).astype(jnp.float32),
        lax.psum_scatter(
            g_up.astype(jnp.bfloat16), ("dp", "head"), scatter_dimension=0, tiled=True
        ).astype(jnp.float32),
        lax.psum_scatter(
            g_down.astype(jnp.bfloat16), ("dp", "head"), scatter_dimension=1, tiled=True
        ).astype(jnp.float32),
    )
    return tuple(attn_parts) + tuple(ffn_parts)


def local(
    inputs,
    cotangent,
    seq_counts,
    seq_bucket,
    attn_norm_gain,
    q_norm_gain,
    k_norm_gain,
    w_query,
    w_key,
    w_value,
    w_headgate,
    w_out,
    ffn_norm_gain,
    w_gate,
    w_up,
    w_down,
):
    micro_batches, row_count, model_width = inputs.shape
    n_head = lax.axis_size("head")
    n_mp = lax.axis_size("mp")
    n_dp = lax.axis_size("dp")
    head_idx = lax.axis_index("head")
    mp_idx = lax.axis_index("mp")
    dp_idx = lax.axis_index("dp")
    head_dim = q_norm_gain.shape[0]
    q_heads = w_query.shape[1] // head_dim
    kv_heads = w_key.shape[1] // head_dim
    group_size = q_heads // kv_heads
    q_scale = head_dim ** (-0.5)
    seq_len = row_count * n_head * n_mp
    key_block = min(512, seq_len)
    n_query = n_head * row_count
    slot_ids = jnp.arange(micro_batches * n_dp, dtype=jnp.int32)
    slot_count = jnp.sum(
        jnp.where(seq_bucket[None, :] == slot_ids[:, None], seq_counts[None, :], 0), axis=1
    )
    local_idx = jnp.arange(row_count, dtype=jnp.int32)
    own_pos = head_idx * n_mp * row_count + mp_idx * row_count + local_idx
    query_idx = jnp.arange(n_query, dtype=jnp.int32)
    query_pos = (
        query_idx // row_count * n_mp * row_count + mp_idx * row_count + query_idx % row_count
    )
    key_idx = jnp.arange(seq_len, dtype=jnp.int32)
    key_pos = (
        key_idx % n_query // row_count * n_mp * row_count
        + key_idx // n_query * row_count
        + key_idx % row_count
    )
    rope_cos, rope_sin = rope_tables(query_pos, head_dim // 2)
    grad_total = None
    gain_attn = jnp.zeros((model_width,), jnp.float32)
    gain_query = jnp.zeros((head_dim,), jnp.float32)
    gain_key = jnp.zeros((head_dim,), jnp.float32)
    gain_ffn = jnp.zeros((model_width,), jnp.float32)
    outputs = []
    input_grads = []
    for micro_batch in range(micro_batches):
        weights = gather_weights(w_query, w_key, w_value, w_headgate, w_out, w_gate, w_up, w_down)
        wq_full, wk_full, wv_full, wg_full, wo_full, wgate_full, wup_full, wdown_full = weights
        live_count = slot_count[micro_batch * n_dp + dp_idx]
        x_float = inputs[micro_batch].astype(jnp.float32)
        scale1 = rms_scale(x_float)
        normed1 = x_float * scale1
        xn1 = (normed1 * attn_norm_gain).astype(jnp.bfloat16)
        gathered_rows = lax.all_gather(xn1, "head", axis=0, tiled=True)
        q_raw = jnp.dot(gathered_rows, wq_full, preferred_element_type=jnp.float32).reshape(
            n_query, q_heads, head_dim
        )
        k_raw = jnp.dot(gathered_rows, wk_full, preferred_element_type=jnp.float32).reshape(
            n_query, kv_heads, head_dim
        )
        value_low = jnp.dot(gathered_rows, wv_full, preferred_element_type=jnp.float32).astype(
            jnp.bfloat16
        )
        gate_logit = jnp.dot(gathered_rows, wg_full, preferred_element_type=jnp.float32)
        q_rms = rms_scale(q_raw)
        q_hat = q_raw * q_rms
        query_low = (rotate(q_hat * q_norm_gain, rope_cos, rope_sin) * q_scale).astype(jnp.bfloat16)
        k_rms = rms_scale(k_raw)
        k_hat = k_raw * k_rms
        key_low = rotate(k_hat * k_norm_gain, rope_cos, rope_sin).astype(jnp.bfloat16)
        all_keys, all_values = (
            lax.all_gather(key_low.reshape(n_query, kv_heads * head_dim), "mp", axis=0, tiled=True),
            lax.all_gather(value_low, "mp", axis=0, tiled=True),
        )
        all_keys = all_keys.reshape(seq_len, kv_heads, head_dim)
        all_values = all_values.reshape(seq_len, kv_heads, head_dim)
        q_group = query_low.reshape(n_query, kv_heads, group_size, head_dim)
        attn_o, log_total = attend_forward(
            q_group, all_keys, all_values, query_pos, key_pos, live_count, key_block
        )
        gate_prob = jax.nn.sigmoid(gate_logit)
        attn_heads = attn_o.reshape(n_query, q_heads, head_dim)
        gated = (
            (attn_heads * gate_prob[..., None])
            .reshape(n_query, q_heads * head_dim)
            .astype(jnp.bfloat16)
        )
        attn_sum = lax.psum_scatter(
            jnp.dot(gated, wo_full, preferred_element_type=jnp.float32).astype(jnp.bfloat16),
            "head",
            scatter_dimension=0,
            tiled=True,
        ).astype(jnp.float32)
        hidden1 = x_float + attn_sum
        scale2 = rms_scale(hidden1)
        normed2 = hidden1 * scale2
        xn2 = (normed2 * ffn_norm_gain).astype(jnp.bfloat16)
        live = (own_pos < live_count).astype(jnp.float32)[:, None]
        cot_live = cotangent[micro_batch].astype(jnp.float32) * live
        ffn_in, cot_rows = (
            lax.all_gather(xn2, "mp", axis=0, tiled=True),
            lax.all_gather(cot_live.astype(jnp.bfloat16), "mp", axis=0, tiled=True),
        )
        gate_pre = jnp.dot(ffn_in, wgate_full, preferred_element_type=jnp.float32)
        up_pre = jnp.dot(ffn_in, wup_full, preferred_element_type=jnp.float32)
        gate_sig = jax.nn.sigmoid(gate_pre)
        gate_act = gate_pre * gate_sig
        hidden = (gate_act * up_pre).astype(jnp.bfloat16)
        ffn_sum = lax.psum_scatter(
            jnp.dot(hidden, wdown_full, preferred_element_type=jnp.float32).astype(jnp.bfloat16),
            "mp",
            scatter_dimension=0,
            tiled=True,
        ).astype(jnp.float32)
        outputs.append((hidden1 + ffn_sum).astype(jnp.bfloat16))
        d_hidden = jnp.einsum("rd,fd->rf", cot_rows, wdown_full, preferred_element_type=jnp.float32)
        grad_down = jnp.einsum("rf,rd->fd", hidden, cot_rows, preferred_element_type=jnp.float32)
        d_up = (d_hidden * gate_act).astype(jnp.bfloat16)
        d_gate = (d_hidden * up_pre * gate_sig * (1.0 + gate_pre * (1.0 - gate_sig))).astype(
            jnp.bfloat16
        )
        grad_gate = jnp.einsum("rd,rf->df", ffn_in, d_gate, preferred_element_type=jnp.float32)
        grad_up = jnp.einsum("rd,rf->df", ffn_in, d_up, preferred_element_type=jnp.float32)
        ffn_term = jnp.einsum(
            "rf,df->rd", d_gate, wgate_full, preferred_element_type=jnp.float32
        ) + jnp.einsum("rf,df->rd", d_up, wup_full, preferred_element_type=jnp.float32)
        d_xn2 = lax.psum_scatter(
            ffn_term.astype(jnp.bfloat16), "mp", scatter_dimension=0, tiled=True
        ).astype(jnp.float32)
        gain_ffn = gain_ffn + jnp.sum(d_xn2 * normed2, axis=0)
        d_hidden1 = cot_live + norm_back(d_xn2, normed2, scale2, ffn_norm_gain)
        d_attn = lax.all_gather(d_hidden1.astype(jnp.bfloat16), "head", axis=0, tiled=True)
        d_gated = jnp.einsum(
            "rd,cd->rc", d_attn, wo_full, preferred_element_type=jnp.float32
        ).reshape(n_query, q_heads, head_dim)
        grad_out = jnp.einsum("rc,rd->cd", gated, d_attn, preferred_element_type=jnp.float32)
        d_out_low = (d_gated * gate_prob[..., None]).astype(jnp.bfloat16)
        d_gate_logit = (
            jnp.sum(d_gated * attn_heads, axis=-1) * gate_prob * (1.0 - gate_prob)
        ).astype(jnp.bfloat16)
        grad_headgate = jnp.einsum(
            "rd,rc->dc", gathered_rows, d_gate_logit, preferred_element_type=jnp.float32
        )
        d_out_group = d_out_low.reshape(n_query, kv_heads, group_size, head_dim)
        delta = jnp.transpose(jnp.sum(d_out_group.astype(jnp.float32) * attn_o, axis=-1), (1, 2, 0))
        d_query, d_key_all, d_value_all = attend_backward(
            q_group,
            all_keys,
            all_values,
            query_pos,
            key_pos,
            live_count,
            key_block,
            log_total,
            d_out_group,
            delta,
        )
        d_key_own, d_value_own = (
            lax.psum_scatter(
                d_key_all.astype(jnp.bfloat16), "mp", scatter_dimension=0, tiled=True
            ).astype(jnp.float32),
            lax.psum_scatter(
                d_value_all.astype(jnp.bfloat16), "mp", scatter_dimension=0, tiled=True
            ).astype(jnp.float32),
        )
        dq_norm = rotate_back(
            (d_query * q_scale).reshape(n_query, q_heads, head_dim), rope_cos, rope_sin
        )
        gain_query = gain_query + jnp.sum(dq_norm * q_hat, axis=(0, 1))
        d_q_raw = (
            norm_back(dq_norm, q_hat, q_rms, q_norm_gain)
            .reshape(n_query, q_heads * head_dim)
            .astype(jnp.bfloat16)
        )
        dk_norm = rotate_back(d_key_own.reshape(n_query, kv_heads, head_dim), rope_cos, rope_sin)
        gain_key = gain_key + jnp.sum(dk_norm * k_hat, axis=(0, 1))
        d_k_raw = (
            norm_back(dk_norm, k_hat, k_rms, k_norm_gain)
            .reshape(n_query, kv_heads * head_dim)
            .astype(jnp.bfloat16)
        )
        d_value_low = d_value_own.astype(jnp.bfloat16)
        grad_query = jnp.einsum(
            "rd,rc->dc", gathered_rows, d_q_raw, preferred_element_type=jnp.float32
        )
        grad_key = jnp.einsum(
            "rd,rc->dc", gathered_rows, d_k_raw, preferred_element_type=jnp.float32
        )
        grad_value = jnp.einsum(
            "rd,rc->dc", gathered_rows, d_value_low, preferred_element_type=jnp.float32
        )
        attn_term = jnp.einsum("rc,dc->rd", d_q_raw, wq_full, preferred_element_type=jnp.float32)
        attn_term = attn_term + jnp.einsum(
            "rc,dc->rd", d_k_raw, wk_full, preferred_element_type=jnp.float32
        )
        attn_term = attn_term + jnp.einsum(
            "rc,dc->rd", d_value_low, wv_full, preferred_element_type=jnp.float32
        )
        attn_term = attn_term + jnp.einsum(
            "rc,dc->rd", d_gate_logit, wg_full, preferred_element_type=jnp.float32
        )
        d_xn1 = lax.psum_scatter(
            attn_term.astype(jnp.bfloat16), "head", scatter_dimension=0, tiled=True
        ).astype(jnp.float32)
        gain_attn = gain_attn + jnp.sum(d_xn1 * normed1, axis=0)
        input_grads.append(
            (d_hidden1 + norm_back(d_xn1, normed1, scale1, attn_norm_gain)).astype(jnp.bfloat16)
        )
        batch_grads = reduce_grads(
            grad_query, grad_key, grad_value, grad_headgate, grad_out, grad_gate, grad_up, grad_down
        )
        if grad_total is None:
            grad_total = batch_grads
        else:
            grad_total = tuple((a + b for a, b in zip(grad_total, batch_grads)))
    sum_attn, sum_query, sum_key, sum_ffn = lax.psum(
        (gain_attn, gain_query, gain_key, gain_ffn), ("dp", "head", "mp")
    )
    return (
        jnp.stack(outputs),
        jnp.stack(input_grads),
        sum_attn,
        sum_query,
        sum_key,
        grad_total[0],
        grad_total[1],
        grad_total[2],
        grad_total[3],
        grad_total[4],
        sum_ffn,
        grad_total[5],
        grad_total[6],
        grad_total[7],
    )


PLANE = ("head", "mp")
BIT_X, BIT_C, BIT_Y = 1, 2, 4
NT = (((1,), (1,)), ((), ()))
NN = (((1,), (0,)), ((), ()))
TN = (((0,), (0,)), ((), ()))
F32 = jnp.float32
BF16 = jnp.bfloat16
COST_SHARE = 0.2
LATE_SHARE = 0.1


def dot(left, right, dims=NN):
    return lax.dot_general(left, right, dims, preferred_element_type=F32)


def swap(values, bits):
    return lax.ppermute(values, PLANE, [(i, i ^ bits) for i in range(8)])


def swap_mixed(values, core0, core1):
    return lax.ppermute(
        values, PLANE, [(i, i ^ (core1 if i & BIT_C else core0)) for i in range(8)]
    )


class Order:
    def __init__(self):
        self.ahead = []
        self.last = None

    def need(self, *values):
        self.ahead.extend(values)

    def pin(self, value):
        if self.last is None:
            return value
        return lax.optimization_barrier((value, self.last))[0]

    def run(self, op, *operands):
        if self.ahead:
            operands = lax.optimization_barrier((tuple(operands), tuple(self.ahead)))[0]
        out = op(*operands)
        self.last = out[0] if isinstance(out, (tuple, list)) else out
        self.ahead = [self.last]
        return out


class Gather:
    def __init__(self, order, rows):
        self.order = order
        self.rows = rows
        self.came = swap_mixed(rows, BIT_X, BIT_Y)

    def second(self):
        came = self.order.pin(self.came)
        near = jnp.concatenate([self.rows, came], axis=0)
        self.came = swap_mixed(near, BIT_Y, BIT_X)
        self.pieces = [near, None, swap(near, BIT_C), None]
        return near

    def third(self):
        far = self.order.pin(self.came)
        self.pieces[1], self.pieces[3] = far, swap(far, BIT_C)
        return far


def add_pieces_kernel(first, second, out):
    out[...] = (first[...].astype(F32) + second[...].astype(F32)).astype(BF16)


def add_pieces(first, second):
    count, width = first.shape
    block = pl.BlockSpec((count // 4, width), lambda i: (i, 0))
    return pl.pallas_call(
        add_pieces_kernel,
        grid=(4,),
        in_specs=[block] * 2,
        out_specs=block,
        out_shape=jax.ShapeDtypeStruct((count, width), BF16),
        cost_estimate=pl.CostEstimate(
            flops=count * width, bytes_accessed=6 * count * width, transcendentals=0
        ),
        name="add_pieces",
    )(first, second)


class Scatter:
    def __init__(self, order, near, far):
        self.order = order
        self.came = (swap(near, BIT_C), swap(far, BIT_C))

    def add(self, near, far):
        near_came, far_came = self.order.pin(self.came)
        self.near = (near, near_came)
        self.far = add_pieces(far, far_came)
        return (self.far,)

    def send_far(self):
        self.came = swap_mixed(self.order.pin(self.far), BIT_Y, BIT_X)

    def take(self):
        terms = (*self.near, self.order.pin(self.came))
        half = terms[0].shape[0] // 2
        low, high = [sum(t[part].astype(F32) for t in terms) for part in (slice(0, half), slice(half, None))]
        self.kept = low
        self.sent = high.astype(BF16)
        return self.sent

    def send_near(self):
        self.came = swap_mixed(self.order.pin(self.sent), BIT_X, BIT_Y)

    def result(self):
        return self.kept + self.order.pin(self.came).astype(F32)


def norm_rope(raw, gain, cosine, sine):
    scale_rows = lax.rsqrt(jnp.mean(raw * raw, axis=-1, keepdims=True) + EPS)
    hat = raw * scale_rows
    turned = hat * gain
    return (turned * cosine + pltpu.roll(turned, 64, 1) * sine, hat, scale_rows)


def norm_rope_back(grad, hat, scale_rows, gain, cosine, sine):
    grad_n = grad * cosine - pltpu.roll(grad, 64, 1) * sine
    gain_part = jnp.sum(grad_n * hat, axis=0, keepdims=True)
    scaled = grad_n * gain
    raw = scale_rows * (scaled - hat * jnp.mean(scaled * hat, axis=-1, keepdims=True))
    return (raw, gain_part)


def two_lanes(first, second, shape):
    lane = lax.broadcasted_iota(jnp.int32, shape, 1)
    return jnp.where(lane == 0, first, jnp.where(lane == 1, second, 0.0))


def cost(flops, traffic, transcendentals=0, share=COST_SHARE):
    return pl.CostEstimate(
        flops=int(flops / share),
        bytes_accessed=int(traffic / share),
        transcendentals=int(transcendentals / share),
    )


SLOT, LIVE, BLOCK, PLACE = 0, 8, 9, 41


def attend_table(plane_idx, core, live_count):
    slot = jnp.arange(8, dtype=jnp.int32)
    across, low, high = slot >> 2, slot & 1, (slot >> 1) & 1
    x_first = (core ^ across) == 0
    apart = across * 2 + jnp.where(x_first, low + 4 * high, high + 4 * low)
    place = apart ^ plane_idx
    slots = jnp.sum(jnp.where(place[None, :] == slot[:, None], slot[None, :], 0), axis=1)
    steps = jnp.arange(8, dtype=jnp.int32)
    blocks = []
    for piece in range(4):
        one, two = place[2 * piece], place[2 * piece + 1]
        first = jnp.where(one < two, 0, 1)
        blocks.append(jnp.where(steps >= jnp.maximum(one, two), 1 - first, first))
    return jnp.concatenate([slots, live_count[None]] + blocks + [place]).astype(jnp.int32)


def take_piece(slot, pieces):
    near = jnp.where(slot < 2, pieces[0][...], pieces[1][...])
    far = jnp.where(slot < 6, pieces[2][...], pieces[3][...])
    return jnp.where(slot < 4, near, far)


def walk_tiles(step, rows, live, add_tile):
    pairs = step // 2
    whole = jnp.minimum(pairs, live // (2 * rows))

    def tile(index, carry):
        add_tile(pl.multiple_of(index * 2 * rows, 2 * rows), 2 * rows, False)
        return carry

    lax.fori_loop(0, whole, tile, 0)
    odd = step % 2 == 1
    edge = pl.multiple_of(pairs * 2 * rows, 2 * rows)

    @pl.when((whole < pairs) & (whole * 2 * rows < live))
    def _():
        add_tile(pl.multiple_of(whole * 2 * rows, 2 * rows), 2 * rows, True)

    @pl.when(odd & (edge < live))
    def _():
        add_tile(edge, 2 * rows, True)

    @pl.when(jnp.logical_not(odd) & (edge < live))
    def _():
        add_tile(edge, rows, True)


def attend_forward_kernel(table, *refs):
    x_pieces, (weights, cosine, sine, q_gain, k_gain) = refs[:4], refs[4:9]
    proj, attn_o, lse, gated = refs[9:13]
    out_pieces, (keys, values, acc) = refs[13:17], refs[17:]
    step = pl.program_id(0)
    rows = proj.shape[0]
    live, slot = table[LIVE], table[SLOT + step]
    cos_b, sin_b = cosine[...], sine[...]
    here = pl.multiple_of(step * rows, rows)
    proj[...] = dot(take_piece(slot, x_pieces), weights[:, 0:640])
    key, _, _ = norm_rope(proj[:, 256:384], k_gain[...], cos_b, sin_b)
    keys[pl.ds(here, rows), :] = key.astype(BF16)
    values[pl.ds(here, rows), 0:128] = proj[:, 384:512].astype(BF16)
    values[pl.ds(here, rows), 128:256] = jnp.ones((rows, 128), BF16)
    q_scale = 128**-0.5
    first, _, _ = norm_rope(proj[:, 0:128], q_gain[...], cos_b, sin_b)
    second, _, _ = norm_rope(proj[:, 128:256], q_gain[...], cos_b, sin_b)
    query = (jnp.concatenate([first, second], axis=0) * q_scale).astype(BF16)

    def add_tile(there, count, masked):
        weight = jnp.exp(dot(query, keys[pl.ds(there, count), :], NT))
        if masked:
            row = lax.broadcasted_iota(jnp.int32, (2 * rows, count), 0)
            place = there + lax.broadcasted_iota(jnp.int32, (2 * rows, count), 1)
            allowed = (place <= here + jnp.where(row >= rows, row - rows, row)) & (place < live)
            weight = jnp.where(allowed, weight, 0.0)
        acc[...] += dot(weight.astype(BF16), values[pl.ds(there, count), :])

    acc[...] = jnp.zeros_like(acc)
    walk_tiles(step, rows, live, add_tile)
    total = acc[:, 128:129]
    out = acc[:, 0:128] / total
    log_total = jnp.log(total)
    gate0 = jax.nn.sigmoid(proj[:, 512:513])
    gate1 = jax.nn.sigmoid(proj[:, 513:514])
    attn_o[:, 0:128] = out[:rows]
    attn_o[:, 128:256] = out[rows:]
    gated[:, 0:128] = (out[:rows] * gate0).astype(BF16)
    gated[:, 128:256] = (out[rows:] * gate1).astype(BF16)
    lse[...] = two_lanes(log_total[:rows], log_total[rows:], (rows, 128))
    part = dot(gated[...], weights[:, 640:896], NT).astype(BF16)
    for piece in range(4):

        @pl.when(slot // 2 == piece)
        def _():
            out_pieces[piece][...] = part


def attend_backward_kernel(table, *refs):
    d_pieces = refs[:4]
    weights, proj, attn_o, lse, cosine, sine, q_gain, k_gain = refs[4:12]
    d_proj, gain_q, gain_k = refs[12:15]
    back_pieces = refs[15:19]
    keys, keys_t, values, k_raw, d_keys, d_values, d_query, d_held = refs[19:]
    step = pl.program_id(0)
    rows = proj.shape[0]
    live = table[LIVE]
    q_scale = 128**-0.5

    @pl.when(step == 0)
    def _():
        gain_q[...] = jnp.zeros_like(gain_q)
        gain_k[...] = jnp.zeros_like(gain_k)

    @pl.when(step < 8)
    def _():
        here = pl.multiple_of(step * rows, rows)
        slot = table[SLOT + step]
        cos_b, sin_b = cosine[pl.ds(here, rows), :], sine[pl.ds(here, rows), :]
        raw_key = proj[:, 256:384]
        k_raw[pl.ds(here, rows), :] = raw_key
        key, _, _ = norm_rope(raw_key, k_gain[...], cos_b, sin_b)
        key = key.astype(BF16)
        keys[pl.ds(here, rows), :] = key
        keys_t[:, pl.ds(here, rows)] = key.T
        values[pl.ds(here, rows), :] = proj[:, 384:512].astype(BF16)
        d_keys[pl.ds(here, rows), :] = jnp.zeros((rows, 128), F32)
        d_values[pl.ds(here, rows), :] = jnp.zeros((rows, 128), F32)
        d_query[...] = jnp.zeros_like(d_query)
        first, hat0, scale0 = norm_rope(proj[:, 0:128], q_gain[...], cos_b, sin_b)
        second, hat1, scale1 = norm_rope(proj[:, 128:256], q_gain[...], cos_b, sin_b)
        query = (jnp.concatenate([first, second], axis=0) * q_scale).astype(BF16)
        gate0 = jax.nn.sigmoid(proj[:, 512:513])
        gate1 = jax.nn.sigmoid(proj[:, 513:514])
        d_gated = dot(take_piece(slot, d_pieces), weights[:, 640:896])
        dg0, dg1 = d_gated[:, 0:128], d_gated[:, 128:256]
        out0, out1 = attn_o[:, 0:128], attn_o[:, 128:256]
        do0, do1 = (dg0 * gate0).astype(BF16), (dg1 * gate1).astype(BF16)
        logit0 = jnp.sum(dg0 * out0, axis=-1, keepdims=True) * gate0 * (1.0 - gate0)
        logit1 = jnp.sum(dg1 * out1, axis=-1, keepdims=True) * gate1 * (1.0 - gate1)
        d_held[pl.ds(here, rows), 512:640] = two_lanes(logit0, logit1, (rows, 128)).astype(BF16)
        delta0 = jnp.sum(do0.astype(F32) * out0, axis=-1, keepdims=True)
        delta1 = jnp.sum(do1.astype(F32) * out1, axis=-1, keepdims=True)
        delta_t = two_lanes(delta0, delta1, (rows, 128)).T
        delta = jnp.concatenate([delta_t[0:1], delta_t[1:2]], axis=1)
        lse_t = lse[...].T
        log_total = jnp.concatenate([lse_t[0:1], lse_t[1:2]], axis=1)
        d_out = jnp.concatenate([do0, do1], axis=0)

        def add_tile(there, count, masked):
            here_keys = pl.ds(there, count)
            scores = dot(keys[here_keys, :], query, NT)
            probs = jnp.exp(scores - log_total)
            if masked:
                place = there + lax.broadcasted_iota(jnp.int32, (count, 2 * rows), 0)
                q_col = lax.broadcasted_iota(jnp.int32, (count, 2 * rows), 1)
                q_place = here + jnp.where(q_col >= rows, q_col - rows, q_col)
                probs = jnp.where((place <= q_place) & (place < live), probs, 0.0)
            d_probs = dot(values[here_keys, :], d_out, NT)
            d_scores = (probs * (d_probs - delta)).astype(BF16)
            d_values[here_keys, :] += dot(probs.astype(BF16), d_out)
            d_keys[here_keys, :] += dot(d_scores, query)
            d_query[...] += dot(keys_t[:, here_keys], d_scores)

        walk_tiles(step, rows, live, add_tile)
        grads = d_query[...].T * q_scale
        raw0, part0 = norm_rope_back(grads[:rows], hat0, scale0, q_gain[...], cos_b, sin_b)
        raw1, part1 = norm_rope_back(grads[rows:], hat1, scale1, q_gain[...], cos_b, sin_b)
        d_held[pl.ds(here, rows), 0:128] = raw0.astype(BF16)
        d_held[pl.ds(here, rows), 128:256] = raw1.astype(BF16)
        gain_q[0:1, :] += part0 + part1

    @pl.when(step >= 8)
    def _():
        slot = (step - 4) % 8
        there = pl.multiple_of(table[PLACE + slot] * rows, rows)
        cos_k, sin_k = cosine[pl.ds(there, rows), :], sine[pl.ds(there, rows), :]
        _, hat, scale_rows = norm_rope(k_raw[pl.ds(there, rows), :], k_gain[...], cos_k, sin_k)
        raw, part = norm_rope_back(
            d_keys[pl.ds(there, rows), :], hat, scale_rows, k_gain[...], cos_k, sin_k
        )
        gain_k[0:1, :] += part
        d_held[pl.ds(there, rows), 256:384] = raw.astype(BF16)
        d_held[pl.ds(there, rows), 384:512] = d_values[pl.ds(there, rows), :].astype(BF16)
        d_block = d_held[pl.ds(there, rows), :]
        d_proj[...] = d_block
        back = dot(d_block, weights[:, 0:640], NT).astype(BF16)
        for piece in range(4):

            @pl.when(slot // 2 == piece)
            def _():
                back_pieces[piece][...] = back


def attend_forward_call(table, pieces, weights, cosine, sine, q_gain, k_gain):
    seq_len, width = cosine.shape[0], weights.shape[0]
    rows = seq_len // 8
    by_slot = lambda i, t: (t[SLOT + i], 0)
    by_place = lambda i, t: (i, 0)
    fixed = lambda i, t: (0, 0)
    whole = [
        pl.BlockSpec((rows, width), lambda i, t, k=k: (t[BLOCK + 8 * k + i], 0)) for k in range(4)
    ]
    pairs = seq_len * (seq_len + rows)
    return pl.pallas_call(
        attend_forward_kernel,
        grid_spec=pltpu.PrefetchScalarGridSpec(
            num_scalar_prefetch=1,
            grid=(8,),
            in_specs=whole
            + [
                pl.BlockSpec(weights.shape, fixed, pipeline_mode=pl.Buffered(1)),
                pl.BlockSpec((rows, 128), by_place),
                pl.BlockSpec((rows, 128), by_place),
                pl.BlockSpec((1, 128), fixed),
                pl.BlockSpec((1, 128), fixed),
            ],
            out_specs=[
                pl.BlockSpec((rows, 640), by_slot),
                pl.BlockSpec((rows, 256), by_slot),
                pl.BlockSpec((rows, 128), by_slot),
                pl.BlockSpec((rows, 256), by_slot),
            ]
            + whole,
            scratch_shapes=[
                pltpu.VMEM((seq_len, 128), BF16),
                pltpu.VMEM((seq_len, 256), BF16),
                pltpu.VMEM((2 * rows, 256), F32),
            ],
        ),
        out_shape=[
            jax.ShapeDtypeStruct((seq_len, 640), F32),
            jax.ShapeDtypeStruct((seq_len, 256), F32),
            jax.ShapeDtypeStruct((seq_len, 128), F32),
            jax.ShapeDtypeStruct((seq_len, 256), BF16),
        ]
        + [jax.ShapeDtypeStruct((2 * rows, width), BF16)] * 4,
        compiler_params=pltpu.CompilerParams(
            dimension_semantics=("arbitrary",), vmem_limit_bytes=62 << 20
        ),
        cost_estimate=cost(
            2 * seq_len * width * 896 + 4 * pairs * 128, 2 * seq_len * (2 * width + 2200), pairs
        ),
        name="attend_forward",
    )(table, *pieces, weights, cosine, sine, q_gain, k_gain)


def attend_backward_call(table, pieces, weights, proj, attn_o, lse, cosine, sine, q_gain, k_gain):
    seq_len, width = cosine.shape[0], weights.shape[0]
    rows = seq_len // 8
    by_slot = lambda i, t: (t[SLOT + jnp.minimum(i, 7)], 0)
    last_slot = lambda i, t: (jnp.where(i < 8, 4, (i - 4) % 8), 0)
    fixed = lambda i, t: (0, 0)
    pairs = seq_len * (seq_len + rows)
    return pl.pallas_call(
        attend_backward_kernel,
        grid_spec=pltpu.PrefetchScalarGridSpec(
            num_scalar_prefetch=1,
            grid=(16,),
            in_specs=[
                pl.BlockSpec(
                    (rows, width), lambda i, t, k=k: (t[BLOCK + 8 * k + jnp.minimum(i, 7)], 0)
                )
                for k in range(4)
            ]
            + [
                pl.BlockSpec(weights.shape, fixed, pipeline_mode=pl.Buffered(1)),
                pl.BlockSpec((rows, 640), by_slot),
                pl.BlockSpec((rows, 256), by_slot),
                pl.BlockSpec((rows, 128), by_slot),
                pl.BlockSpec((seq_len, 128), fixed, pipeline_mode=pl.Buffered(1)),
                pl.BlockSpec((seq_len, 128), fixed, pipeline_mode=pl.Buffered(1)),
                pl.BlockSpec((1, 128), fixed),
                pl.BlockSpec((1, 128), fixed),
            ],
            out_specs=[
                pl.BlockSpec((rows, 640), last_slot),
                pl.BlockSpec((8, 128), fixed),
                pl.BlockSpec((8, 128), fixed),
            ]
            + [
                pl.BlockSpec(
                    (rows, width), lambda i, t, k=k: (jnp.clip(i - 8 - (2 * k + 4) % 8, 0, 1), 0)
                )
                for k in range(4)
            ],
            scratch_shapes=[
                pltpu.VMEM((seq_len, 128), BF16),
                pltpu.VMEM((128, seq_len), BF16),
                pltpu.VMEM((seq_len, 128), BF16),
                pltpu.VMEM((seq_len, 128), F32),
                pltpu.VMEM((seq_len, 128), F32),
                pltpu.VMEM((seq_len, 128), F32),
                pltpu.VMEM((128, 2 * rows), F32),
                pltpu.VMEM((seq_len, 640), BF16),
            ],
        ),
        out_shape=[
            jax.ShapeDtypeStruct((seq_len, 640), BF16),
            jax.ShapeDtypeStruct((8, 128), F32),
            jax.ShapeDtypeStruct((8, 128), F32),
        ]
        + [jax.ShapeDtypeStruct((2 * rows, width), BF16)] * 4,
        compiler_params=pltpu.CompilerParams(
            dimension_semantics=("arbitrary",), vmem_limit_bytes=62 << 20
        ),
        cost_estimate=cost(
            2 * seq_len * width * 896 + 10 * pairs * 128,
            2 * seq_len * (2 * width + 2200),
            pairs,
            LATE_SHARE,
        ),
        name="attend_backward",
    )(table, *pieces, weights, proj, attn_o, lse, cosine, sine, q_gain, k_gain)


def feed_forward_kernel(*refs):
    rows_near, rows_far, cot_near, cot_far, w_down_t, w_inner = refs[:6]
    hidden_out, d_pre_out, down_near, down_far, back_near, back_far = refs[-6:]
    near = pl.program_id(0) < 2
    units = hidden_out.shape[1]
    pre = dot(jnp.where(near, rows_near[...], rows_far[...]), w_inner[...])
    d_hidden = dot(jnp.where(near, cot_near[...], cot_far[...]), w_down_t[...])
    gate_pre, up_pre = pre[:, :units], pre[:, units:]
    gate_sig = jax.nn.sigmoid(gate_pre)
    gate_act = gate_pre * gate_sig
    hidden_out[...] = (gate_act * up_pre).astype(BF16)
    d_pre_out[:, units:] = (d_hidden * gate_act).astype(BF16)
    d_pre_out[:, :units] = (
        d_hidden * up_pre * gate_sig * (1.0 + gate_pre * (1.0 - gate_sig))
    ).astype(BF16)
    back = dot(d_pre_out[...], w_inner[...], NT)
    down = dot(hidden_out[...], w_down_t[...], NT)

    @pl.when(near)
    def _():
        back_near[...] = back.astype(BF16)
        down_near[...] = down.astype(BF16)

    @pl.when(jnp.logical_not(near))
    def _():
        back_far[...] = back.astype(BF16)
        down_far[...] = down.astype(BF16)


def feed_forward_call(rows, cots, w_down_t, w_inner):
    count, width = rows[0].shape
    units = w_down_t.shape[1]
    tile = count // 2
    by_row = lambda i: (i, 0)
    fixed = lambda i: (0, 0)
    near = pl.BlockSpec((tile, width), lambda i: (jnp.minimum(i, 1), 0))
    far = pl.BlockSpec((tile, width), lambda i: (jnp.maximum(i - 2, 0), 0))
    wide = jax.ShapeDtypeStruct((count, width), BF16)
    out = pl.pallas_call(
        feed_forward_kernel,
        grid=(4,),
        in_specs=[near, far, near, far]
        + [pl.BlockSpec(w.shape, fixed, pipeline_mode=pl.Buffered(1)) for w in (w_down_t, w_inner)],
        out_specs=[
            pl.BlockSpec((tile, units), by_row),
            pl.BlockSpec((tile, 2 * units), by_row),
            near,
            far,
            near,
            far,
        ],
        out_shape=[
            jax.ShapeDtypeStruct((2 * count, units), BF16),
            jax.ShapeDtypeStruct((2 * count, 2 * units), BF16),
            wide,
            wide,
            wide,
            wide,
        ],
        compiler_params=pltpu.CompilerParams(
            dimension_semantics=("arbitrary",), vmem_limit_bytes=52 << 20
        ),
        cost_estimate=cost(24 * count * width * units, 2 * width * (8 * count + 3 * units)),
        name="feed_forward",
    )(*rows, *cots, w_down_t, w_inner)
    return (out[0], out[1], (out[2], out[3]), (out[4], out[5]))


def weight_grad_call(n_parts, lefts, terms, weights=None, carried=None, final=True, keep=None):
    n_pieces = len(lefts[0])
    rows, width = lefts[0][0].shape
    columns = [pieces[0][0].shape[1] for _, pieces in terms]
    kept = [keep or c for c in columns]
    starts = [sum(kept[:k]) for k in range(len(terms))]
    total = sum(kept)
    arrays, place = ([], {})
    for _, pieces in terms:
        for array, _ in pieces:
            if id(array) not in place:
                place[id(array)] = len(arrays)
                arrays.append(array)
    n_left, n_terms = len(lefts), len(terms)

    def kernel(*refs):
        left_refs = refs[: n_left * n_pieces]
        right_refs = refs[len(left_refs) : len(left_refs) + len(arrays)]
        rest = list(refs[len(left_refs) + len(arrays) :])
        if weights is not None:
            weights_ref = rest.pop(0)
        if carried is not None:
            carried_ref = rest.pop(0)
        out = rest.pop(0)
        if weights is not None:
            gain = rest.pop(0)
        left_buf, right_buf = rest[:n_left], rest[n_left : n_left + n_terms]
        accs, sems = rest[n_left + n_terms : -1], rest[-1]

        def copies(piece, slot):
            made = [
                pltpu.make_async_copy(
                    left_refs[k * n_pieces + piece], left_buf[k].at[slot], sems.at[slot, k]
                )
                for k in range(n_left)
            ]
            for k, (_, pieces) in enumerate(terms):
                array, first = pieces[piece]
                made.append(
                    pltpu.make_async_copy(
                        right_refs[place[id(array)]].at[pl.ds(first, rows)],
                        right_buf[k].at[slot],
                        sems.at[slot, n_left + k],
                    )
                )
            return made

        for copy in copies(0, 0):
            copy.start()
        if not final:
            accs = [out]
        for acc in accs:
            acc[...] = jnp.zeros_like(acc) if carried is None else carried_ref[...]

        def body(index, carry):
            slot = lax.rem(index, 2)
            for piece in range(1, n_pieces):

                @pl.when(index + 1 == piece)
                def _():
                    for copy in copies(piece, piece % 2):
                        copy.start()

            for copy in copies(0, slot):
                copy.wait()
            for k, (left, _) in enumerate(terms):
                for first in range(0, columns[k], 256):
                    some = slice(first, min(first + 256, columns[k]))
                    accs[k][some, :] += dot(right_buf[k][slot, :, some], left_buf[left][slot], TN)
            return carry

        lax.fori_loop(0, n_pieces, body, 0)
        if not final:
            return
        part = width // n_parts
        for p in range(n_parts):
            for k in range(n_terms):
                start = p * total + starts[k]
                some = accs[k][: kept[k], p * part : (p + 1) * part]
                out[start : start + kept[k], :] = some.astype(BF16)
        if weights is not None:
            scaled = accs[0][...] * weights_ref[:, : columns[0]].T.astype(F32)
            gain[...] = jnp.broadcast_to(jnp.sum(scaled, axis=0, keepdims=True), gain.shape)

    out_shape = [jax.ShapeDtypeStruct((n_parts * total, width // n_parts), BF16)]
    if not final:
        out_shape = [jax.ShapeDtypeStruct((total, width), F32)]
    vmem = pl.BlockSpec(memory_space=pltpu.VMEM)
    operands = [piece for pieces in lefts for piece in pieces] + arrays
    in_specs = [pl.BlockSpec(memory_space=pl.ANY)] * len(operands)
    if weights is not None:
        operands.append(weights)
        in_specs.append(vmem)
        out_shape.append(jax.ShapeDtypeStruct((8, width), F32))
    if carried is not None:
        operands.append(carried)
        in_specs.append(vmem)
    return pl.pallas_call(
        kernel,
        in_specs=in_specs,
        out_specs=[vmem] * len(out_shape),
        out_shape=out_shape,
        scratch_shapes=[pltpu.VMEM((2, rows, width), BF16)] * n_left
        + [pltpu.VMEM((2, rows, c), BF16) for c in columns]
        + [pltpu.VMEM((c, width), F32) for c in columns if final]
        + [pltpu.SemaphoreType.DMA((2, n_left + n_terms))],
        compiler_params=pltpu.CompilerParams(vmem_limit_bytes=56 << 20),
        cost_estimate=cost(
            2 * n_pieces * rows * width * total,
            2 * n_pieces * rows * (n_left * width + total) + 2 * width * total,
            0,
            LATE_SHARE,
        ),
        name="weight_grad",
    )(*operands)


def pack_attention_kernel(index, query, key, value, headgate, out, packed):
    half = pl.program_id(0) ^ index[0]
    packed[0, :, 0:256] = query[...]
    packed[0, :, 256:384] = key[...]
    packed[0, :, 384:512] = value[...]
    gates = headgate[...].astype(F32)
    first = jnp.where(half == 0, gates[:, 0:1], gates[:, 2:3])
    second = jnp.where(half == 0, gates[:, 1:2], gates[:, 3:4])
    packed[0, :, 512:640] = two_lanes(first, second, (packed.shape[1], 128)).astype(BF16)
    packed[0, :, 640:896] = out[...].T


def pack_attention(index, query, key, value, headgate, out):
    rows = query.shape[0]
    half = lambda i, t: (0, i ^ t[0])
    return pl.pallas_call(
        pack_attention_kernel,
        grid_spec=pltpu.PrefetchScalarGridSpec(
            num_scalar_prefetch=1,
            grid=(2,),
            in_specs=[
                pl.BlockSpec((rows, 256), half),
                pl.BlockSpec((rows, 128), half),
                pl.BlockSpec((rows, 128), half),
                pl.BlockSpec(headgate.shape, lambda i, t: (0, 0)),
                pl.BlockSpec((256, out.shape[1]), lambda i, t: (i ^ t[0], 0)),
            ],
            out_specs=pl.BlockSpec((1, rows, 896), lambda i, t: (i, 0, 0)),
        ),
        out_shape=jax.ShapeDtypeStruct((2, rows, 896), BF16),
        cost_estimate=cost(0, 4 * rows * 896 * 2),
        name="pack_attention",
    )(index, query, key, value, headgate, out)


def unpack_attention_kernel(index, kept, came, out_kept, out_came, query, key, value, headgate, out):
    flip = index[0] == 1

    def ordered(mine, other):
        return [
            jnp.where(flip, other[...], mine[...]).astype(F32),
            jnp.where(flip, mine[...], other[...]).astype(F32),
        ]

    for k, part in enumerate(ordered(kept, came)):
        query[:, 256 * k : 256 * k + 256] = part[0:256].T
        key[:, 128 * k : 128 * k + 128] = part[256:384].T
        value[:, 128 * k : 128 * k + 128] = part[384:512].T
        headgate[:, 2 * k : 2 * k + 2] = part[512:528].T[:, 0:2]
    for k, part in enumerate(ordered(out_kept, out_came)):
        out[256 * k : 256 * k + 256, :] = part


def unpack_attention(index, kept, came, out_kept, out_came):
    rows = kept.shape[1]
    vmem = pl.BlockSpec(memory_space=pltpu.VMEM)
    shapes = [(rows, 512), (rows, 256), (rows, 256), (rows, 4), (512, rows)]
    return pl.pallas_call(
        unpack_attention_kernel,
        in_specs=[pl.BlockSpec(memory_space=pltpu.SMEM)] + [vmem] * 4,
        out_specs=[vmem] * 5,
        out_shape=[jax.ShapeDtypeStruct(shape, F32) for shape in shapes],
        cost_estimate=cost(0, 8 * rows * 896),
        name="unpack_attention",
    )(index, kept, came, out_kept, out_came)


def pack_feed_forward_kernel(index, gate, up, down, packed):
    units = gate.shape[1]
    packed[0, :, :units] = down[...].T
    packed[0, :, units : 2 * units] = gate[...]
    packed[0, :, 2 * units :] = up[...]


def pack_feed_forward(index, gate, up, down):
    rows, units = gate.shape[0], gate.shape[1] // 4
    quarter = pl.BlockSpec((rows, units), lambda i, t: (0, i ^ t[0]))
    return pl.pallas_call(
        pack_feed_forward_kernel,
        grid_spec=pltpu.PrefetchScalarGridSpec(
            num_scalar_prefetch=1,
            grid=(4,),
            in_specs=[
                quarter,
                quarter,
                pl.BlockSpec((units, rows), lambda i, t: (i ^ t[0], 0)),
            ],
            out_specs=pl.BlockSpec((1, rows, 3 * units), lambda i, t: (i, 0, 0)),
        ),
        out_shape=jax.ShapeDtypeStruct((4, rows, 3 * units), BF16),
        cost_estimate=cost(0, 8 * rows * units * 6),
        name="pack_feed_forward",
    )(index, gate, up, down)


def unpack_feed_forward_kernel(index, *refs):
    pieces, (gate, up, down) = refs[:8], refs[8:]
    units = gate.shape[1]
    apart = pl.program_id(0) ^ index[0]

    def of_piece(group):
        low = jnp.where(apart == 0, group[0][...], group[1][...])
        high = jnp.where(apart == 2, group[2][...], group[3][...])
        return jnp.where(apart < 2, low, high).astype(F32)

    inner = of_piece(pieces[:4])
    gate[...] = inner[:units].T
    up[...] = inner[units:].T
    down[...] = of_piece(pieces[4:])


def unpack_feed_forward(index, inners, downs):
    units, rows = downs[0].shape
    quarter = pl.BlockSpec((rows, units), lambda i, t: (0, i))
    whole = [pl.BlockSpec(v.shape, lambda i, t: (0, 0)) for v in (*inners, *downs)]
    wide = jax.ShapeDtypeStruct((rows, 4 * units), F32)
    return pl.pallas_call(
        unpack_feed_forward_kernel,
        grid_spec=pltpu.PrefetchScalarGridSpec(
            num_scalar_prefetch=1,
            grid=(4,),
            in_specs=whole,
            out_specs=[quarter, quarter, pl.BlockSpec((units, rows), lambda i, t: (i, 0))],
        ),
        out_shape=[wide, wide, jax.ShapeDtypeStruct((4 * units, rows), F32)],
        cost_estimate=cost(0, 24 * rows * units * 4),
        name="unpack_feed_forward",
    )(index, *inners, *downs)


def pick(flag, first, second):
    return jnp.where(flag, first, second)


def reorder_by(pieces, index):
    low, high = (index & 1) == 1, (index & 2) == 2
    swapped = [pick(low, pieces[j ^ 1], pieces[j]) for j in range(4)]
    return [pick(high, swapped[j ^ 2], swapped[j]) for j in range(4)]


def local_plane(
    inputs,
    cotangent,
    seq_counts,
    seq_bucket,
    attn_norm_gain,
    q_norm_gain,
    k_norm_gain,
    w_query,
    w_key,
    w_value,
    w_headgate,
    w_out,
    ffn_norm_gain,
    w_gate,
    w_up,
    w_down,
):
    micro_batches, row_count, model_width = inputs.shape
    both = range(micro_batches)
    n_dp = lax.axis_size("dp")
    head_idx = lax.axis_index("head")
    mp_idx = lax.axis_index("mp")
    dp_idx = lax.axis_index("dp")
    core = head_idx & 1
    plane_idx = head_idx * 2 + mp_idx
    seq_len = row_count * 8
    units = w_gate.shape[1] // 4
    head_at = head_idx[None].astype(jnp.int32)
    mp_at = mp_idx[None].astype(jnp.int32)
    order = Order()

    def after(value, *ahead):
        return lax.optimization_barrier((value, ahead))[0]

    halves = pack_attention(mp_at, w_query, w_key, w_value, w_headgate, w_out)
    attn_came = swap(halves[1], BIT_X)

    slot_ids = jnp.arange(micro_batches * n_dp, dtype=jnp.int32)
    slot_count = jnp.sum(
        jnp.where(seq_bucket[None, :] == slot_ids[:, None], seq_counts[None, :], 0), axis=1
    )
    own_pos = plane_idx * row_count + jnp.arange(row_count, dtype=jnp.int32)
    live = [slot_count[n * n_dp + dp_idx] for n in both]
    x_float = [inputs[n].astype(F32) for n in both]
    scale1 = [rms_scale(x) for x in x_float]
    normed1 = [x * scale for x, scale in zip(x_float, scale1)]
    xn1_own = [(n * attn_norm_gain).astype(BF16) for n in normed1]
    cot_live = [
        cotangent[n].astype(F32) * (own_pos < live[n]).astype(F32)[:, None] for n in both
    ]
    cot_own = [c.astype(BF16) for c in cot_live]
    xn1, xn2, cot, d_attn = ([None] * micro_batches for _ in range(4))
    xn1[0] = Gather(order, after(xn1_own[0], attn_came))
    is_first = mp_idx == 0
    attn_rows = jnp.concatenate(
        [pick(is_first, halves[0], attn_came), pick(is_first, attn_came, halves[0])], axis=0
    )
    w_attn = lax.all_gather(attn_rows, "dp", axis=0, tiled=True)
    xn1[0].second()
    xn1[0].third()

    quarters = after(pack_feed_forward(head_at, w_gate, w_up, w_down), xn1[0].pieces[1])
    traded = [quarters[0]] + [swap(quarters[r], r * 2) for r in (1, 2, 3)]
    parts = [[t[:, :units] for t in traded], [t[:, units:] for t in traded]]
    ffn_rows = [jnp.concatenate(reorder_by(part, head_idx), axis=0) for part in parts]
    ffn_rows = after(tuple(ffn_rows), attn_rows)
    w_ffn = [lax.all_gather(rows, "dp", axis=0, tiled=True) for rows in ffn_rows]

    xn1[1] = Gather(order, after(xn1_own[1], xn1[0].pieces[1]))
    tables = [attend_table(plane_idx, core, count) for count in live]
    table_cos, table_sin = rope_tables(jnp.arange(seq_len, dtype=jnp.int32), 64)
    table_cos, table_sin = table_cos[:, 0, :], table_sin[:, 0, :]
    cosine = jnp.concatenate([table_cos, table_cos], axis=1)
    sine = jnp.concatenate([-table_sin, table_sin], axis=1)
    fixed = (cosine, sine, q_norm_gain[None, :], k_norm_gain[None, :])
    att, out_sum = ([None] * micro_batches for _ in range(2))

    def attend(n):
        att[n] = order.run(
            lambda *pieces: attend_forward_call(tables[n], pieces, w_attn, *fixed), *xn1[n].pieces
        )

    order.need(xn1[1].second())
    cot[0] = Gather(order, after(cot_own[0], xn1[1].pieces[0]))
    attend(0)
    done = (xn1[1].third(), cot[0].second())
    out_sum[0] = Scatter(order, *after((att[0][6], att[0][7]), *done))
    order.need(*out_sum[0].add(att[0][4], att[0][5]), *done, w_ffn[0])
    out_sum[0].send_far()
    attend(1)
    done = (out_sum[0].take(), cot[0].third())
    out_sum[0].send_near()
    out_sum[1] = Scatter(order, *after((att[1][6], att[1][7]), *done))
    order.need(*done)

    hidden1, scale2, normed2 = ([None] * micro_batches for _ in range(3))

    def middle(n):
        hidden1[n] = x_float[n] + out_sum[n].result()
        scale2[n] = rms_scale(hidden1[n])
        normed2[n] = hidden1[n] * scale2[n]
        rows = (normed2[n] * ffn_norm_gain).astype(BF16)
        xn2[n] = Gather(order, rows)
        return rows

    rows = middle(0)
    order.need(*out_sum[1].add(after(att[1][4], rows), att[1][5]))
    out_sum[1].send_far()
    order.need(xn2[0].second(), out_sum[1].take())
    out_sum[1].send_near()
    order.need(xn2[0].third(), middle(1))
    cot[1] = Gather(order, after(cot_own[1], xn2[0].pieces[1]))

    feed = {}
    down, back = ([None] * micro_batches for _ in range(2))

    def feed_other(n):
        feed[n, 1] = order.run(
            lambda *v: feed_forward_call(v[0:2], v[2:4], *w_ffn), *xn2[n].pieces[2:], *cot[n].pieces[2:]
        )

    def feed_mine(n):
        feed[n, 0] = order.run(
            lambda *v: feed_forward_call(v[0:2], v[2:4], *w_ffn), *xn2[n].pieces[:2], *cot[n].pieces[:2]
        )
        return back[n].add(*feed[n, 0][3])

    d_hidden1 = [None] * micro_batches
    gain_ffn = []

    def turn(n):
        d_xn2 = back[n].result()
        gain_ffn.append(jnp.sum(d_xn2 * normed2[n], axis=0))
        d_hidden1[n] = cot_live[n] + norm_back(d_xn2, normed2[n], scale2[n], ffn_norm_gain)
        rows = d_hidden1[n].astype(BF16)
        d_attn[n] = Gather(order, rows)
        return rows

    def row_pieces(array):
        count = array.shape[0] // (2 * row_count)
        return [(array, 2 * row_count * k) for k in range(count)]

    def of_feed(which):
        return [p for n in both for side in (0, 1) for p in row_pieces(feed[n, side][which])]

    def rows_of(gathers):
        return [piece for gather in gathers for piece in gather.pieces]

    def grad_call(lefts, terms, *more):
        count = [len(left) for left in lefts]
        return order.run(
            lambda *v: weight_grad_call(
                n_dp,
                [list(v[sum(count[:k]) : sum(count[: k + 1])]) for k in range(len(lefts))],
                terms,
                *more,
            ),
            *[piece for left in lefts for piece in left],
        )

    def sum_over_dp(values):
        return lax.psum_scatter(values, "dp", scatter_dimension=0, tiled=True)

    def quarters_of(values):
        width = values.shape[1] // 4
        quarter = lambda k: lax.dynamic_slice_in_dim(values, k * width, width, 1)
        return [quarter(head_idx)] + [swap(quarter(head_idx ^ r), r * 2) for r in (1, 2, 3)]

    feed_other(0)
    done = (xn2[1].second(), cot[1].second())
    back[0] = Scatter(order, *after(feed[0, 1][3], *done))
    order.need(*done)
    sums = feed_mine(0)
    done = (xn2[1].third(), cot[1].third())
    down[0] = Scatter(order, *after(feed[0, 1][2], *done, *sums))
    back[0].send_far()
    order.need(*sums, *done)
    feed_other(1)
    done = (back[0].take(), *down[0].add(*feed[0, 0][2]))
    back[0].send_near()
    down[0].send_far()
    back[1] = Scatter(order, *after(feed[1, 1][3], *done))
    order.need(*done)
    order.need(*feed_mine(1), turn(0), down[0].take())
    back[1].send_far()
    grad_inner = grad_call([rows_of(xn2)], [(0, of_feed(1))])[0]
    done = (d_attn[0].second(), back[1].take())
    back[1].send_near()
    down[1] = Scatter(order, *after(feed[1, 1][2], *done))
    order.need(*done)
    grad_down = grad_call([rows_of(cot)], [(0, of_feed(0))])[0]
    grads_inner = sum_over_dp(order.pin(grad_inner))
    order.need(d_attn[0].third(), turn(1), *down[1].add(*feed[1, 0][2]))
    down[0].send_near()
    down[1].send_far()

    d_proj, gain_parts, rows_sum = ([None] * micro_batches for _ in range(3))

    def attend_back(n):
        out = order.run(
            lambda *v: attend_backward_call(
                tables[n], v, w_attn, att[n][0], att[n][1], att[n][2], *fixed
            ),
            *d_attn[n].pieces,
        )
        d_proj[n] = out[0]
        gain_parts[n] = (out[1][0], out[2][0])
        return out

    def finish(n):
        d_xn1 = rows_sum[n].result()
        return (d_hidden1[n] + norm_back(d_xn1, normed1[n], scale1[n], attn_norm_gain)).astype(BF16)

    outputs, input_grads = ([None] * micro_batches for _ in range(2))
    back_0 = attend_back(0)
    grads_down = sum_over_dp(order.pin(grad_down))
    done = (d_attn[1].second(), down[1].take())
    outputs[0] = (hidden1[0] + down[0].result()).astype(BF16)
    rows_sum[0] = Scatter(order, *after((back_0[5], back_0[6]), *done, outputs[0]))
    order.need(*done, outputs[0], *rows_sum[0].add(back_0[3], back_0[4]))
    grads_proj = grad_call([xn1[0].pieces], [(0, row_pieces(d_proj[0]))], None, None, False)[0]
    order.need(d_attn[1].third())
    grads_out = sum_over_dp(
        grad_call(
            [rows_of(d_attn)], [(0, [p for n in both for p in row_pieces(att[n][3])])]
        )[0]
    )
    rows_sum[0].send_far()
    down[1].send_near()
    inner_quarters = quarters_of(order.pin(grads_inner))
    order.need(grads_inner)
    back_1 = attend_back(1)
    done = (rows_sum[0].take(), *inner_quarters)
    rows_sum[0].send_near()
    rows_sum[1] = Scatter(order, *after((back_1[5], back_1[6]), *done))
    order.need(*done, grads_down)
    grads_proj, gain_rows = grad_call(
        [xn1[1].pieces], [(0, row_pieces(d_proj[1]))], w_attn, grads_proj, True, 528
    )
    grads_proj = sum_over_dp(grads_proj)
    outputs[1] = (hidden1[1] + down[1].result()).astype(BF16)
    input_grads[0] = finish(0)
    order.need(*rows_sum[1].add(*after((back_1[3], back_1[4]), outputs[1], input_grads[0])))
    rows_sum[1].send_far()
    down_quarters = quarters_of(after(grads_down, rows_sum[1].take()))
    rows_sum[1].send_near()
    input_grads[1] = finish(1)
    order.need(input_grads[1])
    grad_gate, grad_up, grad_down = order.run(
        lambda *v: unpack_feed_forward(head_at, v[:4], v[4:]), *inner_quarters, *down_quarters
    )

    gains = jnp.concatenate(
        [gain_rows[0] / attn_norm_gain, gain_ffn[0] + gain_ffn[1]]
        + [gain_parts[0][k] + gain_parts[1][k] for k in range(2)]
    ).reshape(-1, 128)
    gains = gains + swap(gains, BIT_C)
    for step in (1, 2):
        gains = gains + lax.ppermute(gains, "dp", [(i, i ^ step) for i in range(4)])
    gains = after(gains, input_grads[1])
    for bits in (BIT_X, BIT_Y):
        gains = gains + swap(gains, bits)
    gains = gains.reshape(-1)
    sum_attn, sum_gain_ffn = gains[:model_width], gains[model_width : 2 * model_width]
    sum_query, sum_key = gains[-256:-128], gains[-128:]

    def halves_of(values):
        left, right = values[:, :row_count], values[:, row_count:]
        return pick(is_first, left, right), swap(pick(is_first, right, left), BIT_X)

    grad_query, grad_key, grad_value, grad_headgate, grad_out = order.run(
        lambda *v: unpack_attention(mp_at, *v), *halves_of(grads_proj), *halves_of(grads_out)
    )
    return (
        jnp.stack(outputs),
        jnp.stack(input_grads),
        sum_attn,
        sum_query,
        sum_key,
        grad_query,
        grad_key,
        grad_value,
        grad_headgate,
        grad_out,
        sum_gain_ffn,
        grad_gate,
        grad_up,
        grad_down,
    )


def choose_local(mesh):
    if mesh.shape["head"] == 4 and mesh.shape["mp"] == 2 and mesh.shape["dp"] == 4:
        return local_plane
    return local


def solution(mesh):
    placed = (
        P(None, ("dp", "head", "mp"), None),
        P(None, ("dp", "head", "mp"), None),
        P(),
        P(),
        P(),
        P(),
        P(),
        P(("dp", "mp"), "head"),
        P(("dp", "mp"), "head"),
        P(("dp", "mp"), "head"),
        P(("dp", "mp"), "head"),
        P("head", ("dp", "mp")),
        P(),
        P(("dp", "head"), "mp"),
        P(("dp", "head"), "mp"),
        P("mp", ("dp", "head")),
    )
    return jax.shard_map(
        choose_local(mesh),
        mesh=mesh,
        in_specs=placed,
        out_specs=(
            P(None, ("dp", "head", "mp"), None),
            P(None, ("dp", "head", "mp"), None),
            P(),
            P(),
            P(),
            P(("dp", "mp"), "head"),
            P(("dp", "mp"), "head"),
            P(("dp", "mp"), "head"),
            P(("dp", "mp"), "head"),
            P("head", ("dp", "mp")),
            P(),
            P(("dp", "head"), "mp"),
            P(("dp", "head"), "mp"),
            P("mp", ("dp", "head")),
        ),
        check_vma=False,
    )
```

```python
import functools

import jax
import jax.numpy as jnp
from jax import lax
from jax.experimental import pallas as pl
from jax.experimental.pallas import tpu as pltpu
from jax.sharding import PartitionSpec as P

EPS = 1e-06
ROPE_BASE = 1000000.0
NEG_FILL = -1e30


def rms_scale(values):
    return lax.rsqrt(jnp.mean(values * values, axis=-1, keepdims=True) + EPS)


def norm_back(grad_out, normed, scale_rows, gain):
    d_normed = grad_out * gain
    return scale_rows * (d_normed - normed * jnp.mean(d_normed * normed, axis=-1, keepdims=True))


def rope_tables(positions, half):
    freq = jnp.power(ROPE_BASE, -jnp.arange(half, dtype=jnp.float32) / half)
    angle = positions.astype(jnp.float32)[:, None] * freq[None, :]
    return (jnp.cos(angle)[:, None, :], jnp.sin(angle)[:, None, :])


def rotate(values, cosine, sine):
    half = values.shape[-1] // 2
    first = values[..., :half]
    second = values[..., half:]
    return jnp.concatenate(
        [first * cosine - second * sine, second * cosine + first * sine], axis=-1
    )


def rotate_back(grads, cosine, sine):
    half = grads.shape[-1] // 2
    first = grads[..., :half]
    second = grads[..., half:]
    return jnp.concatenate(
        [first * cosine + second * sine, second * cosine - first * sine], axis=-1
    )


def masked_scores(q_group, key_piece, query_pos, key_pos, live_count):
    scores = jnp.einsum("qhgd,khd->hgqk", q_group, key_piece, preferred_element_type=jnp.float32)
    allowed = (key_pos[None, :] <= query_pos[:, None]) & (key_pos[None, :] < live_count)
    return (scores, allowed)


def split_keys(keys, values, key_pos, key_block):
    n_blocks = keys.shape[0] // key_block
    key_pieces = keys.reshape(n_blocks, key_block, keys.shape[1], keys.shape[2])
    value_pieces = values.reshape(n_blocks, key_block, values.shape[1], values.shape[2])
    return (key_pieces, value_pieces, key_pos.reshape(n_blocks, key_block))


def attend_forward(q_group, keys, values, query_pos, key_pos, live_count, key_block):
    n_query, kv_here, group_size, head_dim = q_group.shape
    key_pieces, value_pieces, pos_pieces = split_keys(keys, values, key_pos, key_block)

    def stats(carry, piece):
        row_max, row_total = carry
        key_piece, piece_pos = piece
        scores, allowed = masked_scores(q_group, key_piece, query_pos, piece_pos, live_count)
        scores = jnp.where(allowed, scores, NEG_FILL)
        new_max = jnp.maximum(row_max, jnp.max(scores, axis=-1))
        kept_exp = jnp.where(allowed, jnp.exp(scores - new_max[..., None]), 0.0)
        row_total = row_total * jnp.exp(row_max - new_max) + jnp.sum(kept_exp, axis=-1)
        return ((new_max, row_total), None)

    start = (
        jnp.full((kv_here, group_size, n_query), NEG_FILL, jnp.float32),
        jnp.zeros((kv_here, group_size, n_query), jnp.float32),
    )
    (row_max, row_total), unused = lax.scan(stats, start, (key_pieces, pos_pieces))
    log_total = row_max + jnp.log(row_total)

    def weigh(acc, piece):
        key_piece, value_piece, piece_pos = piece
        scores, allowed = masked_scores(q_group, key_piece, query_pos, piece_pos, live_count)
        prob_low = jnp.where(allowed, jnp.exp(scores - log_total[..., None]), 0.0).astype(
            jnp.bfloat16
        )
        acc = acc + jnp.einsum(
            "hgqk,khd->qhgd", prob_low, value_piece, preferred_element_type=jnp.float32
        )
        return (acc, None)

    attn_o, unused = lax.scan(
        weigh, jnp.zeros(q_group.shape, jnp.float32), (key_pieces, value_pieces, pos_pieces)
    )
    return (attn_o, log_total)


def attend_backward(
    q_group, keys, values, query_pos, key_pos, live_count, key_block, log_total, d_out, delta
):
    kv_here = keys.shape[1]
    head_dim = keys.shape[2]
    key_pieces, value_pieces, pos_pieces = split_keys(keys, values, key_pos, key_block)

    def backstep(d_query, piece):
        key_piece, value_piece, piece_pos = piece
        scores, allowed = masked_scores(q_group, key_piece, query_pos, piece_pos, live_count)
        probs = jnp.where(allowed, jnp.exp(scores - log_total[..., None]), 0.0)
        d_probs = jnp.einsum(
            "qhgd,khd->hgqk", d_out, value_piece, preferred_element_type=jnp.float32
        )
        d_scores = (probs * (d_probs - delta[..., None])).astype(jnp.bfloat16)
        d_query = d_query + jnp.einsum(
            "hgqk,khd->qhgd", d_scores, key_piece, preferred_element_type=jnp.float32
        )
        d_key = jnp.einsum("hgqk,qhgd->khd", d_scores, q_group, preferred_element_type=jnp.float32)
        d_value = jnp.einsum(
            "hgqk,qhgd->khd", probs.astype(jnp.bfloat16), d_out, preferred_element_type=jnp.float32
        )
        return (d_query, (d_key, d_value))

    d_query, (d_key, d_value) = lax.scan(
        backstep, jnp.zeros(q_group.shape, jnp.float32), (key_pieces, value_pieces, pos_pieces)
    )
    return (d_query, d_key.reshape(-1, kv_here * head_dim), d_value.reshape(-1, kv_here * head_dim))


def gather_weights(w_query, w_key, w_value, w_headgate, w_out, w_gate, w_up, w_down):
    attn_parts = (
        lax.all_gather(w_query, ("dp", "mp"), axis=0, tiled=True),
        lax.all_gather(w_key, ("dp", "mp"), axis=0, tiled=True),
        lax.all_gather(w_value, ("dp", "mp"), axis=0, tiled=True),
        lax.all_gather(w_headgate, ("dp", "mp"), axis=0, tiled=True),
        lax.all_gather(w_out, ("dp", "mp"), axis=1, tiled=True),
    )
    ffn_parts = (
        lax.all_gather(w_gate, ("dp", "head"), axis=0, tiled=True),
        lax.all_gather(w_up, ("dp", "head"), axis=0, tiled=True),
        lax.all_gather(w_down, ("dp", "head"), axis=1, tiled=True),
    )
    return tuple(attn_parts) + tuple(ffn_parts)


def reduce_grads(g_query, g_key, g_value, g_headgate, g_out, g_gate, g_up, g_down):
    attn_parts = (
        lax.psum_scatter(
            g_query.astype(jnp.bfloat16), ("dp", "mp"), scatter_dimension=0, tiled=True
        ).astype(jnp.float32),
        lax.psum_scatter(
            g_key.astype(jnp.bfloat16), ("dp", "mp"), scatter_dimension=0, tiled=True
        ).astype(jnp.float32),
        lax.psum_scatter(
            g_value.astype(jnp.bfloat16), ("dp", "mp"), scatter_dimension=0, tiled=True
        ).astype(jnp.float32),
        lax.psum_scatter(
            g_headgate.astype(jnp.bfloat16), ("dp", "mp"), scatter_dimension=0, tiled=True
        ).astype(jnp.float32),
        lax.psum_scatter(
            g_out.astype(jnp.bfloat16), ("dp", "mp"), scatter_dimension=1, tiled=True
        ).astype(jnp.float32),
    )
    ffn_parts = (
        lax.psum_scatter(
            g_gate.astype(jnp.bfloat16), ("dp", "head"), scatter_dimension=0, tiled=True
        ).astype(jnp.float32),
        lax.psum_scatter(
            g_up.astype(jnp.bfloat16), ("dp", "head"), scatter_dimension=0, tiled=True
        ).astype(jnp.float32),
        lax.psum_scatter(
            g_down.astype(jnp.bfloat16), ("dp", "head"), scatter_dimension=1, tiled=True
        ).astype(jnp.float32),
    )
    return tuple(attn_parts) + tuple(ffn_parts)


def local(
    inputs,
    cotangent,
    seq_counts,
    seq_bucket,
    attn_norm_gain,
    q_norm_gain,
    k_norm_gain,
    w_query,
    w_key,
    w_value,
    w_headgate,
    w_out,
    ffn_norm_gain,
    w_gate,
    w_up,
    w_down,
):
    micro_batches, row_count, model_width = inputs.shape
    n_head = lax.axis_size("head")
    n_mp = lax.axis_size("mp")
    n_dp = lax.axis_size("dp")
    head_idx = lax.axis_index("head")
    mp_idx = lax.axis_index("mp")
    dp_idx = lax.axis_index("dp")
    head_dim = q_norm_gain.shape[0]
    q_heads = w_query.shape[1] // head_dim
    kv_heads = w_key.shape[1] // head_dim
    group_size = q_heads // kv_heads
    q_scale = head_dim ** (-0.5)
    seq_len = row_count * n_head * n_mp
    key_block = min(512, seq_len)
    n_query = n_head * row_count
    slot_ids = jnp.arange(micro_batches * n_dp, dtype=jnp.int32)
    slot_count = jnp.sum(
        jnp.where(seq_bucket[None, :] == slot_ids[:, None], seq_counts[None, :], 0), axis=1
    )
    local_idx = jnp.arange(row_count, dtype=jnp.int32)
    own_pos = head_idx * n_mp * row_count + mp_idx * row_count + local_idx
    query_idx = jnp.arange(n_query, dtype=jnp.int32)
    query_pos = (
        query_idx // row_count * n_mp * row_count + mp_idx * row_count + query_idx % row_count
    )
    key_idx = jnp.arange(seq_len, dtype=jnp.int32)
    key_pos = (
        key_idx % n_query // row_count * n_mp * row_count
        + key_idx // n_query * row_count
        + key_idx % row_count
    )
    rope_cos, rope_sin = rope_tables(query_pos, head_dim // 2)
    grad_total = None
    gain_attn = jnp.zeros((model_width,), jnp.float32)
    gain_query = jnp.zeros((head_dim,), jnp.float32)
    gain_key = jnp.zeros((head_dim,), jnp.float32)
    gain_ffn = jnp.zeros((model_width,), jnp.float32)
    outputs = []
    input_grads = []
    for micro_batch in range(micro_batches):
        weights = gather_weights(w_query, w_key, w_value, w_headgate, w_out, w_gate, w_up, w_down)
        wq_full, wk_full, wv_full, wg_full, wo_full, wgate_full, wup_full, wdown_full = weights
        live_count = slot_count[micro_batch * n_dp + dp_idx]
        x_float = inputs[micro_batch].astype(jnp.float32)
        scale1 = rms_scale(x_float)
        normed1 = x_float * scale1
        xn1 = (normed1 * attn_norm_gain).astype(jnp.bfloat16)
        gathered_rows = lax.all_gather(xn1, "head", axis=0, tiled=True)
        q_raw = jnp.dot(gathered_rows, wq_full, preferred_element_type=jnp.float32).reshape(
            n_query, q_heads, head_dim
        )
        k_raw = jnp.dot(gathered_rows, wk_full, preferred_element_type=jnp.float32).reshape(
            n_query, kv_heads, head_dim
        )
        value_low = jnp.dot(gathered_rows, wv_full, preferred_element_type=jnp.float32).astype(
            jnp.bfloat16
        )
        gate_logit = jnp.dot(gathered_rows, wg_full, preferred_element_type=jnp.float32)
        q_rms = rms_scale(q_raw)
        q_hat = q_raw * q_rms
        query_low = (rotate(q_hat * q_norm_gain, rope_cos, rope_sin) * q_scale).astype(jnp.bfloat16)
        k_rms = rms_scale(k_raw)
        k_hat = k_raw * k_rms
        key_low = rotate(k_hat * k_norm_gain, rope_cos, rope_sin).astype(jnp.bfloat16)
        all_keys, all_values = (
            lax.all_gather(key_low.reshape(n_query, kv_heads * head_dim), "mp", axis=0, tiled=True),
            lax.all_gather(value_low, "mp", axis=0, tiled=True),
        )
        all_keys = all_keys.reshape(seq_len, kv_heads, head_dim)
        all_values = all_values.reshape(seq_len, kv_heads, head_dim)
        q_group = query_low.reshape(n_query, kv_heads, group_size, head_dim)
        attn_o, log_total = attend_forward(
            q_group, all_keys, all_values, query_pos, key_pos, live_count, key_block
        )
        gate_prob = jax.nn.sigmoid(gate_logit)
        attn_heads = attn_o.reshape(n_query, q_heads, head_dim)
        gated = (
            (attn_heads * gate_prob[..., None])
            .reshape(n_query, q_heads * head_dim)
            .astype(jnp.bfloat16)
        )
        attn_sum = lax.psum_scatter(
            jnp.dot(gated, wo_full, preferred_element_type=jnp.float32).astype(jnp.bfloat16),
            "head",
            scatter_dimension=0,
            tiled=True,
        ).astype(jnp.float32)
        hidden1 = x_float + attn_sum
        scale2 = rms_scale(hidden1)
        normed2 = hidden1 * scale2
        xn2 = (normed2 * ffn_norm_gain).astype(jnp.bfloat16)
        live = (own_pos < live_count).astype(jnp.float32)[:, None]
        cot_live = cotangent[micro_batch].astype(jnp.float32) * live
        ffn_in, cot_rows = (
            lax.all_gather(xn2, "mp", axis=0, tiled=True),
            lax.all_gather(cot_live.astype(jnp.bfloat16), "mp", axis=0, tiled=True),
        )
        gate_pre = jnp.dot(ffn_in, wgate_full, preferred_element_type=jnp.float32)
        up_pre = jnp.dot(ffn_in, wup_full, preferred_element_type=jnp.float32)
        gate_sig = jax.nn.sigmoid(gate_pre)
        gate_act = gate_pre * gate_sig
        hidden = (gate_act * up_pre).astype(jnp.bfloat16)
        ffn_sum = lax.psum_scatter(
            jnp.dot(hidden, wdown_full, preferred_element_type=jnp.float32).astype(jnp.bfloat16),
            "mp",
            scatter_dimension=0,
            tiled=True,
        ).astype(jnp.float32)
        outputs.append((hidden1 + ffn_sum).astype(jnp.bfloat16))
        d_hidden = jnp.einsum("rd,fd->rf", cot_rows, wdown_full, preferred_element_type=jnp.float32)
        grad_down = jnp.einsum("rf,rd->fd", hidden, cot_rows, preferred_element_type=jnp.float32)
        d_up = (d_hidden * gate_act).astype(jnp.bfloat16)
        d_gate = (d_hidden * up_pre * gate_sig * (1.0 + gate_pre * (1.0 - gate_sig))).astype(
            jnp.bfloat16
        )
        grad_gate = jnp.einsum("rd,rf->df", ffn_in, d_gate, preferred_element_type=jnp.float32)
        grad_up = jnp.einsum("rd,rf->df", ffn_in, d_up, preferred_element_type=jnp.float32)
        ffn_term = jnp.einsum(
            "rf,df->rd", d_gate, wgate_full, preferred_element_type=jnp.float32
        ) + jnp.einsum("rf,df->rd", d_up, wup_full, preferred_element_type=jnp.float32)
        d_xn2 = lax.psum_scatter(
            ffn_term.astype(jnp.bfloat16), "mp", scatter_dimension=0, tiled=True
        ).astype(jnp.float32)
        gain_ffn = gain_ffn + jnp.sum(d_xn2 * normed2, axis=0)
        d_hidden1 = cot_live + norm_back(d_xn2, normed2, scale2, ffn_norm_gain)
        d_attn = lax.all_gather(d_hidden1.astype(jnp.bfloat16), "head", axis=0, tiled=True)
        d_gated = jnp.einsum(
            "rd,cd->rc", d_attn, wo_full, preferred_element_type=jnp.float32
        ).reshape(n_query, q_heads, head_dim)
        grad_out = jnp.einsum("rc,rd->cd", gated, d_attn, preferred_element_type=jnp.float32)
        d_out_low = (d_gated * gate_prob[..., None]).astype(jnp.bfloat16)
        d_gate_logit = (
            jnp.sum(d_gated * attn_heads, axis=-1) * gate_prob * (1.0 - gate_prob)
        ).astype(jnp.bfloat16)
        grad_headgate = jnp.einsum(
            "rd,rc->dc", gathered_rows, d_gate_logit, preferred_element_type=jnp.float32
        )
        d_out_group = d_out_low.reshape(n_query, kv_heads, group_size, head_dim)
        delta = jnp.transpose(jnp.sum(d_out_group.astype(jnp.float32) * attn_o, axis=-1), (1, 2, 0))
        d_query, d_key_all, d_value_all = attend_backward(
            q_group,
            all_keys,
            all_values,
            query_pos,
            key_pos,
            live_count,
            key_block,
            log_total,
            d_out_group,
            delta,
        )
        d_key_own, d_value_own = (
            lax.psum_scatter(
                d_key_all.astype(jnp.bfloat16), "mp", scatter_dimension=0, tiled=True
            ).astype(jnp.float32),
            lax.psum_scatter(
                d_value_all.astype(jnp.bfloat16), "mp", scatter_dimension=0, tiled=True
            ).astype(jnp.float32),
        )
        dq_norm = rotate_back(
            (d_query * q_scale).reshape(n_query, q_heads, head_dim), rope_cos, rope_sin
        )
        gain_query = gain_query + jnp.sum(dq_norm * q_hat, axis=(0, 1))
        d_q_raw = (
            norm_back(dq_norm, q_hat, q_rms, q_norm_gain)
            .reshape(n_query, q_heads * head_dim)
            .astype(jnp.bfloat16)
        )
        dk_norm = rotate_back(d_key_own.reshape(n_query, kv_heads, head_dim), rope_cos, rope_sin)
        gain_key = gain_key + jnp.sum(dk_norm * k_hat, axis=(0, 1))
        d_k_raw = (
            norm_back(dk_norm, k_hat, k_rms, k_norm_gain)
            .reshape(n_query, kv_heads * head_dim)
            .astype(jnp.bfloat16)
        )
        d_value_low = d_value_own.astype(jnp.bfloat16)
        grad_query = jnp.einsum(
            "rd,rc->dc", gathered_rows, d_q_raw, preferred_element_type=jnp.float32
        )
        grad_key = jnp.einsum(
            "rd,rc->dc", gathered_rows, d_k_raw, preferred_element_type=jnp.float32
        )
        grad_value = jnp.einsum(
            "rd,rc->dc", gathered_rows, d_value_low, preferred_element_type=jnp.float32
        )
        attn_term = jnp.einsum("rc,dc->rd", d_q_raw, wq_full, preferred_element_type=jnp.float32)
        attn_term = attn_term + jnp.einsum(
            "rc,dc->rd", d_k_raw, wk_full, preferred_element_type=jnp.float32
        )
        attn_term = attn_term + jnp.einsum(
            "rc,dc->rd", d_value_low, wv_full, preferred_element_type=jnp.float32
        )
        attn_term = attn_term + jnp.einsum(
            "rc,dc->rd", d_gate_logit, wg_full, preferred_element_type=jnp.float32
        )
        d_xn1 = lax.psum_scatter(
            attn_term.astype(jnp.bfloat16), "head", scatter_dimension=0, tiled=True
        ).astype(jnp.float32)
        gain_attn = gain_attn + jnp.sum(d_xn1 * normed1, axis=0)
        input_grads.append(
            (d_hidden1 + norm_back(d_xn1, normed1, scale1, attn_norm_gain)).astype(jnp.bfloat16)
        )
        batch_grads = reduce_grads(
            grad_query, grad_key, grad_value, grad_headgate, grad_out, grad_gate, grad_up, grad_down
        )
        if grad_total is None:
            grad_total = batch_grads
        else:
            grad_total = tuple((a + b for a, b in zip(grad_total, batch_grads)))
    sum_attn, sum_query, sum_key, sum_ffn = lax.psum(
        (gain_attn, gain_query, gain_key, gain_ffn), ("dp", "head", "mp")
    )
    return (
        jnp.stack(outputs),
        jnp.stack(input_grads),
        sum_attn,
        sum_query,
        sum_key,
        grad_total[0],
        grad_total[1],
        grad_total[2],
        grad_total[3],
        grad_total[4],
        sum_ffn,
        grad_total[5],
        grad_total[6],
        grad_total[7],
    )


PLANE = ("head", "mp")
BIT_X, BIT_C, BIT_Y = 1, 2, 4
NT = (((1,), (1,)), ((), ()))
NN = (((1,), (0,)), ((), ()))
TN = (((0,), (0,)), ((), ()))
F32 = jnp.float32
BF16 = jnp.bfloat16
COST_SHARE = 0.2
LATE_SHARE = 0.1


def dot(left, right, dims=NN):
    return lax.dot_general(left, right, dims, preferred_element_type=F32)


def swap(values, bits):
    return lax.ppermute(values, PLANE, [(i, i ^ bits) for i in range(8)])


def swap_mixed(values, core0, core1):
    return lax.ppermute(
        values, PLANE, [(i, i ^ (core1 if i & BIT_C else core0)) for i in range(8)]
    )


class Order:
    def __init__(self):
        self.ahead = []
        self.last = None

    def need(self, *values):
        self.ahead.extend(values)

    def pin(self, value):
        if self.last is None:
            return value
        return lax.optimization_barrier((value, self.last))[0]

    def run(self, op, *operands):
        if self.ahead:
            operands = lax.optimization_barrier((tuple(operands), tuple(self.ahead)))[0]
        out = op(*operands)
        self.last = out[0] if isinstance(out, (tuple, list)) else out
        self.ahead = [self.last]
        return out


class Gather:
    def __init__(self, order, rows):
        self.order = order
        self.rows = rows
        self.came = swap_mixed(rows, BIT_X, BIT_Y)

    def second(self):
        came = self.order.pin(self.came)
        near = jnp.concatenate([self.rows, came], axis=0)
        self.came = swap_mixed(near, BIT_Y, BIT_X)
        self.pieces = [near, None, swap(near, BIT_C), None]
        return near

    def third(self):
        far = self.order.pin(self.came)
        self.pieces[1], self.pieces[3] = far, swap(far, BIT_C)
        return far


def add_pieces_kernel(first, second, out):
    out[...] = (first[...].astype(F32) + second[...].astype(F32)).astype(BF16)


def add_pieces(first, second):
    count, width = first.shape
    block = pl.BlockSpec((count // 4, width), lambda i: (i, 0))
    return pl.pallas_call(
        add_pieces_kernel,
        grid=(4,),
        in_specs=[block] * 2,
        out_specs=block,
        out_shape=jax.ShapeDtypeStruct((count, width), BF16),
        cost_estimate=pl.CostEstimate(
            flops=count * width, bytes_accessed=6 * count * width, transcendentals=0
        ),
        name="add_pieces",
    )(first, second)


class Scatter:
    def __init__(self, order, near, far):
        self.order = order
        self.came = (swap(near, BIT_C), swap(far, BIT_C))

    def add(self, near, far):
        near_came, far_came = self.order.pin(self.came)
        self.near = (near, near_came)
        self.far = add_pieces(far, far_came)
        return (self.far,)

    def send_far(self):
        self.came = swap_mixed(self.order.pin(self.far), BIT_Y, BIT_X)

    def take(self):
        self.second_came = self.order.pin(self.came)
        terms = (*self.near, self.second_came)
        half = terms[0].shape[0] // 2
        low, high = [sum(t[part].astype(F32) for t in terms) for part in (slice(0, half), slice(half, None))]
        self.kept = low
        self.sent = high.astype(BF16)
        return self.sent

    def send_near(self):
        self.came = swap_mixed(self.order.pin(self.sent), BIT_X, BIT_Y)

    def result(self):
        return self.kept + self.order.pin(self.came).astype(F32)

    def terms(self):
        return (*self.near, self.second_came, self.order.pin(self.came))


def norm_rope(raw, gain, cosine, sine):
    scale_rows = lax.rsqrt(jnp.mean(raw * raw, axis=-1, keepdims=True) + EPS)
    hat = raw * scale_rows
    turned = hat * gain
    return (turned * cosine + pltpu.roll(turned, 64, 1) * sine, hat, scale_rows)


def norm_rope_back(grad, hat, scale_rows, gain, cosine, sine):
    grad_n = grad * cosine - pltpu.roll(grad, 64, 1) * sine
    gain_part = jnp.sum(grad_n * hat, axis=0, keepdims=True)
    scaled = grad_n * gain
    raw = scale_rows * (scaled - hat * jnp.mean(scaled * hat, axis=-1, keepdims=True))
    return (raw, gain_part)


def two_lanes(first, second, shape):
    lane = lax.broadcasted_iota(jnp.int32, shape, 1)
    return jnp.where(lane == 0, first, jnp.where(lane == 1, second, 0.0))


def cost(flops, traffic, transcendentals=0, share=COST_SHARE):
    return pl.CostEstimate(
        flops=int(flops / share),
        bytes_accessed=int(traffic / share),
        transcendentals=int(transcendentals / share),
    )


SLOT, LIVE, BLOCK, PLACE = 0, 8, 9, 41


def attend_table(plane_idx, core, live_count):
    slot = jnp.arange(8, dtype=jnp.int32)
    across, low, high = slot >> 2, slot & 1, (slot >> 1) & 1
    x_first = (core ^ across) == 0
    apart = across * 2 + jnp.where(x_first, low + 4 * high, high + 4 * low)
    place = apart ^ plane_idx
    slots = jnp.sum(jnp.where(place[None, :] == slot[:, None], slot[None, :], 0), axis=1)
    steps = jnp.arange(8, dtype=jnp.int32)
    blocks = []
    for piece in range(4):
        one, two = place[2 * piece], place[2 * piece + 1]
        first = jnp.where(one < two, 0, 1)
        blocks.append(jnp.where(steps >= jnp.maximum(one, two), 1 - first, first))
    return jnp.concatenate([slots, live_count[None]] + blocks + [place]).astype(jnp.int32)


def take_piece(slot, pieces):
    near = jnp.where(slot < 2, pieces[0][...], pieces[1][...])
    far = jnp.where(slot < 6, pieces[2][...], pieces[3][...])
    return jnp.where(slot < 4, near, far)


def walk_tiles(step, rows, live, add_tile):
    pairs = step // 2
    whole = jnp.minimum(pairs, live // (2 * rows))

    def tile(index, carry):
        add_tile(pl.multiple_of(index * 2 * rows, 2 * rows), 2 * rows, False)
        return carry

    lax.fori_loop(0, whole, tile, 0)
    odd = step % 2 == 1
    edge = pl.multiple_of(pairs * 2 * rows, 2 * rows)

    @pl.when((whole < pairs) & (whole * 2 * rows < live))
    def _():
        add_tile(pl.multiple_of(whole * 2 * rows, 2 * rows), 2 * rows, True)

    @pl.when(odd & (edge < live))
    def _():
        add_tile(edge, 2 * rows, True)

    @pl.when(jnp.logical_not(odd) & (edge < live))
    def _():
        add_tile(edge, rows, True)


def attend_forward_kernel(table, *refs):
    x_pieces, (weights, cosine, sine, q_gain, k_gain) = refs[:4], refs[4:9]
    proj, attn_o, lse, gated = refs[9:13]
    out_pieces, (keys, values, acc) = refs[13:17], refs[17:]
    step = pl.program_id(0)
    rows = proj.shape[0]
    live, slot = table[LIVE], table[SLOT + step]
    cos_b, sin_b = cosine[...], sine[...]
    here = pl.multiple_of(step * rows, rows)
    proj[...] = dot(take_piece(slot, x_pieces), weights[:, 0:640])
    key, _, _ = norm_rope(proj[:, 256:384], k_gain[...], cos_b, sin_b)
    keys[pl.ds(here, rows), :] = key.astype(BF16)
    values[pl.ds(here, rows), 0:128] = proj[:, 384:512].astype(BF16)
    values[pl.ds(here, rows), 128:256] = jnp.ones((rows, 128), BF16)
    q_scale = 128**-0.5
    first, _, _ = norm_rope(proj[:, 0:128], q_gain[...], cos_b, sin_b)
    second, _, _ = norm_rope(proj[:, 128:256], q_gain[...], cos_b, sin_b)
    query = (jnp.concatenate([first, second], axis=0) * q_scale).astype(BF16)

    def add_tile(there, count, masked):
        weight = jnp.exp(dot(query, keys[pl.ds(there, count), :], NT))
        if masked:
            row = lax.broadcasted_iota(jnp.int32, (2 * rows, count), 0)
            place = there + lax.broadcasted_iota(jnp.int32, (2 * rows, count), 1)
            allowed = (place <= here + jnp.where(row >= rows, row - rows, row)) & (place < live)
            weight = jnp.where(allowed, weight, 0.0)
        acc[...] += dot(weight.astype(BF16), values[pl.ds(there, count), :])

    acc[...] = jnp.zeros_like(acc)
    walk_tiles(step, rows, live, add_tile)
    total = acc[:, 128:129]
    out = acc[:, 0:128] / total
    log_total = jnp.log(total)
    gate0 = jax.nn.sigmoid(proj[:, 512:513])
    gate1 = jax.nn.sigmoid(proj[:, 513:514])
    attn_o[:, 0:128] = out[:rows]
    attn_o[:, 128:256] = out[rows:]
    gated[:, 0:128] = (out[:rows] * gate0).astype(BF16)
    gated[:, 128:256] = (out[rows:] * gate1).astype(BF16)
    lse[...] = two_lanes(log_total[:rows], log_total[rows:], (rows, 128))
    part = dot(gated[...], weights[:, 640:896], NT).astype(BF16)
    for piece in range(4):

        @pl.when(slot // 2 == piece)
        def _():
            out_pieces[piece][...] = part


def attend_backward_kernel(table, *refs):
    d_pieces = refs[:4]
    weights, proj, attn_o, lse, cosine, sine, q_gain, k_gain = refs[4:12]
    d_proj, gain_q, gain_k = refs[12:15]
    back_pieces = refs[15:19]
    keys, keys_t, values, k_raw, d_keys, d_values, d_query, d_held = refs[19:]
    step = pl.program_id(0)
    rows = proj.shape[0]
    live = table[LIVE]
    q_scale = 128**-0.5

    @pl.when(step == 0)
    def _():
        gain_q[...] = jnp.zeros_like(gain_q)
        gain_k[...] = jnp.zeros_like(gain_k)

    @pl.when(step < 8)
    def _():
        here = pl.multiple_of(step * rows, rows)
        slot = table[SLOT + step]
        cos_b, sin_b = cosine[pl.ds(here, rows), :], sine[pl.ds(here, rows), :]
        raw_key = proj[:, 256:384]
        k_raw[pl.ds(here, rows), :] = raw_key
        key, _, _ = norm_rope(raw_key, k_gain[...], cos_b, sin_b)
        key = key.astype(BF16)
        keys[pl.ds(here, rows), :] = key
        keys_t[:, pl.ds(here, rows)] = key.T
        values[pl.ds(here, rows), :] = proj[:, 384:512].astype(BF16)
        d_keys[pl.ds(here, rows), :] = jnp.zeros((rows, 128), F32)
        d_values[pl.ds(here, rows), :] = jnp.zeros((rows, 128), F32)
        d_query[...] = jnp.zeros_like(d_query)
        first, hat0, scale0 = norm_rope(proj[:, 0:128], q_gain[...], cos_b, sin_b)
        second, hat1, scale1 = norm_rope(proj[:, 128:256], q_gain[...], cos_b, sin_b)
        query = (jnp.concatenate([first, second], axis=0) * q_scale).astype(BF16)
        gate0 = jax.nn.sigmoid(proj[:, 512:513])
        gate1 = jax.nn.sigmoid(proj[:, 513:514])
        d_gated = dot(take_piece(slot, d_pieces), weights[:, 640:896])
        dg0, dg1 = d_gated[:, 0:128], d_gated[:, 128:256]
        out0, out1 = attn_o[:, 0:128], attn_o[:, 128:256]
        do0, do1 = (dg0 * gate0).astype(BF16), (dg1 * gate1).astype(BF16)
        logit0 = jnp.sum(dg0 * out0, axis=-1, keepdims=True) * gate0 * (1.0 - gate0)
        logit1 = jnp.sum(dg1 * out1, axis=-1, keepdims=True) * gate1 * (1.0 - gate1)
        d_held[pl.ds(here, rows), 512:640] = two_lanes(logit0, logit1, (rows, 128)).astype(BF16)
        delta0 = jnp.sum(do0.astype(F32) * out0, axis=-1, keepdims=True)
        delta1 = jnp.sum(do1.astype(F32) * out1, axis=-1, keepdims=True)
        delta_t = two_lanes(delta0, delta1, (rows, 128)).T
        delta = jnp.concatenate([delta_t[0:1], delta_t[1:2]], axis=1)
        lse_t = lse[...].T
        log_total = jnp.concatenate([lse_t[0:1], lse_t[1:2]], axis=1)
        d_out = jnp.concatenate([do0, do1], axis=0)

        def add_tile(there, count, masked):
            here_keys = pl.ds(there, count)
            scores = dot(keys[here_keys, :], query, NT)
            probs = jnp.exp(scores - log_total)
            if masked:
                place = there + lax.broadcasted_iota(jnp.int32, (count, 2 * rows), 0)
                q_col = lax.broadcasted_iota(jnp.int32, (count, 2 * rows), 1)
                q_place = here + jnp.where(q_col >= rows, q_col - rows, q_col)
                probs = jnp.where((place <= q_place) & (place < live), probs, 0.0)
            d_probs = dot(values[here_keys, :], d_out, NT)
            d_scores = (probs * (d_probs - delta)).astype(BF16)
            d_values[here_keys, :] += dot(probs.astype(BF16), d_out)
            d_keys[here_keys, :] += dot(d_scores, query)
            d_query[...] += dot(keys_t[:, here_keys], d_scores)

        walk_tiles(step, rows, live, add_tile)
        grads = d_query[...].T * q_scale
        raw0, part0 = norm_rope_back(grads[:rows], hat0, scale0, q_gain[...], cos_b, sin_b)
        raw1, part1 = norm_rope_back(grads[rows:], hat1, scale1, q_gain[...], cos_b, sin_b)
        d_held[pl.ds(here, rows), 0:128] = raw0.astype(BF16)
        d_held[pl.ds(here, rows), 128:256] = raw1.astype(BF16)
        gain_q[0:1, :] += part0 + part1

    @pl.when(step >= 8)
    def _():
        slot = (step - 4) % 8
        there = pl.multiple_of(table[PLACE + slot] * rows, rows)
        cos_k, sin_k = cosine[pl.ds(there, rows), :], sine[pl.ds(there, rows), :]
        _, hat, scale_rows = norm_rope(k_raw[pl.ds(there, rows), :], k_gain[...], cos_k, sin_k)
        raw, part = norm_rope_back(
            d_keys[pl.ds(there, rows), :], hat, scale_rows, k_gain[...], cos_k, sin_k
        )
        gain_k[0:1, :] += part
        d_held[pl.ds(there, rows), 256:384] = raw.astype(BF16)
        d_held[pl.ds(there, rows), 384:512] = d_values[pl.ds(there, rows), :].astype(BF16)
        d_block = d_held[pl.ds(there, rows), :]
        d_proj[...] = d_block
        back = dot(d_block, weights[:, 0:640], NT).astype(BF16)
        for piece in range(4):

            @pl.when(slot // 2 == piece)
            def _():
                back_pieces[piece][...] = back


def attend_forward_call(table, pieces, weights, cosine, sine, q_gain, k_gain):
    seq_len, width = cosine.shape[0], weights.shape[0]
    rows = seq_len // 8
    by_slot = lambda i, t: (t[SLOT + i], 0)
    by_place = lambda i, t: (i, 0)
    fixed = lambda i, t: (0, 0)
    whole = [
        pl.BlockSpec((rows, width), lambda i, t, k=k: (t[BLOCK + 8 * k + i], 0)) for k in range(4)
    ]
    pairs = seq_len * (seq_len + rows)
    return pl.pallas_call(
        attend_forward_kernel,
        grid_spec=pltpu.PrefetchScalarGridSpec(
            num_scalar_prefetch=1,
            grid=(8,),
            in_specs=whole
            + [
                pl.BlockSpec(weights.shape, fixed, pipeline_mode=pl.Buffered(1)),
                pl.BlockSpec((rows, 128), by_place),
                pl.BlockSpec((rows, 128), by_place),
                pl.BlockSpec((1, 128), fixed),
                pl.BlockSpec((1, 128), fixed),
            ],
            out_specs=[
                pl.BlockSpec((rows, 640), by_slot),
                pl.BlockSpec((rows, 256), by_slot),
                pl.BlockSpec((rows, 128), by_slot),
                pl.BlockSpec((rows, 256), by_slot),
            ]
            + whole,
            scratch_shapes=[
                pltpu.VMEM((seq_len, 128), BF16),
                pltpu.VMEM((seq_len, 256), BF16),
                pltpu.VMEM((2 * rows, 256), F32),
            ],
        ),
        out_shape=[
            jax.ShapeDtypeStruct((seq_len, 640), F32),
            jax.ShapeDtypeStruct((seq_len, 256), F32),
            jax.ShapeDtypeStruct((seq_len, 128), F32),
            jax.ShapeDtypeStruct((seq_len, 256), BF16),
        ]
        + [jax.ShapeDtypeStruct((2 * rows, width), BF16)] * 4,
        compiler_params=pltpu.CompilerParams(
            dimension_semantics=("arbitrary",), vmem_limit_bytes=62 << 20
        ),
        cost_estimate=cost(
            2 * seq_len * width * 896 + 4 * pairs * 128, 2 * seq_len * (2 * width + 2200), pairs
        ),
        name="attend_forward",
    )(table, *pieces, weights, cosine, sine, q_gain, k_gain)


def attend_backward_call(table, pieces, weights, proj, attn_o, lse, cosine, sine, q_gain, k_gain):
    seq_len, width = cosine.shape[0], weights.shape[0]
    rows = seq_len // 8
    by_slot = lambda i, t: (t[SLOT + jnp.minimum(i, 7)], 0)
    last_slot = lambda i, t: (jnp.where(i < 8, 4, (i - 4) % 8), 0)
    fixed = lambda i, t: (0, 0)
    pairs = seq_len * (seq_len + rows)
    return pl.pallas_call(
        attend_backward_kernel,
        grid_spec=pltpu.PrefetchScalarGridSpec(
            num_scalar_prefetch=1,
            grid=(16,),
            in_specs=[
                pl.BlockSpec(
                    (rows, width), lambda i, t, k=k: (t[BLOCK + 8 * k + jnp.minimum(i, 7)], 0)
                )
                for k in range(4)
            ]
            + [
                pl.BlockSpec(weights.shape, fixed, pipeline_mode=pl.Buffered(1)),
                pl.BlockSpec((rows, 640), by_slot),
                pl.BlockSpec((rows, 256), by_slot),
                pl.BlockSpec((rows, 128), by_slot),
                pl.BlockSpec((seq_len, 128), fixed, pipeline_mode=pl.Buffered(1)),
                pl.BlockSpec((seq_len, 128), fixed, pipeline_mode=pl.Buffered(1)),
                pl.BlockSpec((1, 128), fixed),
                pl.BlockSpec((1, 128), fixed),
            ],
            out_specs=[
                pl.BlockSpec((rows, 640), last_slot),
                pl.BlockSpec((8, 128), fixed),
                pl.BlockSpec((8, 128), fixed),
            ]
            + [
                pl.BlockSpec(
                    (rows, width), lambda i, t, k=k: (jnp.clip(i - 8 - (2 * k + 4) % 8, 0, 1), 0)
                )
                for k in range(4)
            ],
            scratch_shapes=[
                pltpu.VMEM((seq_len, 128), BF16),
                pltpu.VMEM((128, seq_len), BF16),
                pltpu.VMEM((seq_len, 128), BF16),
                pltpu.VMEM((seq_len, 128), F32),
                pltpu.VMEM((seq_len, 128), F32),
                pltpu.VMEM((seq_len, 128), F32),
                pltpu.VMEM((128, 2 * rows), F32),
                pltpu.VMEM((seq_len, 640), BF16),
            ],
        ),
        out_shape=[
            jax.ShapeDtypeStruct((seq_len, 640), BF16),
            jax.ShapeDtypeStruct((8, 128), F32),
            jax.ShapeDtypeStruct((8, 128), F32),
        ]
        + [jax.ShapeDtypeStruct((2 * rows, width), BF16)] * 4,
        compiler_params=pltpu.CompilerParams(
            dimension_semantics=("arbitrary",), vmem_limit_bytes=62 << 20
        ),
        cost_estimate=cost(
            2 * seq_len * width * 896 + 10 * pairs * 128,
            2 * seq_len * (2 * width + 2200),
            pairs,
            LATE_SHARE,
        ),
        name="attend_backward",
    )(table, *pieces, weights, proj, attn_o, lse, cosine, sine, q_gain, k_gain)


def feed_forward_kernel(*refs):
    rows_near, rows_far, cot_near, cot_far, w_down_t, w_inner = refs[:6]
    hidden_out, d_pre_out, down_near, down_far, back_near, back_far = refs[-6:]
    near = pl.program_id(0) < 2
    units = hidden_out.shape[1]
    pre = dot(jnp.where(near, rows_near[...], rows_far[...]), w_inner[...])
    d_hidden = dot(jnp.where(near, cot_near[...], cot_far[...]), w_down_t[...])
    gate_pre, up_pre = pre[:, :units], pre[:, units:]
    gate_sig = jax.nn.sigmoid(gate_pre)
    gate_act = gate_pre * gate_sig
    hidden_out[...] = (gate_act * up_pre).astype(BF16)
    d_pre_out[:, units:] = (d_hidden * gate_act).astype(BF16)
    d_pre_out[:, :units] = (
        d_hidden * up_pre * gate_sig * (1.0 + gate_pre * (1.0 - gate_sig))
    ).astype(BF16)
    back = dot(d_pre_out[...], w_inner[...], NT)
    down = dot(hidden_out[...], w_down_t[...], NT)

    @pl.when(near)
    def _():
        back_near[...] = back.astype(BF16)
        down_near[...] = down.astype(BF16)

    @pl.when(jnp.logical_not(near))
    def _():
        back_far[...] = back.astype(BF16)
        down_far[...] = down.astype(BF16)


def feed_forward_call(rows, cots, w_down_t, w_inner):
    count, width = rows[0].shape
    units = w_down_t.shape[1]
    tile = count // 2
    by_row = lambda i: (i, 0)
    fixed = lambda i: (0, 0)
    near = pl.BlockSpec((tile, width), lambda i: (jnp.minimum(i, 1), 0))
    far = pl.BlockSpec((tile, width), lambda i: (jnp.maximum(i - 2, 0), 0))
    wide = jax.ShapeDtypeStruct((count, width), BF16)
    out = pl.pallas_call(
        feed_forward_kernel,
        grid=(4,),
        in_specs=[near, far, near, far]
        + [pl.BlockSpec(w.shape, fixed, pipeline_mode=pl.Buffered(1)) for w in (w_down_t, w_inner)],
        out_specs=[
            pl.BlockSpec((tile, units), by_row),
            pl.BlockSpec((tile, 2 * units), by_row),
            near,
            far,
            near,
            far,
        ],
        out_shape=[
            jax.ShapeDtypeStruct((2 * count, units), BF16),
            jax.ShapeDtypeStruct((2 * count, 2 * units), BF16),
            wide,
            wide,
            wide,
            wide,
        ],
        compiler_params=pltpu.CompilerParams(
            dimension_semantics=("arbitrary",), vmem_limit_bytes=52 << 20
        ),
        cost_estimate=cost(24 * count * width * units, 2 * width * (8 * count + 3 * units)),
        name="feed_forward",
    )(*rows, *cots, w_down_t, w_inner)
    return (out[0], out[1], (out[2], out[3]), (out[4], out[5]))


def weight_grad_call(n_parts, lefts, terms, weights=None, carried=None, final=True, keep=None):
    n_pieces = len(lefts[0])
    rows, width = lefts[0][0].shape
    columns = [pieces[0][0].shape[1] for _, pieces in terms]
    kept = [keep or c for c in columns]
    starts = [sum(kept[:k]) for k in range(len(terms))]
    total = sum(kept)
    arrays, place = ([], {})
    for _, pieces in terms:
        for array, _ in pieces:
            if id(array) not in place:
                place[id(array)] = len(arrays)
                arrays.append(array)
    n_left, n_terms = len(lefts), len(terms)

    def kernel(*refs):
        left_refs = refs[: n_left * n_pieces]
        right_refs = refs[len(left_refs) : len(left_refs) + len(arrays)]
        rest = list(refs[len(left_refs) + len(arrays) :])
        if weights is not None:
            weights_ref = rest.pop(0)
        if carried is not None:
            carried_ref = rest.pop(0)
        out = rest.pop(0)
        if weights is not None:
            gain = rest.pop(0)
        left_buf, right_buf = rest[:n_left], rest[n_left : n_left + n_terms]
        accs, sems = rest[n_left + n_terms : -1], rest[-1]

        def copies(piece, slot):
            made = [
                pltpu.make_async_copy(
                    left_refs[k * n_pieces + piece], left_buf[k].at[slot], sems.at[slot, k]
                )
                for k in range(n_left)
            ]
            for k, (_, pieces) in enumerate(terms):
                array, first = pieces[piece]
                made.append(
                    pltpu.make_async_copy(
                        right_refs[place[id(array)]].at[pl.ds(first, rows)],
                        right_buf[k].at[slot],
                        sems.at[slot, n_left + k],
                    )
                )
            return made

        for copy in copies(0, 0):
            copy.start()
        if not final:
            accs = [out]
        for acc in accs:
            acc[...] = jnp.zeros_like(acc) if carried is None else carried_ref[...]

        def body(index, carry):
            slot = lax.rem(index, 2)
            for piece in range(1, n_pieces):

                @pl.when(index + 1 == piece)
                def _():
                    for copy in copies(piece, piece % 2):
                        copy.start()

            for copy in copies(0, slot):
                copy.wait()
            for k, (left, _) in enumerate(terms):
                for first in range(0, columns[k], 256):
                    some = slice(first, min(first + 256, columns[k]))
                    accs[k][some, :] += dot(right_buf[k][slot, :, some], left_buf[left][slot], TN)
            return carry

        lax.fori_loop(0, n_pieces, body, 0)
        if not final:
            return
        part = width // n_parts
        for p in range(n_parts):
            for k in range(n_terms):
                start = p * total + starts[k]
                some = accs[k][: kept[k], p * part : (p + 1) * part]
                out[start : start + kept[k], :] = some.astype(BF16)
        if weights is not None:
            scaled = accs[0][...] * weights_ref[:, : columns[0]].T.astype(F32)
            gain[...] = jnp.broadcast_to(jnp.sum(scaled, axis=0, keepdims=True), gain.shape)

    out_shape = [jax.ShapeDtypeStruct((n_parts * total, width // n_parts), BF16)]
    if not final:
        out_shape = [jax.ShapeDtypeStruct((total, width), F32)]
    vmem = pl.BlockSpec(memory_space=pltpu.VMEM)
    operands = [piece for pieces in lefts for piece in pieces] + arrays
    in_specs = [pl.BlockSpec(memory_space=pl.ANY)] * len(operands)
    if weights is not None:
        operands.append(weights)
        in_specs.append(vmem)
        out_shape.append(jax.ShapeDtypeStruct((8, width), F32))
    if carried is not None:
        operands.append(carried)
        in_specs.append(vmem)
    return pl.pallas_call(
        kernel,
        in_specs=in_specs,
        out_specs=[vmem] * len(out_shape),
        out_shape=out_shape,
        scratch_shapes=[pltpu.VMEM((2, rows, width), BF16)] * n_left
        + [pltpu.VMEM((2, rows, c), BF16) for c in columns]
        + [pltpu.VMEM((c, width), F32) for c in columns if final]
        + [pltpu.SemaphoreType.DMA((2, n_left + n_terms))],
        compiler_params=pltpu.CompilerParams(vmem_limit_bytes=56 << 20),
        cost_estimate=cost(
            2 * n_pieces * rows * width * total,
            2 * n_pieces * rows * (n_left * width + total) + 2 * width * total,
            0,
            LATE_SHARE,
        ),
        name="weight_grad",
    )(*operands)


def pack_attention_kernel(index, query, key, value, headgate, out, packed):
    half = pl.program_id(0) ^ index[0]
    packed[0, :, 0:256] = query[...]
    packed[0, :, 256:384] = key[...]
    packed[0, :, 384:512] = value[...]
    gates = headgate[...].astype(F32)
    first = jnp.where(half == 0, gates[:, 0:1], gates[:, 2:3])
    second = jnp.where(half == 0, gates[:, 1:2], gates[:, 3:4])
    packed[0, :, 512:640] = two_lanes(first, second, (packed.shape[1], 128)).astype(BF16)
    packed[0, :, 640:896] = out[...].T


def pack_attention(index, query, key, value, headgate, out):
    rows = query.shape[0]
    half = lambda i, t: (0, i ^ t[0])
    return pl.pallas_call(
        pack_attention_kernel,
        grid_spec=pltpu.PrefetchScalarGridSpec(
            num_scalar_prefetch=1,
            grid=(2,),
            in_specs=[
                pl.BlockSpec((rows, 256), half),
                pl.BlockSpec((rows, 128), half),
                pl.BlockSpec((rows, 128), half),
                pl.BlockSpec(headgate.shape, lambda i, t: (0, 0)),
                pl.BlockSpec((256, out.shape[1]), lambda i, t: (i ^ t[0], 0)),
            ],
            out_specs=pl.BlockSpec((1, rows, 896), lambda i, t: (i, 0, 0)),
        ),
        out_shape=jax.ShapeDtypeStruct((2, rows, 896), BF16),
        cost_estimate=cost(0, 4 * rows * 896 * 2),
        name="pack_attention",
    )(index, query, key, value, headgate, out)


def unpack_attention_kernel(index, kept, came, out_kept, out_came, query, key, value, headgate, out):
    flip = index[0] == 1

    def ordered(mine, other):
        return [
            jnp.where(flip, other[...], mine[...]).astype(F32),
            jnp.where(flip, mine[...], other[...]).astype(F32),
        ]

    for k, part in enumerate(ordered(kept, came)):
        query[:, 256 * k : 256 * k + 256] = part[0:256].T
        key[:, 128 * k : 128 * k + 128] = part[256:384].T
        value[:, 128 * k : 128 * k + 128] = part[384:512].T
        headgate[:, 2 * k : 2 * k + 2] = part[512:528].T[:, 0:2]
    for k, part in enumerate(ordered(out_kept, out_came)):
        out[256 * k : 256 * k + 256, :] = part


def unpack_attention(index, kept, came, out_kept, out_came):
    rows = kept.shape[1]
    vmem = pl.BlockSpec(memory_space=pltpu.VMEM)
    shapes = [(rows, 512), (rows, 256), (rows, 256), (rows, 4), (512, rows)]
    return pl.pallas_call(
        unpack_attention_kernel,
        in_specs=[pl.BlockSpec(memory_space=pltpu.SMEM)] + [vmem] * 4,
        out_specs=[vmem] * 5,
        out_shape=[jax.ShapeDtypeStruct(shape, F32) for shape in shapes],
        cost_estimate=cost(0, 8 * rows * 896),
        name="unpack_attention",
    )(index, kept, came, out_kept, out_came)


def pack_feed_forward_kernel(index, gate, up, down, packed):
    units = gate.shape[1]
    packed[0, :, :units] = down[...].T
    packed[0, :, units : 2 * units] = gate[...]
    packed[0, :, 2 * units :] = up[...]


def pack_feed_forward(index, gate, up, down):
    rows, units = gate.shape[0], gate.shape[1] // 4
    quarter = pl.BlockSpec((rows, units), lambda i, t: (0, i ^ t[0]))
    return pl.pallas_call(
        pack_feed_forward_kernel,
        grid_spec=pltpu.PrefetchScalarGridSpec(
            num_scalar_prefetch=1,
            grid=(4,),
            in_specs=[
                quarter,
                quarter,
                pl.BlockSpec((units, rows), lambda i, t: (i ^ t[0], 0)),
            ],
            out_specs=pl.BlockSpec((1, rows, 3 * units), lambda i, t: (i, 0, 0)),
        ),
        out_shape=jax.ShapeDtypeStruct((4, rows, 3 * units), BF16),
        cost_estimate=cost(0, 8 * rows * units * 6),
        name="pack_feed_forward",
    )(index, gate, up, down)


def unpack_feed_forward_kernel(index, *refs):
    pieces, (gate, up, down) = refs[:8], refs[8:]
    units = gate.shape[1]
    apart = pl.program_id(0) ^ index[0]

    def of_piece(group):
        low = jnp.where(apart == 0, group[0][...], group[1][...])
        high = jnp.where(apart == 2, group[2][...], group[3][...])
        return jnp.where(apart < 2, low, high).astype(F32)

    inner = of_piece(pieces[:4])
    gate[...] = inner[:units].T
    up[...] = inner[units:].T
    down[...] = of_piece(pieces[4:])


def unpack_feed_forward(index, inners, downs):
    units, rows = downs[0].shape
    quarter = pl.BlockSpec((rows, units), lambda i, t: (0, i))
    whole = [pl.BlockSpec(v.shape, lambda i, t: (0, 0)) for v in (*inners, *downs)]
    wide = jax.ShapeDtypeStruct((rows, 4 * units), F32)
    return pl.pallas_call(
        unpack_feed_forward_kernel,
        grid_spec=pltpu.PrefetchScalarGridSpec(
            num_scalar_prefetch=1,
            grid=(4,),
            in_specs=whole,
            out_specs=[quarter, quarter, pl.BlockSpec((units, rows), lambda i, t: (i, 0))],
        ),
        out_shape=[wide, wide, jax.ShapeDtypeStruct((4 * units, rows), F32)],
        cost_estimate=cost(0, 24 * rows * units * 4),
        name="unpack_feed_forward",
    )(index, *inners, *downs)


def row_sum(refs):
    return sum(ref[...].astype(F32) for ref in refs)


def middle_kernel(rows, t0, t1, t2, t3, gain, hidden, normed_rows):
    total = rows[...].astype(F32) + row_sum((t0, t1, t2, t3))
    hidden[...] = total
    normed_rows[...] = (total * rms_scale(total) * gain[...]).astype(BF16)


def turn_kernel(hidden, cot, t0, t1, t2, t3, gain, grad, grad_rows, gain_sum):
    values = hidden[...]
    scale = rms_scale(values)
    normed = values * scale
    d_rows = row_sum((t0, t1, t2, t3))
    total = cot[...].astype(F32) + norm_back(d_rows, normed, scale, gain[...])
    grad[...] = total
    grad_rows[...] = total.astype(BF16)

    @pl.when(pl.program_id(0) == 0)
    def _():
        gain_sum[...] = jnp.zeros_like(gain_sum)

    gain_sum[0:1, :] += jnp.sum(d_rows * normed, axis=0, keepdims=True)


def finish_kernel(rows, grad, t0, t1, t2, t3, gain, out):
    values = rows[...].astype(F32)
    scale = rms_scale(values)
    back = norm_back(row_sum((t0, t1, t2, t3)), values * scale, scale, gain[...])
    out[...] = (grad[...] + back).astype(BF16)


def on_rows(kernel, rows, gain, out_types, with_sum, name):
    count, width = rows[0].shape
    block = pl.BlockSpec((count // 4, width), lambda i: (i, 0))
    fixed = lambda size: pl.BlockSpec((size, width), lambda i: (0, 0))
    extra = int(with_sum)
    return pl.pallas_call(
        kernel,
        grid=(4,),
        in_specs=[block] * len(rows) + [fixed(1)],
        out_specs=[block] * len(out_types) + [fixed(8)] * extra,
        out_shape=[jax.ShapeDtypeStruct((count, width), t) for t in out_types]
        + [jax.ShapeDtypeStruct((8, width), F32)] * extra,
        cost_estimate=pl.CostEstimate(
            flops=20 * count * width, bytes_accessed=18 * count * width, transcendentals=0
        ),
        name=name,
    )(*rows, gain[None, :])


def pick(flag, first, second):
    return jnp.where(flag, first, second)


def reorder_by(pieces, index):
    low, high = (index & 1) == 1, (index & 2) == 2
    swapped = [pick(low, pieces[j ^ 1], pieces[j]) for j in range(4)]
    return [pick(high, swapped[j ^ 2], swapped[j]) for j in range(4)]


def local_plane(
    inputs,
    cotangent,
    seq_counts,
    seq_bucket,
    attn_norm_gain,
    q_norm_gain,
    k_norm_gain,
    w_query,
    w_key,
    w_value,
    w_headgate,
    w_out,
    ffn_norm_gain,
    w_gate,
    w_up,
    w_down,
):
    micro_batches, row_count, model_width = inputs.shape
    both = range(micro_batches)
    n_dp = lax.axis_size("dp")
    head_idx = lax.axis_index("head")
    mp_idx = lax.axis_index("mp")
    dp_idx = lax.axis_index("dp")
    core = head_idx & 1
    plane_idx = head_idx * 2 + mp_idx
    seq_len = row_count * 8
    units = w_gate.shape[1] // 4
    head_at = head_idx[None].astype(jnp.int32)
    mp_at = mp_idx[None].astype(jnp.int32)
    order = Order()

    def after(value, *ahead):
        return lax.optimization_barrier((value, ahead))[0]

    halves = pack_attention(mp_at, w_query, w_key, w_value, w_headgate, w_out)
    attn_came = swap(halves[1], BIT_X)

    slot_ids = jnp.arange(micro_batches * n_dp, dtype=jnp.int32)
    slot_count = jnp.sum(
        jnp.where(seq_bucket[None, :] == slot_ids[:, None], seq_counts[None, :], 0), axis=1
    )
    own_pos = plane_idx * row_count + jnp.arange(row_count, dtype=jnp.int32)
    live = [slot_count[n * n_dp + dp_idx] for n in both]
    x_float = [inputs[n].astype(F32) for n in both]
    scale1 = [rms_scale(x) for x in x_float]
    normed1 = [x * scale for x, scale in zip(x_float, scale1)]
    xn1_own = [(n * attn_norm_gain).astype(BF16) for n in normed1]
    cot_live = [
        cotangent[n].astype(F32) * (own_pos < live[n]).astype(F32)[:, None] for n in both
    ]
    cot_own = [c.astype(BF16) for c in cot_live]
    xn1, xn2, cot, d_attn = ([None] * micro_batches for _ in range(4))
    xn1[0] = Gather(order, after(xn1_own[0], attn_came))
    is_first = mp_idx == 0
    attn_rows = jnp.concatenate(
        [pick(is_first, halves[0], attn_came), pick(is_first, attn_came, halves[0])], axis=0
    )
    w_attn = lax.all_gather(attn_rows, "dp", axis=0, tiled=True)
    xn1[0].second()
    xn1[0].third()

    quarters = after(pack_feed_forward(head_at, w_gate, w_up, w_down), xn1[0].pieces[1])
    traded = [quarters[0]] + [swap(quarters[r], r * 2) for r in (1, 2, 3)]
    parts = [[t[:, :units] for t in traded], [t[:, units:] for t in traded]]
    ffn_rows = [jnp.concatenate(reorder_by(part, head_idx), axis=0) for part in parts]
    ffn_rows = after(tuple(ffn_rows), attn_rows)
    w_ffn = [lax.all_gather(rows, "dp", axis=0, tiled=True) for rows in ffn_rows]

    xn1[1] = Gather(order, after(xn1_own[1], xn1[0].pieces[1]))
    tables = [attend_table(plane_idx, core, count) for count in live]
    table_cos, table_sin = rope_tables(jnp.arange(seq_len, dtype=jnp.int32), 64)
    table_cos, table_sin = table_cos[:, 0, :], table_sin[:, 0, :]
    cosine = jnp.concatenate([table_cos, table_cos], axis=1)
    sine = jnp.concatenate([-table_sin, table_sin], axis=1)
    fixed = (cosine, sine, q_norm_gain[None, :], k_norm_gain[None, :])
    att, out_sum = ([None] * micro_batches for _ in range(2))

    def attend(n):
        att[n] = order.run(
            lambda *pieces: attend_forward_call(tables[n], pieces, w_attn, *fixed), *xn1[n].pieces
        )

    order.need(xn1[1].second())
    cot[0] = Gather(order, after(cot_own[0], xn1[1].pieces[0]))
    attend(0)
    done = (xn1[1].third(), cot[0].second())
    out_sum[0] = Scatter(order, *after((att[0][6], att[0][7]), *done))
    order.need(*out_sum[0].add(att[0][4], att[0][5]), *done, w_ffn[0])
    out_sum[0].send_far()
    attend(1)
    done = (out_sum[0].take(), cot[0].third())
    out_sum[0].send_near()
    out_sum[1] = Scatter(order, *after((att[1][6], att[1][7]), *done))
    order.need(*done)

    hidden1, scale2, normed2 = ([None] * micro_batches for _ in range(3))

    def middle(n):
        hidden1[n], rows = on_rows(
            middle_kernel, (inputs[n], *out_sum[n].terms()), ffn_norm_gain, (F32, BF16), False, "middle"
        )
        xn2[n] = Gather(order, rows)
        return rows

    rows = middle(0)
    order.need(*out_sum[1].add(after(att[1][4], rows), att[1][5]))
    out_sum[1].send_far()
    order.need(xn2[0].second(), out_sum[1].take())
    out_sum[1].send_near()
    order.need(xn2[0].third(), middle(1))
    cot[1] = Gather(order, after(cot_own[1], xn2[0].pieces[1]))

    feed = {}
    down, back = ([None] * micro_batches for _ in range(2))

    def feed_other(n):
        feed[n, 1] = order.run(
            lambda *v: feed_forward_call(v[0:2], v[2:4], *w_ffn), *xn2[n].pieces[2:], *cot[n].pieces[2:]
        )

    def feed_mine(n):
        feed[n, 0] = order.run(
            lambda *v: feed_forward_call(v[0:2], v[2:4], *w_ffn), *xn2[n].pieces[:2], *cot[n].pieces[:2]
        )
        return back[n].add(*feed[n, 0][3])

    d_hidden1 = [None] * micro_batches
    gain_ffn = []

    def turn(n):
        d_hidden1[n], rows, part = on_rows(
            turn_kernel,
            (hidden1[n], cot_own[n], *back[n].terms()),
            ffn_norm_gain,
            (F32, BF16),
            True,
            "turn",
        )
        gain_ffn.append(part[0])
        d_attn[n] = Gather(order, rows)
        return rows

    def row_pieces(array):
        count = array.shape[0] // (2 * row_count)
        return [(array, 2 * row_count * k) for k in range(count)]

    def of_feed(which):
        return [p for n in both for side in (0, 1) for p in row_pieces(feed[n, side][which])]

    def rows_of(gathers):
        return [piece for gather in gathers for piece in gather.pieces]

    def grad_call(lefts, terms, *more):
        count = [len(left) for left in lefts]
        return order.run(
            lambda *v: weight_grad_call(
                n_dp,
                [list(v[sum(count[:k]) : sum(count[: k + 1])]) for k in range(len(lefts))],
                terms,
                *more,
            ),
            *[piece for left in lefts for piece in left],
        )

    def sum_over_dp(values):
        return lax.psum_scatter(values, "dp", scatter_dimension=0, tiled=True)

    def quarters_of(values):
        width = values.shape[1] // 4
        quarter = lambda k: lax.dynamic_slice_in_dim(values, k * width, width, 1)
        return [quarter(head_idx)] + [swap(quarter(head_idx ^ r), r * 2) for r in (1, 2, 3)]

    feed_other(0)
    done = (xn2[1].second(), cot[1].second())
    back[0] = Scatter(order, *after(feed[0, 1][3], *done))
    order.need(*done)
    sums = feed_mine(0)
    done = (xn2[1].third(), cot[1].third())
    down[0] = Scatter(order, *after(feed[0, 1][2], *done, *sums))
    back[0].send_far()
    order.need(*sums, *done)
    feed_other(1)
    done = (back[0].take(), *down[0].add(*feed[0, 0][2]))
    back[0].send_near()
    down[0].send_far()
    back[1] = Scatter(order, *after(feed[1, 1][3], *done))
    order.need(*done)
    order.need(*feed_mine(1), turn(0), down[0].take())
    back[1].send_far()
    grad_inner = grad_call([rows_of(xn2)], [(0, of_feed(1))])[0]
    done = (d_attn[0].second(), back[1].take())
    back[1].send_near()
    down[1] = Scatter(order, *after(feed[1, 1][2], *done))
    order.need(*done)
    grad_down = grad_call([rows_of(cot)], [(0, of_feed(0))])[0]
    grads_inner = sum_over_dp(order.pin(grad_inner))
    order.need(d_attn[0].third(), turn(1), *down[1].add(*feed[1, 0][2]))
    down[0].send_near()
    down[1].send_far()

    d_proj, gain_parts, rows_sum = ([None] * micro_batches for _ in range(3))

    def attend_back(n):
        out = order.run(
            lambda *v: attend_backward_call(
                tables[n], v, w_attn, att[n][0], att[n][1], att[n][2], *fixed
            ),
            *d_attn[n].pieces,
        )
        d_proj[n] = out[0]
        gain_parts[n] = (out[1][0], out[2][0])
        return out

    def finish(n):
        return on_rows(
            finish_kernel,
            (inputs[n], d_hidden1[n], *rows_sum[n].terms()),
            attn_norm_gain,
            (BF16,),
            False,
            "finish",
        )[0]

    outputs, input_grads = ([None] * micro_batches for _ in range(2))
    back_0 = attend_back(0)
    grads_down = sum_over_dp(order.pin(grad_down))
    done = (d_attn[1].second(), down[1].take())
    outputs[0] = (hidden1[0] + down[0].result()).astype(BF16)
    rows_sum[0] = Scatter(order, *after((back_0[5], back_0[6]), *done, outputs[0]))
    order.need(*done, outputs[0], *rows_sum[0].add(back_0[3], back_0[4]))
    grads_proj = grad_call([xn1[0].pieces], [(0, row_pieces(d_proj[0]))], None, None, False)[0]
    order.need(d_attn[1].third())
    grads_out = sum_over_dp(
        grad_call(
            [rows_of(d_attn)], [(0, [p for n in both for p in row_pieces(att[n][3])])]
        )[0]
    )
    rows_sum[0].send_far()
    down[1].send_near()
    inner_quarters = quarters_of(order.pin(grads_inner))
    order.need(grads_inner)
    back_1 = attend_back(1)
    done = (rows_sum[0].take(), *inner_quarters)
    rows_sum[0].send_near()
    rows_sum[1] = Scatter(order, *after((back_1[5], back_1[6]), *done))
    order.need(*done, grads_down)
    grads_proj, gain_rows = grad_call(
        [xn1[1].pieces], [(0, row_pieces(d_proj[1]))], w_attn, grads_proj, True, 528
    )
    grads_proj = sum_over_dp(grads_proj)
    outputs[1] = (hidden1[1] + down[1].result()).astype(BF16)
    input_grads[0] = finish(0)
    order.need(*rows_sum[1].add(*after((back_1[3], back_1[4]), outputs[1], input_grads[0])))
    rows_sum[1].send_far()
    down_quarters = quarters_of(after(grads_down, rows_sum[1].take()))
    rows_sum[1].send_near()
    input_grads[1] = finish(1)
    order.need(input_grads[1])
    grad_gate, grad_up, grad_down = order.run(
        lambda *v: unpack_feed_forward(head_at, v[:4], v[4:]), *inner_quarters, *down_quarters
    )

    gains = jnp.concatenate(
        [gain_rows[0] / attn_norm_gain, gain_ffn[0] + gain_ffn[1]]
        + [gain_parts[0][k] + gain_parts[1][k] for k in range(2)]
    ).reshape(-1, 128)
    gains = gains + swap(gains, BIT_C)
    for step in (1, 2):
        gains = gains + lax.ppermute(gains, "dp", [(i, i ^ step) for i in range(4)])
    gains = after(gains, input_grads[1])
    for bits in (BIT_X, BIT_Y):
        gains = gains + swap(gains, bits)
    gains = gains.reshape(-1)
    sum_attn, sum_gain_ffn = gains[:model_width], gains[model_width : 2 * model_width]
    sum_query, sum_key = gains[-256:-128], gains[-128:]

    def halves_of(values):
        left, right = values[:, :row_count], values[:, row_count:]
        return pick(is_first, left, right), swap(pick(is_first, right, left), BIT_X)

    grad_query, grad_key, grad_value, grad_headgate, grad_out = order.run(
        lambda *v: unpack_attention(mp_at, *v), *halves_of(grads_proj), *halves_of(grads_out)
    )
    return (
        jnp.stack(outputs),
        jnp.stack(input_grads),
        sum_attn,
        sum_query,
        sum_key,
        grad_query,
        grad_key,
        grad_value,
        grad_headgate,
        grad_out,
        sum_gain_ffn,
        grad_gate,
        grad_up,
        grad_down,
    )


def choose_local(mesh):
    if mesh.shape["head"] == 4 and mesh.shape["mp"] == 2 and mesh.shape["dp"] == 4:
        return local_plane
    return local


def solution(mesh):
    placed = (
        P(None, ("dp", "head", "mp"), None),
        P(None, ("dp", "head", "mp"), None),
        P(),
        P(),
        P(),
        P(),
        P(),
        P(("dp", "mp"), "head"),
        P(("dp", "mp"), "head"),
        P(("dp", "mp"), "head"),
        P(("dp", "mp"), "head"),
        P("head", ("dp", "mp")),
        P(),
        P(("dp", "head"), "mp"),
        P(("dp", "head"), "mp"),
        P("mp", ("dp", "head")),
    )
    return jax.shard_map(
        choose_local(mesh),
        mesh=mesh,
        in_specs=placed,
        out_specs=(
            P(None, ("dp", "head", "mp"), None),
            P(None, ("dp", "head", "mp"), None),
            P(),
            P(),
            P(),
            P(("dp", "mp"), "head"),
            P(("dp", "mp"), "head"),
            P(("dp", "mp"), "head"),
            P(("dp", "mp"), "head"),
            P("head", ("dp", "mp")),
            P(),
            P(("dp", "head"), "mp"),
            P(("dp", "head"), "mp"),
            P("mp", ("dp", "head")),
        ),
        check_vma=False,
    )
```
